128 devices in a mesh: tm: 16 (over z, y_lo, core), lat: 8 (over x, y_hi).
Axes of the slice: x: 4, y: 4 (y_hi: 2, y_lo: 2; y = y_hi * 2 + y_lo), z: 4, core: 2. Of those that a mesh axis runs over, the one named last changes fastest.
Arguments:
- window_snapshots: bfloat16 [16, 64, 64, 128], P('tm', None, 'lat'), may hold values from -6 to 6
- background: bfloat16 [64, 64, 128], P(None, 'lat'), may hold values from -6 to 6
- obs_values: bfloat16 [16, 64, 2048], P('tm', None, 'lat'), may hold values from -6 to 6
- obs_index: int32 [16, 2048], P('tm', 'lat'), may hold values from 0 to 8191, as said below
- input_kernel_weight: bfloat16 [3, 3, 256, 64], replicated, may hold values from -0.25 to 0.25
- hidden_bias_vector: float32 [256], replicated, may hold values from -3 to 3
- output_pointwise_weight: bfloat16 [64, 256], replicated, may hold values from -0.375 to 0.375
Outputs:
- analysis: bfloat16 [16, 64, 64, 128], P('tm', None, 'lat')
The draws below stay inside these ranges and needn't reach their ends.
Inputs may be any that keep to these rules, and one draw needn't show every extreme that they name: `obs_index`: entry [k, j] is a grid column counted latitude by latitude over 128 longitudes; observations s * 256 to (s + 1) * 256 - 1 lie in latitudes s * 8 to (s + 1) * 8 - 1; a column may be observed more than once.
All inputs are finite; a program needn't handle non-finite values.
Results may differ from the reference program's by a relative error of at most 0.015.
Values may be sent and summed in bfloat16 or wider, within the bound.
No kernel may reach another device: no remote copies, remote signals or barrier semaphores. Data moves between devices by JAX's collectives and lax.ppermute only.
A program may use at most 64 MiB of HBM per device.

```python
import jax
import jax.numpy as jnp
from jax import lax

C = 64
HID = 256
LAT_DEV = 8
LON = 128
OBS_DEV = 256
ITERS = 2
SUB = 16
LAT = 64
OBS = 2048


def draw_obs_index(key, part):
    strips = OBS // OBS_DEV
    strip_cells = LAT_DEV * LON
    local_cells = jax.random.randint(key, (SUB, strips, OBS_DEV), 0, strip_cells, dtype=jnp.int32)
    local_cells = local_cells.at[:, 0, 0].set(0)
    local_cells = local_cells.at[:, strips - 1, OBS_DEV - 1].set(strip_cells - 1)
    offsets = jnp.arange(strips, dtype=jnp.int32)[None, :, None] * strip_cells
    return (local_cells + offsets).reshape(SUB, OBS).astype(jnp.int32)


def block_levels(own_key, dims, pieces, low, high):
    level, own = 1.0, jax.random.fold_in(own_key, 6)
    for position, parts in pieces:
        heights = jnp.exp(jax.random.uniform(jax.random.fold_in(own, position), (parts,), jnp.float32, low / len(pieces), high / len(pieces)))
        level = level * jnp.repeat(heights, dims[position] // parts).reshape([-1 if axis == position else 1 for axis in range(len(dims))])
    return level


def gaussian(rng, shape, width, limit, shards=(), held_as=jnp.bfloat16):
    level = block_levels(rng, shape, shards, -0.22, 0.18) if shards else 1.0
    values = jax.random.normal(rng, shape, jnp.float32) * width * level
    return jnp.minimum(jnp.maximum(values, -limit), limit).astype(held_as)


def setup_inputs(seed: int = 0) -> dict:
    key_list = jax.random.split(jax.random.key(seed), 8)
    window_snapshots = gaussian(key_list[0], (SUB, C, LAT, LON), 1.0, 6.0, ((0, 16), (2, 8)))
    background = gaussian(key_list[1], (C, LAT, LON), 1.0, 6.0, ((1, 8),))
    obs_values = gaussian(key_list[2], (SUB, C, OBS), 1.0, 6.0, ((0, 16), (2, 8)))
    obs_index = draw_obs_index(jax.random.fold_in(key_list[7], 71), 0)
    input_kernel_weight = gaussian(key_list[4], (3, 3, HID, C), (9 * C) ** -0.5, 0.25)
    hidden_bias_vector = gaussian(key_list[5], (HID,), 0.5, 3.0, (), jnp.float32)
    output_pointwise_weight = gaussian(key_list[6], (C, HID), HID ** -0.5, 0.375)
    return {"window_snapshots": window_snapshots, "background": background, "obs_values": obs_values, "obs_index": obs_index, "input_kernel_weight": input_kernel_weight, "hidden_bias_vector": hidden_bias_vector, "output_pointwise_weight": output_pointwise_weight}


step_size = 0.3


def conv_forward(grid_field, input_kernel_weight):
    height = grid_field.shape[1]
    padded = jnp.pad(grid_field.astype(jnp.float32), ((0, 0), (1, 1), (0, 0)))
    weights = input_kernel_weight.astype(jnp.float32)
    summed = jnp.zeros((input_kernel_weight.shape[2], height, grid_field.shape[2]), jnp.float32)
    for row_step in range(3):
        stripe = padded[:, row_step:row_step + height, :]
        for col_step in range(3):
            moved = jnp.roll(stripe, 1 - col_step, axis=2)
            summed = summed + jnp.einsum("hc,clm->hlm", weights[row_step, col_step], moved, precision=lax.Precision.HIGHEST)
    return summed


def conv_transpose(cotangent, input_kernel_weight):
    height = cotangent.shape[1]
    weights = input_kernel_weight.astype(jnp.float32)
    source = cotangent.astype(jnp.float32)
    summed = jnp.zeros((input_kernel_weight.shape[3], height + 2, cotangent.shape[2]), jnp.float32)
    for row_step in range(3):
        partial_value = jnp.zeros((input_kernel_weight.shape[3], height, cotangent.shape[2]), jnp.float32)
        for col_step in range(3):
            product = jnp.einsum("hc,hlm->clm", weights[row_step, col_step], source, precision=lax.Precision.HIGHEST)
            partial_value = partial_value + jnp.roll(product, col_step - 1, axis=2)
        summed = summed + jnp.pad(partial_value, ((0, 0), (row_step, 2 - row_step), (0, 0)))
    return summed[:, 1:height + 1]


def misfit_map(grid_state, values, column_index):
    channels = grid_state.shape[0]
    flattened = grid_state.reshape(channels, -1)
    misfit = jnp.take(flattened, column_index, axis=1).astype(jnp.float32) - values.astype(jnp.float32)
    spread_out = jnp.zeros(flattened.shape, jnp.float32).at[:, column_index].add(misfit)
    return spread_out.reshape(grid_state.shape)


def reference(window_snapshots, background, obs_values, obs_index, input_kernel_weight, hidden_bias_vector, output_pointwise_weight):
    windows = window_snapshots.shape[0]
    weights_out = output_pointwise_weight.astype(jnp.float32)
    for repeat in range(ITERS):
        def couple(paired):
            earlier_snapshot = paired[0]
            current_snapshot = paired[1]
            before = conv_forward(earlier_snapshot, input_kernel_weight) + hidden_bias_vector[:, None, None]
            active = jnp.tanh(before).astype(jnp.bfloat16)
            latent_activation_layer = jnp.einsum("ch,hlm->clm", weights_out, active.astype(jnp.float32), precision=lax.Precision.HIGHEST)
            surrogate_projection = (earlier_snapshot.astype(jnp.float32) + latent_activation_layer).astype(jnp.bfloat16)
            dynamics_mismatch = (current_snapshot.astype(jnp.float32) - surrogate_projection.astype(jnp.float32)).astype(jnp.bfloat16)
            projected = jnp.einsum("ch,clm->hlm", weights_out, dynamics_mismatch.astype(jnp.float32), precision=lax.Precision.HIGHEST)
            squashed = active.astype(jnp.float32)
            cotangent = ((1.0 - squashed * squashed) * projected).astype(jnp.bfloat16)
            pulled = (dynamics_mismatch.astype(jnp.float32) + conv_transpose(cotangent, input_kernel_weight)).astype(jnp.bfloat16)
            return dynamics_mismatch, pulled

        later_resid, pulled = lax.map(couple, (window_snapshots[:windows - 1], window_snapshots[1:]))
        first_resid = (window_snapshots[0].astype(jnp.float32) - background.astype(jnp.float32)).astype(jnp.bfloat16)
        dynamics_mismatch = jnp.concatenate([first_resid[None], later_resid], axis=0)
        adjoint = jnp.concatenate([pulled, jnp.zeros_like(window_snapshots[:1])], axis=0)
        innovation = lax.map(lambda paired: misfit_map(paired[0], paired[1], paired[2]), (window_snapshots, obs_values, obs_index))
        gradient = dynamics_mismatch.astype(jnp.float32) - adjoint.astype(jnp.float32) + innovation
        window_snapshots = (window_snapshots.astype(jnp.float32) - step_size * gradient).astype(jnp.bfloat16)
    return window_snapshots
```

```python
import functools

import jax
import jax.numpy as jnp
from jax import lax
from jax.experimental import pallas as pl
from jax.experimental.pallas import tpu as pltpu
from jax.sharding import PartitionSpec as P

C = 64
HID = 256
ROWS = 8
LON = 128
OBS = 256
STEP = 0.3

F32 = jnp.float32
BF16 = jnp.bfloat16
VMEM = pl.BlockSpec(memory_space=pltpu.VMEM)

X_PART = 4 * C
BG_PART = X_PART + 2 * C
OBS_PART = BG_PART + 2 * C
PAYLOAD = OBS_PART + 16


def call(kernel, outs, scratch, flops, bytes_accessed):
    def run(*args):
        return pl.pallas_call(
            kernel,
            out_shape=outs,
            in_specs=[VMEM] * len(args),
            out_specs=jax.tree.map(lambda _: VMEM, outs),
            scratch_shapes=scratch,
            cost_estimate=pl.CostEstimate(
                flops=flops, bytes_accessed=bytes_accessed, transcendentals=0
            ),
            compiler_params=pltpu.CompilerParams(vmem_limit_bytes=48 << 20),
        )(*args)

    return run


def rows_of(ref, first, width=C):
    return ref[first * width : (first + 1) * width, :]


def observation_sums(values, low, high, row):
    cell = lax.broadcasted_iota(jnp.int32, (LON, OBS), 0)
    hit = jnp.where((low == cell) & (high == row), 1.0, 0.0).astype(BF16)
    return lax.dot_general(
        values, hit, (((1,), (1,)), ((), ())), preferred_element_type=F32
    )


def pack_kernel(x_ref, bg_ref, obs_ref, index_ref, own_ref, bg_rows_ref, up_ref, down_ref, xs, bs):
    xs[...] = x_ref[...].astype(F32)
    bs[...] = bg_ref[...].astype(F32)
    for row in range(ROWS):
        value = xs[:, row, :].astype(BF16)
        own_ref[row * C : (row + 1) * C, :] = value
        if row < 4:
            up_ref[row * C : (row + 1) * C, :] = value
        else:
            down_ref[(row - 4) * C : (row - 3) * C, :] = value
        ground = bs[:, row, :].astype(BF16)
        bg_rows_ref[row * C : (row + 1) * C, :] = ground
        if row < 2:
            up_ref[X_PART + row * C : X_PART + (row + 1) * C, :] = ground
        if row >= 6:
            down_ref[X_PART + (row - 6) * C : X_PART + (row - 5) * C, :] = ground
    local = index_ref[...] - lax.axis_index("lat") * (ROWS * LON)
    high = lax.shift_right_arithmetic(local, 7)
    low = local - high * LON
    place = lax.broadcasted_iota(jnp.int32, (16, LON), 0)
    coded = jnp.zeros((16, LON), jnp.int32)
    for spot, part in enumerate(
        (high[:, :LON], high[:, LON:], low[:, :LON], low[:, LON:])
    ):
        coded = jnp.where(place == spot, jnp.broadcast_to(part, (16, LON)), coded)
    coded = coded.astype(F32).astype(BF16)
    for ref in (up_ref, down_ref):
        ref[BG_PART : BG_PART + C, :] = obs_ref[:, :LON]
        ref[BG_PART + C : OBS_PART, :] = obs_ref[:, LON:]
        ref[OBS_PART:PAYLOAD, :] = coded


def extend_kernel(own_ref, bg_rows_ref, above_ref, below_ref, ext_ref, sent_ref, bg_ref):
    strip = lax.axis_index("lat")
    first = strip > 0
    last = strip < lax.axis_size("lat") - 1
    zero = jnp.zeros((X_PART, LON), BF16)
    above = jnp.where(first, above_ref[:X_PART, :], zero)
    below = jnp.where(last, below_ref[:X_PART, :], zero)
    ext_ref[:X_PART, :] = above
    ext_ref[X_PART : X_PART + ROWS * C, :] = own_ref[...]
    ext_ref[X_PART + ROWS * C :, :] = below
    sent_ref[: 3 * C, :] = above[C:, :]
    sent_ref[3 * C : 11 * C, :] = own_ref[...]
    sent_ref[11 * C :, :] = below[: 3 * C, :]
    bg_ref[: 2 * C, :] = above_ref[X_PART:BG_PART, :]
    bg_ref[2 * C : 10 * C, :] = bg_rows_ref[...]
    bg_ref[10 * C :, :] = below_ref[X_PART:BG_PART, :]


def roll_rows(state_ref, shifted, count):
    for row in range(count):
        at = slice(row * C, (row + 1) * C)
        value = state_ref[at, :]
        wide = value.astype(F32)
        shifted[0, at, :] = pltpu.roll(wide, 1, 1).astype(BF16)
        shifted[1, at, :] = value
        shifted[2, at, :] = pltpu.roll(wide, LON - 1, 1).astype(BF16)


def hidden(shifted, kernel_ref, bias, row):
    def stack(first):
        return jnp.concatenate(
            [shifted[b, first * C : (first + 3) * C, :] for b in range(3)], axis=0
        )

    cells = jnp.concatenate([stack(row), stack(row + 1)], axis=1)
    before = jnp.dot(kernel_ref[...], cells, preferred_element_type=F32) + bias
    return jnp.tanh(before).astype(BF16)


def side_by_side(ref, first):
    return jnp.concatenate([rows_of(ref, first), rows_of(ref, first + 1)], axis=1)


def store_pair(ref, first, value, width=C):
    ref[first * width : (first + 1) * width, :] = value[:, :LON]
    ref[(first + 1) * width : (first + 2) * width, :] = value[:, LON:]


def forward_part(count, state_ref, kernel_ref, bias_ref, out_weight_ref, active_ref, forecast_ref, shifted):
    roll_rows(state_ref, shifted, count + 2)
    bias = jnp.broadcast_to(bias_ref[...], (HID, 2 * LON))
    for row in range(0, count, 2):
        active = hidden(shifted, kernel_ref, bias, row)
        store_pair(active_ref, row, active, HID)
        step = jnp.dot(out_weight_ref[...], active, preferred_element_type=F32)
        centre = side_by_side(state_ref, row + 1).astype(F32)
        store_pair(forecast_ref, row, (centre + step).astype(BF16))


def forward_kernel(count, *refs):
    forward_part(count, *refs)


def sums_kernel(obs_ref, index_ref, above_ref, below_ref, sums_ref):
    ones = jnp.ones((16, OBS), BF16)

    def decode(ref):
        values = jnp.concatenate(
            [ref[BG_PART : BG_PART + C, :], ref[BG_PART + C : OBS_PART, :]], axis=1
        )
        coded = ref[OBS_PART:PAYLOAD, :].astype(F32).astype(jnp.int32)
        high = jnp.concatenate([coded[0:1, :], coded[1:2, :]], axis=1)
        low = jnp.concatenate([coded[2:3, :], coded[3:4, :]], axis=1)
        return jnp.concatenate([values, ones], axis=0), low, high

    local = index_ref[...] - lax.axis_index("lat") * (ROWS * LON)
    high = lax.shift_right_arithmetic(local, 7)
    own = (jnp.concatenate([obs_ref[...], ones], axis=0), local - high * LON, high)
    above = decode(above_ref)
    below = decode(below_ref)
    for place in range(12):
        source, row = (above, 6 + place) if place < 2 else (own, place - 2)
        if place >= 10:
            source, row = below, place - 10
        sums_ref[place] = observation_sums(*source, row)[:72, :]


def gradient_part(
    count, margin, prev_ref, next_ref, own_ref, own_first, active_ref, forecast_ref, bg_ref,
    bg_first, sums_ref, kernel_ref, back_ref, bias_ref, out_weight_ref, out_back_ref,
    emit, shifted, cot, resid, target,
):
    strip = lax.axis_index("lat")
    window = lax.axis_index("tm")
    top = -strip * ROWS
    bottom = (lax.axis_size("lat") - strip) * ROWS
    roll_rows(prev_ref, shifted, count + 2)
    bias = jnp.broadcast_to(bias_ref[...], (HID, 2 * LON))
    opening = window == 0
    for row in range(0, count, 2):
        active = hidden(shifted, kernel_ref, bias, row)
        step = jnp.dot(out_weight_ref[...], active, preferred_element_type=F32)
        centre = side_by_side(prev_ref, row + 1).astype(F32)
        guess = (centre + step).astype(BF16).astype(F32)
        ground = side_by_side(bg_ref, bg_first + row).astype(F32)
        guess = jnp.where(opening, ground, guess)
        own = side_by_side(own_ref, own_first + row).astype(F32)
        store_pair(resid, row, (own - guess).astype(BF16))
    for row in range(0, count + 2, 2):
        later = side_by_side(next_ref, row).astype(F32) - side_by_side(forecast_ref, row).astype(F32)
        later = later.astype(BF16)
        store_pair(target, row, later)
        projected = jnp.dot(out_back_ref[...], later, preferred_element_type=F32)
        for half in range(2):
            place = row + half - margin - 1
            inside = (place >= top) & (place < bottom)
            active = active_ref[(row + half) * HID : (row + half + 1) * HID, :].astype(F32)
            value = (1.0 - active * active) * projected[:, half * LON : (half + 1) * LON]
            value = jnp.where(inside, value, 0.0).astype(BF16)
            cot[(row + half) * HID : (row + half + 1) * HID, :] = value
    closing = window == lax.axis_size("tm") - 1
    for row in range(0, count, 2):
        cells = jnp.concatenate(
            [cot[row * HID : (row + 3) * HID, :], cot[(row + 1) * HID : (row + 4) * HID, :]], axis=1
        )
        spread = jnp.dot(back_ref[...], cells, preferred_element_type=F32)
        for half in range(2):
            lanes = slice(half * LON, (half + 1) * LON)
            pulled = (
                pltpu.roll(spread[:C, lanes], LON - 1, 1)
                + spread[C : 2 * C, lanes]
                + pltpu.roll(spread[2 * C :, lanes], 1, 1)
            )
            place = row + half
            later = rows_of(target, place + 1).astype(F32)
            adjoint = jnp.where(closing, 0.0, (later + pulled).astype(BF16).astype(F32))
            own = rows_of(own_ref, own_first + place).astype(F32)
            sums = sums_ref[2 - margin + place]
            innovation = sums[C : C + 1, :] * own - sums[:C, :]
            gradient = rows_of(resid, place).astype(F32) - adjoint + innovation
            value = own - STEP * gradient
            latitude = place - margin
            inside = (latitude >= top) & (latitude < bottom)
            emit(place, jnp.where(inside, value, 0.0) if margin else value)


def first_kernel(
    prev_ref, next_ref, ext_ref, active_ref, forecast_ref, bg_ref, sums_ref, kernel_ref, back_ref,
    bias_ref, out_weight_ref, out_back_ref, state_ref, sent_ref, shifted, cot, resid, target,
):
    def emit(place, value):
        value = value.astype(BF16)
        state_ref[place * C : (place + 1) * C, :] = value
        if 1 <= place < 11:
            sent_ref[(place - 1) * C : place * C, :] = value

    gradient_part(
        12, 2, prev_ref, next_ref, ext_ref, 2, active_ref, forecast_ref, bg_ref, 0, sums_ref,
        kernel_ref, back_ref, bias_ref, out_weight_ref, out_back_ref, emit, shifted, cot, resid,
        target,
    )


def second_kernel(
    prev_ref, next_ref, state_ref, active_ref, forecast_ref, bg_ref, sums_ref, kernel_ref, back_ref,
    bias_ref, out_weight_ref, out_back_ref, out_ref, shifted, cot, resid, target, wide,
):
    def emit(place, value):
        wide[:, place, :] = value

    gradient_part(
        8, 0, prev_ref, next_ref, state_ref, 2, active_ref, forecast_ref, bg_ref, 2, sums_ref,
        kernel_ref, back_ref, bias_ref, out_weight_ref, out_back_ref, emit, shifted, cot, resid,
        target,
    )
    out_ref[...] = wide[...].astype(BF16)


def ring(value, axis, by):
    count = lax.axis_size(axis)
    return lax.ppermute(value, axis, [(i, (i + by) % count) for i in range(count)])


def shape(rows, dtype=BF16):
    return jax.ShapeDtypeStruct((rows, LON), dtype)


def gradient_scratch(count):
    return [
        pltpu.VMEM((3, (count + 2) * C, LON), BF16),
        pltpu.VMEM(((count + 2) * HID, LON), BF16),
        pltpu.VMEM((count * C, LON), BF16),
        pltpu.VMEM(((count + 2) * C, LON), BF16),
    ]


def on_device(
    window_snapshots, background, obs_values, obs_index, input_kernel_weight, hidden_bias_vector,
    output_pointwise_weight,
):
    own, bg_rows, up, down = call(
        pack_kernel,
        (shape(ROWS * C), shape(ROWS * C), shape(PAYLOAD), shape(PAYLOAD)),
        [pltpu.VMEM((C, ROWS, LON), F32), pltpu.VMEM((C, ROWS, LON), F32)],
        0, 1 << 20,
    )(window_snapshots[0], background, obs_values[0], obs_index)
    below = ring(up, "lat", -1)
    above = ring(down, "lat", 1)

    forward_weight = jnp.transpose(input_kernel_weight, (2, 1, 0, 3)).reshape(HID, 9 * C)
    back_weight = jnp.transpose(input_kernel_weight[::-1], (1, 3, 0, 2)).reshape(3 * C, 3 * HID)
    bias = hidden_bias_vector[:, None]
    out_weight = output_pointwise_weight
    out_back = output_pointwise_weight.T

    ext, sent, ground = call(
        extend_kernel, (shape(16 * C), shape(14 * C), shape(12 * C)), [], 0, 1 << 20
    )(own, bg_rows, above, below)
    earlier = ring(sent, "tm", 1)
    later = ring(sent, "tm", -1)
    sums = call(
        sums_kernel, jax.ShapeDtypeStruct((12, 72, LON), F32), [], 12 * 2 * 80 * OBS * LON, 1 << 20
    )(obs_values[0], obs_index, above, below)
    active, forecast = call(
        functools.partial(forward_kernel, 14),
        (shape(14 * HID), shape(14 * C)),
        [pltpu.VMEM((3, 16 * C, LON), BF16)],
        14 * 2 * LON * HID * 10 * C, 2 << 20,
    )(ext, forward_weight, bias, out_weight)
    state, sent = call(
        first_kernel,
        (shape(12 * C), shape(10 * C)),
        gradient_scratch(12),
        28 * 2 * LON * HID * 10 * C, 2 << 20,
    )(
        earlier, later, ext, active, forecast, ground, sums, forward_weight, back_weight, bias,
        out_weight, out_back,
    )
    earlier = ring(sent, "tm", 1)
    later = ring(sent, "tm", -1)
    active, forecast = call(
        functools.partial(forward_kernel, 10),
        (shape(10 * HID), shape(10 * C)),
        [pltpu.VMEM((3, 12 * C, LON), BF16)],
        10 * 2 * LON * HID * 10 * C, 2 << 20,
    )(state, forward_weight, bias, out_weight)
    analysis = call(
        second_kernel,
        jax.ShapeDtypeStruct((C, ROWS, LON), BF16),
        gradient_scratch(8) + [pltpu.VMEM((C, ROWS, LON), F32)],
        20 * 2 * LON * HID * 10 * C, 2 << 20,
    )(
        earlier, later, state, active, forecast, ground, sums, forward_weight, back_weight, bias,
        out_weight, out_back,
    )
    return analysis[None]


def solution(mesh):
    placed = (
        P("tm", None, "lat", None),
        P(None, "lat", None),
        P("tm", None, "lat"),
        P("tm", "lat"),
        P(),
        P(),
        P(),
    )
    return jax.shard_map(
        on_device, mesh=mesh, in_specs=placed, out_specs=P("tm", None, "lat", None), check_vma=False
    )
```

```python
import functools

import jax
import jax.numpy as jnp
from jax import lax
from jax.experimental import pallas as pl
from jax.experimental.pallas import tpu as pltpu
from jax.sharding import PartitionSpec as P

C = 64
HID = 256
ROWS = 8
LON = 128
OBS = 256
STEP = 0.3

F32 = jnp.float32
BF16 = jnp.bfloat16
VMEM = pl.BlockSpec(memory_space=pltpu.VMEM)

X_PART = 4 * C
PAYLOAD = X_PART + 2 * C


def call(kernel, outs, scratch, flops, bytes_accessed, spec=VMEM, grant=48 << 20):
    def run(*args):
        return pl.pallas_call(
            kernel,
            out_shape=outs,
            in_specs=[spec] * len(args),
            out_specs=jax.tree.map(lambda _: VMEM, outs),
            scratch_shapes=scratch,
            cost_estimate=pl.CostEstimate(
                flops=flops, bytes_accessed=bytes_accessed, transcendentals=0
            ),
            compiler_params=pltpu.CompilerParams(vmem_limit_bytes=grant),
        )(*args)

    return run


def rows_of(ref, first, width=C):
    return ref[first * width : (first + 1) * width, :]


def local_cells(index):
    local = index - lax.axis_index("lat") * (ROWS * LON)
    high = lax.shift_right_arithmetic(local, 7)
    return local - high * LON, high


def with_ones(values):
    return jnp.concatenate([values, jnp.ones((16, OBS), BF16)], axis=0)


def observation_sums(values, low, high, row):
    cell = lax.broadcasted_iota(jnp.int32, (LON, OBS), 0)
    hit = jnp.where((low == cell) & (high == row), 1.0, 0.0).astype(BF16)
    return lax.dot_general(
        values, hit, (((1,), (1,)), ((), ())), preferred_element_type=F32
    )


def innovation_of(sums, own):
    return sums[C : C + 1, :] * own - sums[:C, :]


def pack_kernel(
    x_hbm, bg_hbm, obs_hbm, index_hbm, own_ref, bg_rows_ref, up_ref, down_ref,
    x_ref, bg_ref, obs_ref, index_ref, xs, bs, sems,
):
    copies = [
        pltpu.make_async_copy(source, target, sems.at[place])
        for place, (source, target) in enumerate(
            ((x_hbm, x_ref), (obs_hbm, obs_ref), (index_hbm, index_ref), (bg_hbm, bg_ref))
        )
    ]
    for copy in copies:
        copy.start()
    copies[0].wait()
    xs[...] = x_ref[...].astype(F32)
    for row in range(ROWS):
        value = xs[:, row, :].astype(BF16)
        own_ref[row * C : (row + 1) * C, :] = value
        if row < 4:
            up_ref[row * C : (row + 1) * C, :] = value
        else:
            down_ref[(row - 4) * C : (row - 3) * C, :] = value
    copies[1].wait()
    copies[2].wait()
    low, high = local_cells(index_ref[...])
    values = with_ones(obs_ref[...])
    sums = [observation_sums(values, low, high, row) for row in (0, 1, 6, 7)]
    copies[3].wait()
    bs[...] = bg_ref[...].astype(F32)
    opening = lax.axis_index("tm") == 0
    for row in range(ROWS):
        ground = bs[:, row, :]
        bg_rows_ref[row * C : (row + 1) * C, :] = ground.astype(BF16)
        if row < 2 or row >= 6:
            own = xs[:, row, :]
            edge = innovation_of(sums[row if row < 2 else row - 4], own)
            edge = edge + jnp.where(opening, own - ground, 0.0)
            ref, place = (up_ref, row) if row < 2 else (down_ref, row - 6)
            ref[X_PART + place * C : X_PART + (place + 1) * C, :] = edge.astype(BF16)


def extend_kernel(own_ref, above_ref, below_ref, ext_ref, sent_ref):
    strip = lax.axis_index("lat")
    first = strip > 0
    last = strip < lax.axis_size("lat") - 1
    zero = jnp.zeros((X_PART, LON), BF16)
    above = jnp.where(first, above_ref[:X_PART, :], zero)
    below = jnp.where(last, below_ref[:X_PART, :], zero)
    ext_ref[:X_PART, :] = above
    ext_ref[X_PART : X_PART + ROWS * C, :] = own_ref[...]
    ext_ref[X_PART + ROWS * C :, :] = below
    sent_ref[: 3 * C, :] = above[C:, :]
    sent_ref[3 * C : 11 * C, :] = own_ref[...]
    sent_ref[11 * C :, :] = below[: 3 * C, :]


def roll_rows(state_ref, shifted, count):
    for row in range(count):
        at = slice(row * C, (row + 1) * C)
        value = state_ref[at, :]
        wide = value.astype(F32)
        shifted[0, at, :] = pltpu.roll(wide, 1, 1).astype(BF16)
        shifted[1, at, :] = value
        shifted[2, at, :] = pltpu.roll(wide, LON - 1, 1).astype(BF16)


def hidden(shifted, kernel_ref, bias, row):
    def stack(first):
        return jnp.concatenate(
            [
                shifted[b, (first + a) * C : (first + a + 1) * C, :]
                for a in range(3)
                for b in range(3)
            ],
            axis=0,
        )

    cells = jnp.concatenate([stack(row), stack(row + 1)], axis=1)
    before = jnp.dot(kernel_ref[...], cells, preferred_element_type=F32) + bias
    return jnp.tanh(before).astype(BF16)


def side_by_side(ref, first):
    return jnp.concatenate([rows_of(ref, first), rows_of(ref, first + 1)], axis=1)


def store_pair(ref, first, value, width=C):
    ref[first * width : (first + 1) * width, :] = value[:, :LON]
    ref[(first + 1) * width : (first + 2) * width, :] = value[:, LON:]


def forward_part(count, state_ref, kernel_ref, bias_ref, out_weight_ref, active_ref, forecast_ref, shifted):
    roll_rows(state_ref, shifted, count + 2)
    bias = jnp.concatenate([bias_ref[...], bias_ref[...]], axis=1)
    for row in range(0, count, 2):
        active = hidden(shifted, kernel_ref, bias, row)
        store_pair(active_ref, row, active, HID)
        step = jnp.dot(out_weight_ref[...], active, preferred_element_type=F32)
        centre = side_by_side(state_ref, row + 1).astype(F32)
        store_pair(forecast_ref, row, (centre + step).astype(BF16))


def prepare_kernel(
    obs_ref, index_ref, kernel_ref, bias_ref, out_weight_ref, sums_ref, forward_ref, back_ref,
    wide_bias_ref, out_back_ref,
):
    low, high = local_cells(index_ref[...])
    values = with_ones(obs_ref[...])
    for row in range(ROWS):
        sums_ref[row] = observation_sums(values, low, high, row)[:72, :]
    forward_ref[...] = kernel_ref[...].T
    out_back_ref[...] = out_weight_ref[...].T
    wide_bias_ref[...] = jnp.broadcast_to(bias_ref[...], (LON, HID)).T
    for a in range(3):
        back_ref[:, a * HID : (a + 1) * HID] = kernel_ref[(2 - a) * 3 * C : (3 - a) * 3 * C, :]


def residual_kernel(
    count, margin, prev_ref, own_ref, bg_ref, kernel_ref, bias_ref, out_weight_ref, resid_ref, shifted
):
    roll_rows(prev_ref, shifted, count + 2)
    bias = jnp.concatenate([bias_ref[...], bias_ref[...]], axis=1)
    opening = lax.axis_index("tm") == 0
    for row in range(0, count, 2):
        active = hidden(shifted, kernel_ref, bias, row)
        step = jnp.dot(out_weight_ref[...], active, preferred_element_type=F32)
        centre = side_by_side(prev_ref, row + 1).astype(F32)
        guess = (centre + step).astype(BF16).astype(F32)
        own = side_by_side(own_ref, row + 2).astype(F32)
        latitude = row - margin
        known = side_by_side(bg_ref, latitude).astype(F32) if 0 <= latitude < ROWS else own
        guess = jnp.where(opening, known, guess)
        store_pair(resid_ref, row, (own - guess).astype(BF16))


def gradient_part(
    count, margin, next_ref, own_ref, active_ref, forecast_ref, resid_ref, innovation, back_ref,
    out_back_ref, emit, cot, target,
):
    strip = lax.axis_index("lat")
    top = -strip * ROWS
    bottom = (lax.axis_size("lat") - strip) * ROWS
    for row in range(0, count + 2, 2):
        later = side_by_side(next_ref, row).astype(F32) - side_by_side(forecast_ref, row).astype(F32)
        later = later.astype(BF16)
        store_pair(target, row, later)
        projected = jnp.dot(out_back_ref[...], later, preferred_element_type=F32)
        for half in range(2):
            place = row + half - margin - 1
            active = rows_of(active_ref, row + half, HID).astype(F32)
            value = (1.0 - active * active) * projected[:, half * LON : (half + 1) * LON]
            if not 0 <= place < ROWS:
                value = jnp.where((place >= top) & (place < bottom), value, 0.0)
            cot[(row + half) * HID : (row + half + 1) * HID, :] = value.astype(BF16)
    closing = lax.axis_index("tm") == lax.axis_size("tm") - 1
    for row in range(0, count, 2):
        cells = jnp.concatenate(
            [cot[row * HID : (row + 3) * HID, :], cot[(row + 1) * HID : (row + 4) * HID, :]], axis=1
        )
        spread = jnp.dot(back_ref[...], cells, preferred_element_type=F32)
        for half in range(2):
            lanes = slice(half * LON, (half + 1) * LON)
            pulled = (
                pltpu.roll(spread[:C, lanes], LON - 1, 1)
                + spread[C : 2 * C, lanes]
                + pltpu.roll(spread[2 * C :, lanes], 1, 1)
            )
            place = row + half
            later = rows_of(target, place + 1).astype(F32)
            adjoint = jnp.where(closing, 0.0, (later + pulled).astype(BF16).astype(F32))
            own = rows_of(own_ref, place + 2).astype(F32)
            latitude = place - margin
            gradient = rows_of(resid_ref, place).astype(F32) - adjoint + innovation(latitude, own)
            value = own - STEP * gradient
            if not 0 <= latitude < ROWS:
                value = jnp.where((latitude >= top) & (latitude < bottom), value, 0.0)
            emit(place, value)


def first_kernel(
    next_ref, ext_ref, active_ref, forecast_ref, resid_ref, sums_ref, above_ref, below_ref,
    back_ref, out_back_ref, state_ref, sent_ref, cot, target,
):
    def innovation(latitude, own):
        if latitude < 0:
            return rows_of(above_ref, 6 + latitude).astype(F32)
        if latitude >= ROWS:
            return rows_of(below_ref, 4 + latitude - ROWS).astype(F32)
        return innovation_of(sums_ref[latitude], own)

    def emit(place, value):
        value = value.astype(BF16)
        state_ref[place * C : (place + 1) * C, :] = value
        if 1 <= place < 11:
            sent_ref[(place - 1) * C : place * C, :] = value

    gradient_part(
        12, 2, next_ref, ext_ref, active_ref, forecast_ref, resid_ref, innovation, back_ref,
        out_back_ref, emit, cot, target,
    )


def second_kernel(
    next_ref, state_ref, active_ref, forecast_ref, resid_ref, sums_ref, back_ref, out_back_ref,
    out_ref, cot, target, wide,
):
    def emit(place, value):
        wide[:, place, :] = value

    gradient_part(
        8, 0, next_ref, state_ref, active_ref, forecast_ref, resid_ref,
        lambda latitude, own: innovation_of(sums_ref[latitude], own), back_ref, out_back_ref, emit,
        cot, target,
    )
    out_ref[...] = wide[...].astype(BF16)


def ring(value, axis, by):
    count = lax.axis_size(axis)
    return lax.ppermute(value, axis, [(i, (i + by) % count) for i in range(count)])


def shape(rows, dtype=BF16):
    return jax.ShapeDtypeStruct((rows, LON), dtype)


def shifted_scratch(count):
    return [pltpu.VMEM((3, (count + 2) * C, LON), BF16)]


def gradient_scratch(count):
    return [
        pltpu.VMEM(((count + 2) * HID, LON), BF16),
        pltpu.VMEM(((count + 2) * C, LON), BF16),
    ]


def row_flops(rows):
    return rows * 2 * LON * HID * 10 * C


def on_device(
    window_snapshots, background, obs_values, obs_index, input_kernel_weight, hidden_bias_vector,
    output_pointwise_weight,
):
    own, ground, up, down = call(
        pack_kernel,
        (shape(ROWS * C), shape(ROWS * C), shape(PAYLOAD), shape(PAYLOAD)),
        [
            pltpu.VMEM((C, ROWS, LON), BF16),
            pltpu.VMEM((C, ROWS, LON), BF16),
            pltpu.VMEM((C, OBS), BF16),
            pltpu.VMEM((1, OBS), jnp.int32),
            pltpu.VMEM((C, ROWS, LON), F32),
            pltpu.VMEM((C, ROWS, LON), F32),
            pltpu.SemaphoreType.DMA((4,)),
        ],
        0, 1 << 20, pl.BlockSpec(memory_space=pltpu.HBM),
    )(
        *(
            pltpu.with_memory_space_constraint(value, pltpu.HBM)
            for value in (window_snapshots[0], background, obs_values[0], obs_index)
        )
    )
    below = ring(up, "lat", -1)
    above = ring(down, "lat", 1)

    out_weight = output_pointwise_weight
    taps = jnp.transpose(input_kernel_weight, (0, 1, 3, 2)).reshape(9 * C, HID)
    prepared = call(
        prepare_kernel,
        (
            jax.ShapeDtypeStruct((ROWS, 72, LON), F32),
            jax.ShapeDtypeStruct((HID, 9 * C), BF16),
            jax.ShapeDtypeStruct((3 * C, 3 * HID), BF16),
            jax.ShapeDtypeStruct((HID, LON), F32),
            jax.ShapeDtypeStruct((HID, C), BF16),
        ),
        [], ROWS * 2 * 80 * OBS * LON, 1 << 20,
    )(obs_values[0], obs_index, taps, hidden_bias_vector[None, :], out_weight)
    above, below, prepared = lax.optimization_barrier((above, below, prepared))
    sums, forward_weight, back_weight, bias, out_back = prepared

    ext, sent = call(extend_kernel, (shape(16 * C), shape(14 * C)), [], 0, 1 << 20)(
        own, above, below
    )
    earlier = ring(sent, "tm", 1)
    later = ring(sent, "tm", -1)

    def forward(count, state):
        return call(
            functools.partial(forward_part, count),
            (shape(count * HID), shape(count * C)),
            shifted_scratch(count),
            row_flops(count), 2 << 20,
        )(state, forward_weight, bias, out_weight)

    def residual(count, margin, prev, state):
        return call(
            functools.partial(residual_kernel, count, margin),
            shape(count * C), shifted_scratch(count), row_flops(count), 2 << 20,
        )(prev, state, ground, forward_weight, bias, out_weight)

    active, forecast = forward(14, ext)
    resid = residual(12, 2, earlier, ext)
    state, sent = call(
        first_kernel, (shape(12 * C), shape(10 * C)), gradient_scratch(12), row_flops(12), 2 << 20
    )(later, ext, active, forecast, resid, sums, above, below, back_weight, out_back)
    earlier = ring(sent, "tm", 1)
    later = ring(sent, "tm", -1)
    active, forecast = forward(10, state)
    resid = residual(8, 0, earlier, state)
    analysis = call(
        second_kernel,
        jax.ShapeDtypeStruct((C, ROWS, LON), BF16),
        gradient_scratch(8) + [pltpu.VMEM((C, ROWS, LON), F32)],
        row_flops(8), 2 << 20,
    )(later, state, active, forecast, resid, sums, back_weight, out_back)
    return analysis[None]


def solution(mesh):
    placed = (
        P("tm", None, "lat", None),
        P(None, "lat", None),
        P("tm", None, "lat"),
        P("tm", "lat"),
        P(),
        P(),
        P(),
    )
    return jax.shard_map(
        on_device, mesh=mesh, in_specs=placed, out_specs=P("tm", None, "lat", None), check_vma=False
    )
```

```python
import functools

import jax
import jax.numpy as jnp
from jax import lax
from jax.experimental import pallas as pl
from jax.experimental.pallas import tpu as pltpu
from jax.sharding import PartitionSpec as P


C = 64
HID = 256
ROWS = 8
LON = 128
OBS = 256
STEP = 0.3

F32 = jnp.float32
BF16 = jnp.bfloat16
VMEM = pl.BlockSpec(memory_space=pltpu.VMEM)

X_PART = 4 * C
PAYLOAD = X_PART + 2 * C


def call(kernel, outs, scratch, flops, bytes_accessed, spec=VMEM, grant=48 << 20):
    def run(*args):
        return pl.pallas_call(
            kernel,
            out_shape=outs,
            in_specs=[spec] * len(args),
            out_specs=jax.tree.map(lambda _: VMEM, outs),
            scratch_shapes=scratch,
            cost_estimate=pl.CostEstimate(
                flops=flops, bytes_accessed=bytes_accessed, transcendentals=0
            ),
            compiler_params=pltpu.CompilerParams(vmem_limit_bytes=grant),
        )(*args)

    return run


def rows_of(ref, first, width=C):
    return ref[first * width : (first + 1) * width, :]


def latitude(row):
    return pl.ds(row, C, stride=ROWS)


def local_cells(index):
    local = index - lax.axis_index("lat") * (ROWS * LON)
    high = lax.shift_right_arithmetic(local, 7)
    return local - high * LON, high


def with_ones(values):
    return jnp.concatenate([values, jnp.ones((16, OBS), BF16)], axis=0)


def observation_sums(values, low, high, row):
    cell = lax.broadcasted_iota(jnp.int32, (LON, OBS), 0)
    hit = jnp.where((low == cell) & (high == row), 1.0, 0.0).astype(BF16)
    return lax.dot_general(
        values, hit, (((1,), (1,)), ((), ())), preferred_element_type=F32
    )


def innovation_of(sums, own):
    return sums[C : C + 1, :] * own - sums[:C, :]


def pack_kernel(
    x_hbm, bg_hbm, obs_hbm, index_hbm, own_ref, bg_rows_ref, up_ref, down_ref,
    x_ref, bg_ref, obs_ref, index_ref, xs, bs, sems,
):
    copies = [
        pltpu.make_async_copy(source, target, sems.at[place])
        for place, (source, target) in enumerate(
            ((x_hbm, x_ref), (obs_hbm, obs_ref), (index_hbm, index_ref), (bg_hbm, bg_ref))
        )
    ]
    for copy in copies:
        copy.start()
    copies[0].wait()
    xs[...] = x_ref[...].astype(F32).reshape(ROWS * C, LON)
    for row in range(ROWS):
        value = xs[latitude(row), :].astype(BF16)
        own_ref[row * C : (row + 1) * C, :] = value
        if row < 4:
            up_ref[row * C : (row + 1) * C, :] = value
        else:
            down_ref[(row - 4) * C : (row - 3) * C, :] = value
    copies[1].wait()
    copies[2].wait()
    low, high = local_cells(index_ref[...])
    values = with_ones(obs_ref[...])
    sums = [observation_sums(values, low, high, row) for row in (0, 1, 6, 7)]
    copies[3].wait()
    bs[...] = bg_ref[...].astype(F32).reshape(ROWS * C, LON)
    opening = lax.axis_index("tm") == 0
    for row in range(ROWS):
        ground = bs[latitude(row), :]
        bg_rows_ref[row * C : (row + 1) * C, :] = ground.astype(BF16)
        if row < 2 or row >= 6:
            own = xs[latitude(row), :]
            edge = innovation_of(sums[row if row < 2 else row - 4], own)
            edge = edge + jnp.where(opening, own - ground, 0.0)
            ref, place = (up_ref, row) if row < 2 else (down_ref, row - 6)
            ref[X_PART + place * C : X_PART + (place + 1) * C, :] = edge.astype(BF16)


def extend_kernel(own_ref, above_ref, below_ref, ext_ref, sent_ref):
    strip = lax.axis_index("lat")
    first = strip > 0
    last = strip < lax.axis_size("lat") - 1
    zero = jnp.zeros((X_PART, LON), BF16)
    above = jnp.where(first, above_ref[:X_PART, :], zero)
    below = jnp.where(last, below_ref[:X_PART, :], zero)
    ext_ref[:X_PART, :] = above
    ext_ref[X_PART : X_PART + ROWS * C, :] = own_ref[...]
    ext_ref[X_PART + ROWS * C :, :] = below
    sent_ref[: 3 * C, :] = above[C:, :]
    sent_ref[3 * C : 11 * C, :] = own_ref[...]
    sent_ref[11 * C :, :] = below[: 3 * C, :]


def roll_rows(state_ref, shifted, count):
    for row in range(count):
        at = slice(row * C, (row + 1) * C)
        value = state_ref[at, :]
        wide = value.astype(F32)
        shifted[0, at, :] = pltpu.roll(wide, 1, 1).astype(BF16)
        shifted[1, at, :] = value
        shifted[2, at, :] = pltpu.roll(wide, LON - 1, 1).astype(BF16)


def hidden(shifted, kernel_ref, bias, row):
    def stack(first):
        return jnp.concatenate(
            [
                shifted[b, (first + a) * C : (first + a + 1) * C, :]
                for a in range(3)
                for b in range(3)
            ],
            axis=0,
        )

    cells = jnp.concatenate([stack(row), stack(row + 1)], axis=1)
    before = jnp.dot(kernel_ref[...], cells, preferred_element_type=F32) + bias
    return jnp.tanh(before).astype(BF16)


def side_by_side(ref, first):
    return jnp.concatenate([rows_of(ref, first), rows_of(ref, first + 1)], axis=1)


def store_pair(ref, first, value, width=C):
    ref[first * width : (first + 1) * width, :] = value[:, :LON]
    ref[(first + 1) * width : (first + 2) * width, :] = value[:, LON:]


def forward_part(count, state_ref, kernel_ref, bias_ref, out_weight_ref, active_ref, forecast_ref, shifted):
    roll_rows(state_ref, shifted, count + 2)
    bias = jnp.concatenate([bias_ref[...], bias_ref[...]], axis=1)
    for row in range(0, count, 2):
        active = hidden(shifted, kernel_ref, bias, row)
        store_pair(active_ref, row, active, HID)
        step = jnp.dot(out_weight_ref[...], active, preferred_element_type=F32)
        centre = side_by_side(state_ref, row + 1).astype(F32)
        store_pair(forecast_ref, row, (centre + step).astype(BF16))


def prepare_kernel(
    obs_ref, index_ref, kernel_ref, bias_ref, out_weight_ref, sums_ref, forward_ref, back_ref,
    wide_bias_ref, out_back_ref,
):
    low, high = local_cells(index_ref[...])
    values = with_ones(obs_ref[...])
    for row in range(ROWS):
        sums_ref[row] = observation_sums(values, low, high, row)[:72, :]
    forward_ref[...] = kernel_ref[...].T
    out_back_ref[...] = out_weight_ref[...].T
    wide_bias_ref[...] = jnp.broadcast_to(bias_ref[...], (LON, HID)).T
    for a in range(3):
        back_ref[:, a * HID : (a + 1) * HID] = kernel_ref[(2 - a) * 3 * C : (3 - a) * 3 * C, :]


def residual_part(
    count, margin, prev_ref, own_ref, bg_ref, kernel_ref, bias_ref, out_weight_ref, shifted, take
):
    roll_rows(prev_ref, shifted, count + 2)
    bias = jnp.concatenate([bias_ref[...], bias_ref[...]], axis=1)
    opening = lax.axis_index("tm") == 0
    for row in range(0, count, 2):
        active = hidden(shifted, kernel_ref, bias, row)
        step = jnp.dot(out_weight_ref[...], active, preferred_element_type=F32)
        centre = side_by_side(prev_ref, row + 1).astype(F32)
        guess = (centre + step).astype(BF16).astype(F32)
        own = side_by_side(own_ref, row + 2).astype(F32)
        place = row - margin
        known = side_by_side(bg_ref, place).astype(F32) if 0 <= place < ROWS else own
        resid = (own - jnp.where(opening, known, guess)).astype(BF16)
        take(row, resid[:, :LON])
        take(row + 1, resid[:, LON:])


def strip_ends():
    strip = lax.axis_index("lat")
    return -strip * ROWS, (lax.axis_size("lat") - strip) * ROWS


def adjoint_part(
    count, margin, next_ref, active_ref, forecast_ref, back_ref, out_back_ref, cot, target, take
):
    top, bottom = strip_ends()
    for row in range(0, count + 2, 2):
        later = side_by_side(next_ref, row).astype(F32) - side_by_side(forecast_ref, row).astype(F32)
        later = later.astype(BF16)
        store_pair(target, row, later)
        projected = jnp.dot(out_back_ref[...], later, preferred_element_type=F32)
        for half in range(2):
            place = row + half - margin - 1
            active = rows_of(active_ref, row + half, HID).astype(F32)
            value = (1.0 - active * active) * projected[:, half * LON : (half + 1) * LON]
            if not 0 <= place < ROWS:
                value = jnp.where((place >= top) & (place < bottom), value, 0.0)
            cot[(row + half) * HID : (row + half + 1) * HID, :] = value.astype(BF16)
    closing = lax.axis_index("tm") == lax.axis_size("tm") - 1
    for row in range(0, count, 2):
        cells = jnp.concatenate(
            [cot[row * HID : (row + 3) * HID, :], cot[(row + 1) * HID : (row + 4) * HID, :]], axis=1
        )
        spread = jnp.dot(back_ref[...], cells, preferred_element_type=F32)
        for half in range(2):
            lanes = slice(half * LON, (half + 1) * LON)
            pulled = (
                pltpu.roll(spread[:C, lanes], LON - 1, 1)
                + spread[C : 2 * C, lanes]
                + pltpu.roll(spread[2 * C :, lanes], 1, 1)
            )
            later = rows_of(target, row + half + 1).astype(F32)
            take(row + half, jnp.where(closing, 0.0, later + pulled).astype(BF16))


def is_even():
    return lax.rem(lax.axis_index("tm"), 2) == 0


def near_kernel(
    count, margin, near_ref, own_ref, bg_ref, active_ref, forecast_ref, kernel_ref, bias_ref,
    out_weight_ref, back_ref, out_back_ref, part_ref, shifted, cot, target,
):
    def take(row, value):
        part_ref[row * C : (row + 1) * C, :] = value

    even = is_even()

    @pl.when(even)
    def _():
        adjoint_part(
            count, margin, near_ref, active_ref, forecast_ref, back_ref, out_back_ref, cot, target, take
        )

    @pl.when(jnp.logical_not(even))
    def _():
        residual_part(
            count, margin, near_ref, own_ref, bg_ref, kernel_ref, bias_ref, out_weight_ref, shifted, take
        )


def far_part(
    count, margin, far_ref, part_ref, own_ref, bg_ref, active_ref, forecast_ref, kernel_ref, bias_ref,
    out_weight_ref, back_ref, out_back_ref, innovation, emit, shifted, cot, target,
):
    top, bottom = strip_ends()

    def step(row, resid, adjoint):
        own = rows_of(own_ref, row + 2).astype(F32)
        place = row - margin
        gradient = resid.astype(F32) - adjoint.astype(F32) + innovation(place, own)
        value = own - STEP * gradient
        if not 0 <= place < ROWS:
            value = jnp.where((place >= top) & (place < bottom), value, 0.0)
        emit(row, value)

    even = is_even()

    @pl.when(even)
    def _():
        residual_part(
            count, margin, far_ref, own_ref, bg_ref, kernel_ref, bias_ref, out_weight_ref, shifted,
            lambda row, resid: step(row, resid, rows_of(part_ref, row)),
        )

    @pl.when(jnp.logical_not(even))
    def _():
        adjoint_part(
            count, margin, far_ref, active_ref, forecast_ref, back_ref, out_back_ref, cot, target,
            lambda row, adjoint: step(row, rows_of(part_ref, row), adjoint),
        )


def first_kernel(
    far_ref, part_ref, own_ref, bg_ref, active_ref, forecast_ref, kernel_ref, bias_ref,
    out_weight_ref, back_ref, out_back_ref, sums_ref, above_ref, below_ref, state_ref, sent_ref,
    shifted, cot, target,
):
    def innovation(place, own):
        if place < 0:
            return rows_of(above_ref, 6 + place).astype(F32)
        if place >= ROWS:
            return rows_of(below_ref, 4 + place - ROWS).astype(F32)
        return innovation_of(sums_ref[place], own)

    def emit(row, value):
        value = value.astype(BF16)
        state_ref[row * C : (row + 1) * C, :] = value
        if 1 <= row < 11:
            sent_ref[(row - 1) * C : row * C, :] = value

    far_part(
        12, 2, far_ref, part_ref, own_ref, bg_ref, active_ref, forecast_ref, kernel_ref, bias_ref,
        out_weight_ref, back_ref, out_back_ref, innovation, emit, shifted, cot, target,
    )


def second_kernel(
    far_ref, part_ref, own_ref, bg_ref, active_ref, forecast_ref, kernel_ref, bias_ref,
    out_weight_ref, back_ref, out_back_ref, sums_ref, out_ref, shifted, cot, target, wide,
):
    def emit(place, value):
        wide[latitude(place), :] = value

    far_part(
        8, 0, far_ref, part_ref, own_ref, bg_ref, active_ref, forecast_ref, kernel_ref, bias_ref,
        out_weight_ref, back_ref, out_back_ref,
        lambda place, own: innovation_of(sums_ref[place], own), emit, shifted, cot, target,
    )
    out_ref[...] = wide[...].reshape(C, ROWS, LON).astype(BF16)


def ring(value, axis, by):
    count = lax.axis_size(axis)
    return lax.ppermute(value, axis, [(i, (i + by) % count) for i in range(count)])


def swap(value, first):
    count = lax.axis_size("tm")
    pairs = [(i, (i + 1) % count) for i in range(first, count, 2)]
    return lax.ppermute(value, "tm", pairs + [(j, i) for i, j in pairs])


def shape(rows, dtype=BF16):
    return jax.ShapeDtypeStruct((rows, LON), dtype)


def shifted_scratch(count):
    return [pltpu.VMEM((3, (count + 2) * C, LON), BF16)]


def gradient_scratch(count):
    return shifted_scratch(count) + [
        pltpu.VMEM(((count + 2) * HID, LON), BF16),
        pltpu.VMEM(((count + 2) * C, LON), BF16),
    ]


def row_flops(rows):
    return rows * 2 * LON * HID * 10 * C


def on_device(
    window_snapshots, background, obs_values, obs_index, input_kernel_weight, hidden_bias_vector,
    output_pointwise_weight,
):
    own, ground, up, down = call(
        pack_kernel,
        (shape(ROWS * C), shape(ROWS * C), shape(PAYLOAD), shape(PAYLOAD)),
        [
            pltpu.VMEM((C, ROWS, LON), BF16),
            pltpu.VMEM((C, ROWS, LON), BF16),
            pltpu.VMEM((C, OBS), BF16),
            pltpu.VMEM((1, OBS), jnp.int32),
            pltpu.VMEM((C * ROWS, LON), F32),
            pltpu.VMEM((C * ROWS, LON), F32),
            pltpu.SemaphoreType.DMA((4,)),
        ],
        0, 1 << 20, pl.BlockSpec(memory_space=pltpu.HBM),
    )(
        *(
            pltpu.with_memory_space_constraint(value, pltpu.HBM)
            for value in (window_snapshots[0], background, obs_values[0], obs_index)
        )
    )
    below = ring(up, "lat", -1)
    above = ring(down, "lat", 1)

    out_weight = output_pointwise_weight
    taps = jnp.transpose(input_kernel_weight, (0, 1, 3, 2)).reshape(9 * C, HID)
    prepared = call(
        prepare_kernel,
        (
            jax.ShapeDtypeStruct((ROWS, 72, LON), F32),
            jax.ShapeDtypeStruct((HID, 9 * C), BF16),
            jax.ShapeDtypeStruct((3 * C, 3 * HID), BF16),
            jax.ShapeDtypeStruct((HID, LON), F32),
            jax.ShapeDtypeStruct((HID, C), BF16),
        ),
        [], ROWS * 2 * 80 * OBS * LON, 1 << 20,
    )(obs_values[0], obs_index, taps, hidden_bias_vector[None, :], out_weight)
    above, below, prepared = lax.optimization_barrier((above, below, prepared))
    sums, forward_weight, back_weight, bias, out_back = prepared

    ext, sent = call(extend_kernel, (shape(16 * C), shape(14 * C)), [], 0, 1 << 20)(
        own, above, below
    )
    weights = (forward_weight, bias, out_weight, back_weight, out_back)

    def exchange(sent):
        far = swap(sent, 1)
        near = swap(sent, 0)
        return far, near

    def forward(count, state):
        return call(
            functools.partial(forward_part, count),
            (shape(count * HID), shape(count * C)),
            shifted_scratch(count),
            row_flops(count), 2 << 20,
        )(state, forward_weight, bias, out_weight)

    def near_part(count, margin, near, *given):
        return call(
            functools.partial(near_kernel, count, margin),
            shape(count * C), gradient_scratch(count), row_flops(count), 2 << 20,
        )(near, *given)

    far, near = exchange(sent)
    given = (ext, ground, *forward(14, ext), *weights)
    part = near_part(12, 2, near, *given)
    state, sent = call(
        first_kernel, (shape(12 * C), shape(10 * C)), gradient_scratch(12), row_flops(12), 2 << 20
    )(far, part, *given, sums, above, below)
    far, near = exchange(sent)
    given = (state, ground, *forward(10, state), *weights)
    part = near_part(8, 0, near, *given)
    analysis = call(
        second_kernel,
        jax.ShapeDtypeStruct((C, ROWS, LON), BF16),
        gradient_scratch(8) + [pltpu.VMEM((C * ROWS, LON), F32)],
        row_flops(8), 2 << 20,
    )(far, part, *given, sums)
    return analysis[None]


def solution(mesh):
    placed = (
        P("tm", None, "lat", None),
        P(None, "lat", None),
        P("tm", None, "lat"),
        P("tm", "lat"),
        P(),
        P(),
        P(),
    )
    return jax.shard_map(
        on_device, mesh=mesh, in_specs=placed, out_specs=P("tm", None, "lat", None), check_vma=False
    )
```

```python
import functools

import jax
import jax.numpy as jnp
from jax import lax
from jax.experimental import pallas as pl
from jax.experimental.pallas import tpu as pltpu
from jax.sharding import PartitionSpec as P


C = 64
HID = 256
ROWS = 8
LON = 128
OBS = 256
STEP = 0.3

F32 = jnp.float32
BF16 = jnp.bfloat16
VMEM = pl.BlockSpec(memory_space=pltpu.VMEM)

X_PART = 4 * C
PAYLOAD = X_PART + 2 * C


def call(kernel, outs, scratch, flops, bytes_accessed, spec=VMEM, grant=48 << 20):
    def run(*args):
        return pl.pallas_call(
            kernel,
            out_shape=outs,
            in_specs=[spec] * len(args),
            out_specs=jax.tree.map(lambda _: VMEM, outs),
            scratch_shapes=scratch,
            cost_estimate=pl.CostEstimate(
                flops=flops, bytes_accessed=bytes_accessed, transcendentals=0
            ),
            compiler_params=pltpu.CompilerParams(vmem_limit_bytes=grant),
        )(*args)

    return run


def rows_of(ref, first, width=C):
    return ref[first * width : (first + 1) * width, :]


def latitude(row):
    return pl.ds(row, C, stride=ROWS)


def local_cells(index):
    local = index - lax.axis_index("lat") * (ROWS * LON)
    high = lax.shift_right_arithmetic(local, 7)
    return local - high * LON, high


def with_ones(values):
    return jnp.concatenate([values, jnp.ones((16, OBS), BF16)], axis=0)


def observation_sums(values, low, high, row):
    cell = lax.broadcasted_iota(jnp.int32, (LON, OBS), 0)
    hit = jnp.where((low == cell) & (high == row), 1.0, 0.0).astype(BF16)
    return lax.dot_general(
        values, hit, (((1,), (1,)), ((), ())), preferred_element_type=F32
    )


def innovation_of(sums, own):
    return sums[C : C + 1, :] * own - sums[:C, :]


def pack_kernel(
    x_hbm, bg_hbm, obs_hbm, index_hbm, own_ref, bg_rows_ref, first_ref, second_ref,
    x_ref, bg_ref, obs_ref, index_ref, xs, bs, sems,
):
    copies = [
        pltpu.make_async_copy(source, target, sems.at[place])
        for place, (source, target) in enumerate(
            ((x_hbm, x_ref), (obs_hbm, obs_ref), (index_hbm, index_ref), (bg_hbm, bg_ref))
        )
    ]
    for copy in copies:
        copy.start()
    copies[0].wait()
    even = lax.rem(lax.axis_index("lat"), 2) == 0

    def send(place, up, down):
        at = slice(place * C, (place + 1) * C)
        first_ref[at, :] = jnp.where(even, down, up).astype(BF16)
        second_ref[at, :] = jnp.where(even, up, down).astype(BF16)

    xs[...] = x_ref[...].astype(F32).reshape(ROWS * C, LON)
    for row in range(4):
        up, down = xs[latitude(row), :], xs[latitude(row + 4), :]
        own_ref[row * C : (row + 1) * C, :] = up.astype(BF16)
        own_ref[(row + 4) * C : (row + 5) * C, :] = down.astype(BF16)
        send(row, up, down)
    copies[1].wait()
    copies[2].wait()
    low, high = local_cells(index_ref[...])
    values = with_ones(obs_ref[...])
    copies[3].wait()
    bs[...] = bg_ref[...].astype(F32).reshape(ROWS * C, LON)
    opening = lax.axis_index("tm") == 0

    def edge(row):
        own = xs[latitude(row), :]
        ground = bs[latitude(row), :]
        value = innovation_of(observation_sums(values, low, high, row), own)
        return value + jnp.where(opening, own - ground, 0.0)

    for row in range(2):
        send(4 + row, edge(row), edge(row + 6))
    for row in range(ROWS):
        bg_rows_ref[row * C : (row + 1) * C, :] = bs[latitude(row), :].astype(BF16)


def extend_kernel(own_ref, first_ref, second_ref, ext_ref, sent_ref, above_edge_ref, below_edge_ref):
    strip = lax.axis_index("lat")
    even = lax.rem(strip, 2) == 0
    zero = jnp.zeros((X_PART, LON), BF16)
    above = jnp.where(even, second_ref[...], first_ref[...])
    below = jnp.where(even, first_ref[...], second_ref[...])
    above_edge_ref[...] = above[X_PART:, :]
    below_edge_ref[...] = below[X_PART:, :]
    above = jnp.where(strip > 0, above[:X_PART, :], zero)
    below = jnp.where(strip < lax.axis_size("lat") - 1, below[:X_PART, :], zero)
    ext_ref[:X_PART, :] = above
    ext_ref[X_PART : X_PART + ROWS * C, :] = own_ref[...]
    ext_ref[X_PART + ROWS * C :, :] = below
    sent_ref[: 3 * C, :] = above[C:, :]
    sent_ref[3 * C : 11 * C, :] = own_ref[...]
    sent_ref[11 * C :, :] = below[: 3 * C, :]


def roll_rows(state_ref, shifted, count):
    for row in range(count):
        at = slice(row * C, (row + 1) * C)
        value = state_ref[at, :]
        wide = value.astype(F32)
        shifted[0, at, :] = pltpu.roll(wide, 1, 1).astype(BF16)
        shifted[1, at, :] = value
        shifted[2, at, :] = pltpu.roll(wide, LON - 1, 1).astype(BF16)


def hidden(shifted, kernel_ref, bias, row):
    def stack(first):
        return jnp.concatenate(
            [
                shifted[b, (first + a) * C : (first + a + 1) * C, :]
                for a in range(3)
                for b in range(3)
            ],
            axis=0,
        )

    cells = jnp.concatenate([stack(row), stack(row + 1)], axis=1)
    before = jnp.dot(kernel_ref[...], cells, preferred_element_type=F32) + bias
    return jnp.tanh(before).astype(BF16)


def side_by_side(ref, first):
    return jnp.concatenate([rows_of(ref, first), rows_of(ref, first + 1)], axis=1)


def store_pair(ref, first, value, width=C):
    ref[first * width : (first + 1) * width, :] = value[:, :LON]
    ref[(first + 1) * width : (first + 2) * width, :] = value[:, LON:]


def forward_part(count, state_ref, kernel_ref, bias_ref, out_weight_ref, active_ref, forecast_ref, shifted):
    roll_rows(state_ref, shifted, count + 2)
    bias = jnp.concatenate([bias_ref[...], bias_ref[...]], axis=1)
    for row in range(0, count, 2):
        active = hidden(shifted, kernel_ref, bias, row)
        store_pair(active_ref, row, active, HID)
        step = jnp.dot(out_weight_ref[...], active, preferred_element_type=F32)
        centre = side_by_side(state_ref, row + 1).astype(F32)
        store_pair(forecast_ref, row, (centre + step).astype(BF16))


def prepare_kernel(
    obs_ref, index_ref, kernel_ref, bias_ref, out_weight_ref, sums_ref, forward_ref, back_ref,
    wide_bias_ref, out_back_ref,
):
    low, high = local_cells(index_ref[...])
    values = with_ones(obs_ref[...])
    for row in range(ROWS):
        sums_ref[row] = observation_sums(values, low, high, row)[:72, :]
    forward_ref[...] = kernel_ref[...].T
    out_back_ref[...] = out_weight_ref[...].T
    wide_bias_ref[...] = jnp.broadcast_to(bias_ref[...], (LON, HID)).T
    for a in range(3):
        back_ref[:, a * HID : (a + 1) * HID] = kernel_ref[(2 - a) * 3 * C : (3 - a) * 3 * C, :]


def residual_part(
    count, margin, prev_ref, own_ref, bg_ref, kernel_ref, bias_ref, out_weight_ref, shifted, take
):
    roll_rows(prev_ref, shifted, count + 2)
    bias = jnp.concatenate([bias_ref[...], bias_ref[...]], axis=1)
    opening = lax.axis_index("tm") == 0
    for row in range(0, count, 2):
        active = hidden(shifted, kernel_ref, bias, row)
        step = jnp.dot(out_weight_ref[...], active, preferred_element_type=F32)
        centre = side_by_side(prev_ref, row + 1).astype(F32)
        guess = (centre + step).astype(BF16).astype(F32)
        own = side_by_side(own_ref, row + 2).astype(F32)
        place = row - margin
        known = side_by_side(bg_ref, place).astype(F32) if 0 <= place < ROWS else own
        resid = (own - jnp.where(opening, known, guess)).astype(BF16)
        take(row, resid[:, :LON])
        take(row + 1, resid[:, LON:])


def strip_ends():
    strip = lax.axis_index("lat")
    return -strip * ROWS, (lax.axis_size("lat") - strip) * ROWS


def adjoint_part(
    count, margin, next_ref, active_ref, forecast_ref, back_ref, out_back_ref, cot, target, take
):
    top, bottom = strip_ends()
    for row in range(0, count + 2, 2):
        later = side_by_side(next_ref, row).astype(F32) - side_by_side(forecast_ref, row).astype(F32)
        later = later.astype(BF16)
        store_pair(target, row, later)
        projected = jnp.dot(out_back_ref[...], later, preferred_element_type=F32)
        for half in range(2):
            place = row + half - margin - 1
            active = rows_of(active_ref, row + half, HID).astype(F32)
            value = (1.0 - active * active) * projected[:, half * LON : (half + 1) * LON]
            if not 0 <= place < ROWS:
                value = jnp.where((place >= top) & (place < bottom), value, 0.0)
            cot[(row + half) * HID : (row + half + 1) * HID, :] = value.astype(BF16)
    closing = lax.axis_index("tm") == lax.axis_size("tm") - 1
    for row in range(0, count, 2):
        cells = jnp.concatenate(
            [cot[row * HID : (row + 3) * HID, :], cot[(row + 1) * HID : (row + 4) * HID, :]], axis=1
        )
        spread = jnp.dot(back_ref[...], cells, preferred_element_type=F32)
        for half in range(2):
            lanes = slice(half * LON, (half + 1) * LON)
            pulled = (
                pltpu.roll(spread[:C, lanes], LON - 1, 1)
                + spread[C : 2 * C, lanes]
                + pltpu.roll(spread[2 * C :, lanes], 1, 1)
            )
            later = rows_of(target, row + half + 1).astype(F32)
            take(row + half, jnp.where(closing, 0.0, later + pulled).astype(BF16))


def is_even():
    return lax.rem(lax.axis_index("tm"), 2) == 0


def near_kernel(
    count, margin, near_ref, own_ref, bg_ref, active_ref, forecast_ref, kernel_ref, bias_ref,
    out_weight_ref, back_ref, out_back_ref, part_ref, shifted, cot, target,
):
    def take(row, value):
        part_ref[row * C : (row + 1) * C, :] = value

    even = is_even()

    @pl.when(even)
    def _():
        adjoint_part(
            count, margin, near_ref, active_ref, forecast_ref, back_ref, out_back_ref, cot, target, take
        )

    @pl.when(jnp.logical_not(even))
    def _():
        residual_part(
            count, margin, near_ref, own_ref, bg_ref, kernel_ref, bias_ref, out_weight_ref, shifted, take
        )


def far_part(
    count, margin, far_ref, part_ref, own_ref, bg_ref, active_ref, forecast_ref, kernel_ref, bias_ref,
    out_weight_ref, back_ref, out_back_ref, innovation, emit, shifted, cot, target,
):
    top, bottom = strip_ends()

    def step(row, resid, adjoint):
        own = rows_of(own_ref, row + 2).astype(F32)
        place = row - margin
        gradient = resid.astype(F32) - adjoint.astype(F32) + innovation(place, own)
        value = own - STEP * gradient
        if not 0 <= place < ROWS:
            value = jnp.where((place >= top) & (place < bottom), value, 0.0)
        emit(row, value)

    even = is_even()

    @pl.when(even)
    def _():
        residual_part(
            count, margin, far_ref, own_ref, bg_ref, kernel_ref, bias_ref, out_weight_ref, shifted,
            lambda row, resid: step(row, resid, rows_of(part_ref, row)),
        )

    @pl.when(jnp.logical_not(even))
    def _():
        adjoint_part(
            count, margin, far_ref, active_ref, forecast_ref, back_ref, out_back_ref, cot, target,
            lambda row, adjoint: step(row, rows_of(part_ref, row), adjoint),
        )


def first_kernel(
    far_ref, part_ref, own_ref, bg_ref, active_ref, forecast_ref, kernel_ref, bias_ref,
    out_weight_ref, back_ref, out_back_ref, sums_ref, above_ref, below_ref, state_ref, sent_ref,
    shifted, cot, target,
):
    def innovation(place, own):
        if place < 0:
            return rows_of(above_ref, 2 + place).astype(F32)
        if place >= ROWS:
            return rows_of(below_ref, place - ROWS).astype(F32)
        return innovation_of(sums_ref[place], own)

    def emit(row, value):
        value = value.astype(BF16)
        state_ref[row * C : (row + 1) * C, :] = value
        if 1 <= row < 11:
            sent_ref[(row - 1) * C : row * C, :] = value

    far_part(
        12, 2, far_ref, part_ref, own_ref, bg_ref, active_ref, forecast_ref, kernel_ref, bias_ref,
        out_weight_ref, back_ref, out_back_ref, innovation, emit, shifted, cot, target,
    )


def second_kernel(
    far_ref, part_ref, own_ref, bg_ref, active_ref, forecast_ref, kernel_ref, bias_ref,
    out_weight_ref, back_ref, out_back_ref, sums_ref, out_ref, shifted, cot, target, wide,
):
    def emit(place, value):
        wide[latitude(place), :] = value

    far_part(
        8, 0, far_ref, part_ref, own_ref, bg_ref, active_ref, forecast_ref, kernel_ref, bias_ref,
        out_weight_ref, back_ref, out_back_ref,
        lambda place, own: innovation_of(sums_ref[place], own), emit, shifted, cot, target,
    )
    out_ref[...] = wide[...].reshape(C, ROWS, LON).astype(BF16)


def exchange(value, partner):
    windows, strips = lax.axis_size("tm"), lax.axis_size("lat")
    pairs = []
    for window in range(windows):
        for strip in range(strips):
            to_window, to_strip = partner(window, strip, windows - 1, strips - 1)
            pairs.append((window * strips + strip, to_window * strips + to_strip))
    return lax.ppermute(value, ("tm", "lat"), pairs)


def near_strip(window, strip, last_window, last_strip):
    return window, strip ^ 1


def far_strip(window, strip, last_window, last_strip):
    if strip in (0, last_strip):
        return window ^ 1, strip
    return window, ((strip + 1) ^ 1) - 1


def near_window(window, strip, last_window, last_strip):
    return window ^ 1, strip


def far_window(window, strip, last_window, last_strip):
    if window in (0, last_window):
        return window, strip ^ 1
    return ((window + 1) ^ 1) - 1, strip


def shape(rows, dtype=BF16):
    return jax.ShapeDtypeStruct((rows, LON), dtype)


def shifted_scratch(count):
    return [pltpu.VMEM((3, (count + 2) * C, LON), BF16)]


def gradient_scratch(count):
    return shifted_scratch(count) + [
        pltpu.VMEM(((count + 2) * HID, LON), BF16),
        pltpu.VMEM(((count + 2) * C, LON), BF16),
    ]


def row_flops(rows):
    return rows * 2 * LON * HID * 10 * C


def on_device(
    window_snapshots, background, obs_values, obs_index, input_kernel_weight, hidden_bias_vector,
    output_pointwise_weight,
):
    own, ground, first, second = call(
        pack_kernel,
        (shape(ROWS * C), shape(ROWS * C), shape(PAYLOAD), shape(PAYLOAD)),
        [
            pltpu.VMEM((C, ROWS, LON), BF16),
            pltpu.VMEM((C, ROWS, LON), BF16),
            pltpu.VMEM((C, OBS), BF16),
            pltpu.VMEM((1, OBS), jnp.int32),
            pltpu.VMEM((C * ROWS, LON), F32),
            pltpu.VMEM((C * ROWS, LON), F32),
            pltpu.SemaphoreType.DMA((4,)),
        ],
        0, 1 << 20, pl.BlockSpec(memory_space=pltpu.HBM),
    )(
        *(
            pltpu.with_memory_space_constraint(value, pltpu.HBM)
            for value in (window_snapshots[0], background, obs_values[0], obs_index)
        )
    )
    first = exchange(first, near_strip)
    second = exchange(second, far_strip)

    out_weight = output_pointwise_weight
    taps = jnp.transpose(input_kernel_weight, (0, 1, 3, 2)).reshape(9 * C, HID)
    prepared = call(
        prepare_kernel,
        (
            jax.ShapeDtypeStruct((ROWS, 72, LON), F32),
            jax.ShapeDtypeStruct((HID, 9 * C), BF16),
            jax.ShapeDtypeStruct((3 * C, 3 * HID), BF16),
            jax.ShapeDtypeStruct((HID, LON), F32),
            jax.ShapeDtypeStruct((HID, C), BF16),
        ),
        [], ROWS * 2 * 80 * OBS * LON, 1 << 20,
    )(obs_values[0], obs_index, taps, hidden_bias_vector[None, :], out_weight)
    first, second, prepared = lax.optimization_barrier((first, second, prepared))
    sums, forward_weight, back_weight, bias, out_back = prepared

    ext, sent, above, below = call(
        extend_kernel, (shape(16 * C), shape(14 * C), shape(2 * C), shape(2 * C)), [], 0, 1 << 20
    )(own, first, second)
    weights = (forward_weight, bias, out_weight, back_weight, out_back)

    def share(sent):
        far = exchange(sent, far_window)
        near = exchange(sent, near_window)
        return far, near

    def forward(count, state):
        return call(
            functools.partial(forward_part, count),
            (shape(count * HID), shape(count * C)),
            shifted_scratch(count),
            row_flops(count), 2 << 20,
        )(state, forward_weight, bias, out_weight)

    def near_part(count, margin, near, *given):
        return call(
            functools.partial(near_kernel, count, margin),
            shape(count * C), gradient_scratch(count), row_flops(count), 2 << 20,
        )(near, *given)

    far, near = share(sent)
    given = (ext, ground, *forward(14, ext), *weights)
    part = near_part(12, 2, near, *given)
    state, sent = call(
        first_kernel, (shape(12 * C), shape(10 * C)), gradient_scratch(12), row_flops(12), 2 << 20
    )(far, part, *given, sums, above, below)
    far, near = share(sent)
    given = (state, ground, *forward(10, state), *weights)
    part = near_part(8, 0, near, *given)
    analysis = call(
        second_kernel,
        jax.ShapeDtypeStruct((C, ROWS, LON), BF16),
        gradient_scratch(8) + [pltpu.VMEM((C * ROWS, LON), F32)],
        row_flops(8), 2 << 20,
    )(far, part, *given, sums)
    return analysis[None]


def solution(mesh):
    placed = (
        P("tm", None, "lat", None),
        P(None, "lat", None),
        P("tm", None, "lat"),
        P("tm", "lat"),
        P(),
        P(),
        P(),
    )
    return jax.shard_map(
        on_device, mesh=mesh, in_specs=placed, out_specs=P("tm", None, "lat", None), check_vma=False
    )
```

```python
import functools

import jax
import jax.numpy as jnp
from jax import lax
from jax.experimental import pallas as pl
from jax.experimental.pallas import tpu as pltpu
from jax.sharding import PartitionSpec as P


C = 64
HID = 256
ROWS = 8
LON = 128
OBS = 256
STEP = 0.3

F32 = jnp.float32
BF16 = jnp.bfloat16
VMEM = pl.BlockSpec(memory_space=pltpu.VMEM)

X_PART = 4 * C
PAYLOAD = X_PART + 2 * C


def call(kernel, outs, scratch, flops, bytes_accessed, spec=VMEM, grant=48 << 20):
    def run(*args):
        return pl.pallas_call(
            kernel,
            out_shape=outs,
            in_specs=[spec] * len(args),
            out_specs=jax.tree.map(lambda _: VMEM, outs),
            scratch_shapes=scratch,
            cost_estimate=pl.CostEstimate(
                flops=flops, bytes_accessed=bytes_accessed, transcendentals=0
            ),
            compiler_params=pltpu.CompilerParams(vmem_limit_bytes=grant),
        )(*args)

    return run


def rows_of(ref, first, width=C):
    return ref[first * width : (first + 1) * width, :]


def rows_in(ref, first, count):
    return [(ref, row) for row in range(first, first + count)]


def at(rows, place, width=C):
    ref, row = rows[place]
    return rows_of(ref, row, width)


def beside(rows, a, b):
    return jnp.concatenate([at(rows, a), at(rows, b)], axis=1)


def latitude(row):
    return pl.ds(row, C, stride=ROWS)


def local_cells(index):
    local = index - lax.axis_index("lat") * (ROWS * LON)
    high = lax.shift_right_arithmetic(local, 7)
    return local - high * LON, high


def with_ones(values):
    return jnp.concatenate([values, jnp.ones((16, OBS), BF16)], axis=0)


def observation_sums(values, low, high, row):
    cell = lax.broadcasted_iota(jnp.int32, (LON, OBS), 0)
    hit = jnp.where((low == cell) & (high == row), 1.0, 0.0).astype(BF16)
    return lax.dot_general(
        values, hit, (((1,), (1,)), ((), ())), preferred_element_type=F32
    )


def innovation_of(sums, own):
    return sums[C : C + 1, :] * own - sums[:C, :]


def pack_kernel(
    x_hbm, bg_hbm, obs_hbm, index_hbm, own_ref, bg_rows_ref, first_ref, second_ref,
    x_ref, bg_ref, obs_ref, index_ref, xs, bs, sems,
):
    copies = [
        pltpu.make_async_copy(source, target, sems.at[place])
        for place, (source, target) in enumerate(
            ((x_hbm, x_ref), (obs_hbm, obs_ref), (index_hbm, index_ref), (bg_hbm, bg_ref))
        )
    ]
    for copy in copies:
        copy.start()
    copies[0].wait()
    even = lax.rem(lax.axis_index("lat"), 2) == 0

    def send(place, up, down):
        at = slice(place * C, (place + 1) * C)
        first_ref[at, :] = jnp.where(even, down, up).astype(BF16)
        second_ref[at, :] = jnp.where(even, up, down).astype(BF16)

    xs[...] = x_ref[...].astype(F32).reshape(ROWS * C, LON)
    for row in range(4):
        up, down = xs[latitude(row), :], xs[latitude(row + 4), :]
        own_ref[row * C : (row + 1) * C, :] = up.astype(BF16)
        own_ref[(row + 4) * C : (row + 5) * C, :] = down.astype(BF16)
        send(row, up, down)
    copies[1].wait()
    copies[2].wait()
    low, high = local_cells(index_ref[...])
    values = with_ones(obs_ref[...])
    copies[3].wait()
    bs[...] = bg_ref[...].astype(F32).reshape(ROWS * C, LON)
    opening = lax.axis_index("tm") == 0

    def edge(row):
        own = xs[latitude(row), :]
        ground = bs[latitude(row), :]
        value = innovation_of(observation_sums(values, low, high, row), own)
        return value + jnp.where(opening, own - ground, 0.0)

    for row in range(2):
        send(4 + row, edge(row), edge(row + 6))
    for row in range(ROWS):
        bg_rows_ref[row * C : (row + 1) * C, :] = bs[latitude(row), :].astype(BF16)


def extend_kernel(
    own_ref, first_ref, second_ref, ext_ref, near_ref, far_ref, above_edge_ref, below_edge_ref
):
    strip = lax.axis_index("lat")
    even = lax.rem(strip, 2) == 0
    zero = jnp.zeros((X_PART, LON), BF16)
    above = jnp.where(even, second_ref[...], first_ref[...])
    below = jnp.where(even, first_ref[...], second_ref[...])
    above_edge_ref[...] = above[X_PART:, :]
    below_edge_ref[...] = below[X_PART:, :]
    above = jnp.where(strip > 0, above[:X_PART, :], zero)
    below = jnp.where(strip < lax.axis_size("lat") - 1, below[:X_PART, :], zero)
    far_ref[: 3 * C, :] = above[C:, :]
    far_ref[3 * C :, :] = below[: 3 * C, :]
    near_ref[: 3 * C, :] = above[C:, :]
    near_ref[3 * C : 11 * C, :] = own_ref[...]
    near_ref[11 * C :, :] = below[: 3 * C, :]
    ext_ref[:X_PART, :] = above
    ext_ref[X_PART : X_PART + ROWS * C, :] = own_ref[...]
    ext_ref[X_PART + ROWS * C :, :] = below


def roll_rows(rows, shifted, pairs):
    for place in sorted({first + a for pair in pairs for first in pair for a in range(3)}):
        into = slice(place * C, (place + 1) * C)
        value = at(rows, place)
        wide = value.astype(F32)
        shifted[0, into, :] = pltpu.roll(wide, 1, 1).astype(BF16)
        shifted[1, into, :] = value
        shifted[2, into, :] = pltpu.roll(wide, LON - 1, 1).astype(BF16)


def hidden(shifted, kernel_ref, bias, pair):
    def stack(first):
        return jnp.concatenate(
            [
                shifted[b, (first + a) * C : (first + a + 1) * C, :]
                for a in range(3)
                for b in range(3)
            ],
            axis=0,
        )

    cells = jnp.concatenate([stack(row) for row in pair], axis=1)
    before = jnp.dot(kernel_ref[...], cells, preferred_element_type=F32) + bias
    return jnp.tanh(before).astype(BF16)


def store_pair(ref, first, value, width=C):
    ref[first * width : (first + 1) * width, :] = value[:, :LON]
    ref[(first + 1) * width : (first + 2) * width, :] = value[:, LON:]


def wide_bias(bias_ref):
    return jnp.concatenate([bias_ref[...], bias_ref[...]], axis=1)


def forward_kernel(
    pairs, state_ref, kernel_ref, bias_ref, out_weight_ref, active_ref, forecast_ref, shifted
):
    rows = rows_in(state_ref, 0, state_ref.shape[0] // C)
    roll_rows(rows, shifted, pairs)
    bias = wide_bias(bias_ref)
    for place, (a, b) in enumerate(pairs):
        active = hidden(shifted, kernel_ref, bias, (a, b))
        store_pair(active_ref, 2 * place, active, HID)
        step = jnp.dot(out_weight_ref[...], active, preferred_element_type=F32)
        centre = beside(rows, a + 1, b + 1).astype(F32)
        store_pair(forecast_ref, 2 * place, (centre + step).astype(BF16))


def prepare_kernel(
    obs_ref, index_ref, kernel_ref, bias_ref, out_weight_ref, sums_ref, forward_ref, back_ref,
    wide_bias_ref, out_back_ref,
):
    low, high = local_cells(index_ref[...])
    values = with_ones(obs_ref[...])
    for row in range(ROWS):
        sums_ref[row] = observation_sums(values, low, high, row)[:72, :]
    forward_ref[...] = kernel_ref[...].T
    out_back_ref[...] = out_weight_ref[...].T
    wide_bias_ref[...] = jnp.broadcast_to(bias_ref[...], (LON, HID)).T
    for a in range(3):
        back_ref[:, a * HID : (a + 1) * HID] = kernel_ref[(2 - a) * 3 * C : (3 - a) * 3 * C, :]


def residual_part(
    pairs, prev, own_ref, kernel_ref, bias_ref, out_weight_ref, shifted, take
):
    roll_rows(prev, shifted, pairs)
    bias = wide_bias(bias_ref)
    own_rows = rows_in(own_ref, 2, max(b for _, b in pairs) + 1)
    for a, b in pairs:
        active = hidden(shifted, kernel_ref, bias, (a, b))
        step = jnp.dot(out_weight_ref[...], active, preferred_element_type=F32)
        centre = beside(prev, a + 1, b + 1).astype(F32)
        guess = (centre + step).astype(BF16).astype(F32)
        resid = (beside(own_rows, a, b).astype(F32) - guess).astype(BF16)
        take(a, resid[:, :LON])
        take(b, resid[:, LON:])


def strip_ends():
    strip = lax.axis_index("lat")
    return -strip * ROWS, (lax.axis_size("lat") - strip) * ROWS


def adjoint_part(
    count, margin, later, active, forecast, back_ref, out_back_ref, cot, target, take
):
    top, bottom = strip_ends()
    for row in range(0, count + 2, 2):
        resid = beside(later, row, row + 1).astype(F32) - beside(forecast, row, row + 1).astype(F32)
        resid = resid.astype(BF16)
        store_pair(target, row, resid)
        projected = jnp.dot(out_back_ref[...], resid, preferred_element_type=F32)
        for half in range(2):
            place = row + half - margin - 1
            value = at(active, row + half, HID).astype(F32)
            value = (1.0 - value * value) * projected[:, half * LON : (half + 1) * LON]
            if not 0 <= place < ROWS:
                value = jnp.where((place >= top) & (place < bottom), value, 0.0)
            cot[(row + half) * HID : (row + half + 1) * HID, :] = value.astype(BF16)
    closing = lax.axis_index("tm") == lax.axis_size("tm") - 1
    for row in range(0, count, 2):
        cells = jnp.concatenate(
            [cot[row * HID : (row + 3) * HID, :], cot[(row + 1) * HID : (row + 4) * HID, :]], axis=1
        )
        spread = jnp.dot(back_ref[...], cells, preferred_element_type=F32)
        for half in range(2):
            lanes = slice(half * LON, (half + 1) * LON)
            pulled = (
                pltpu.roll(spread[:C, lanes], LON - 1, 1)
                + spread[C : 2 * C, lanes]
                + pltpu.roll(spread[2 * C :, lanes], 1, 1)
            )
            resid = rows_of(target, row + half + 1).astype(F32)
            take(row + half, jnp.where(closing, 0.0, resid + pulled).astype(BF16))


def branches():
    window = lax.axis_index("tm")
    even = lax.rem(window, 2) == 0
    opening = window == 0
    return even & jnp.logical_not(opening), opening, jnp.logical_not(even)


def in_order(count):
    return tuple((row, row + 1) for row in range(0, count, 2))


INNER = ((3, 4), (5, 6), (7, 8))
OUTER = ((0, 1), (2, 9), (10, 11))


def first_near_kernel(
    near_ref, far_own_ref, own_ref, active_in_ref, forecast_in_ref, active_out_ref, forecast_out_ref,
    kernel_ref, bias_ref, out_weight_ref, back_ref, out_back_ref, part_ref, inner_ref, shifted, cot,
    target,
):
    def put(ref):
        def take(row, value):
            ref[row * C : (row + 1) * C, :] = value

        return take

    even, _, odd = branches()

    @pl.when(jnp.logical_not(odd))
    def _():
        adjoint_part(
            12, 2, rows_in(near_ref, 0, 14), split_rows(active_out_ref, active_in_ref),
            split_rows(forecast_out_ref, forecast_in_ref), back_ref, out_back_ref, cot, target,
            put(part_ref),
        )

    @pl.when(even)
    def _():
        prev = [None] * 3 + rows_in(far_own_ref, 0, ROWS)
        residual_part(
            INNER, prev, own_ref, kernel_ref, bias_ref, out_weight_ref, shifted, put(inner_ref)
        )

    @pl.when(odd)
    def _():
        residual_part(
            in_order(12), rows_in(near_ref, 0, 14), own_ref, kernel_ref, bias_ref, out_weight_ref,
            shifted, put(part_ref),
        )


def split_rows(outside_ref, inside_ref):
    return rows_in(outside_ref, 0, 4) + rows_in(inside_ref, 0, 6) + rows_in(outside_ref, 4, 4)


def first_kernel(
    far_ref, far_own_ref, part_ref, inner_ref, own_ref, bg_ref, active_in_ref, forecast_in_ref,
    active_out_ref, forecast_out_ref, kernel_ref, bias_ref, out_weight_ref, back_ref, out_back_ref,
    sums_ref, above_ref, below_ref, state_ref, sent_ref, shifted, cot, target,
):
    top, bottom = strip_ends()

    def step(row, resid, adjoint):
        own = rows_of(own_ref, row + 2).astype(F32)
        place = row - 2
        if place < 0:
            innovation = rows_of(above_ref, row).astype(F32)
        elif place >= ROWS:
            innovation = rows_of(below_ref, place - ROWS).astype(F32)
        else:
            innovation = innovation_of(sums_ref[place], own)
        value = own - STEP * (resid.astype(F32) - adjoint.astype(F32) + innovation)
        if not 0 <= place < ROWS:
            value = jnp.where((place >= top) & (place < bottom), value, 0.0)
        value = value.astype(BF16)
        state_ref[row * C : (row + 1) * C, :] = value
        if 1 <= row < 11:
            sent_ref[(row - 1) * C : row * C, :] = value

    even, opening, odd = branches()
    far = rows_in(far_ref, 0, 3) + rows_in(far_own_ref, 0, ROWS) + rows_in(far_ref, 3, 3)

    @pl.when(even)
    def _():
        residual_part(
            OUTER, far, own_ref, kernel_ref, bias_ref, out_weight_ref, shifted,
            lambda row, resid: step(row, resid, rows_of(part_ref, row)),
        )
        for row in range(3, 9):
            step(row, rows_of(inner_ref, row), rows_of(part_ref, row))

    @pl.when(opening)
    def _():
        for row in range(12):
            place = row - 2
            resid = jnp.zeros((C, LON), BF16)
            if 0 <= place < ROWS:
                own = rows_of(own_ref, row + 2).astype(F32)
                resid = (own - rows_of(bg_ref, place).astype(F32)).astype(BF16)
            step(row, resid, rows_of(part_ref, row))

    @pl.when(odd)
    def _():
        adjoint_part(
            12, 2, far, split_rows(active_out_ref, active_in_ref),
            split_rows(forecast_out_ref, forecast_in_ref), back_ref, out_back_ref, cot, target,
            lambda row, adjoint: step(row, rows_of(part_ref, row), adjoint),
        )


def second_near_kernel(
    near_ref, own_ref, active_ref, forecast_ref, kernel_ref, bias_ref, out_weight_ref, back_ref,
    out_back_ref, part_ref, shifted, cot, target,
):
    def take(row, value):
        part_ref[row * C : (row + 1) * C, :] = value

    _, _, odd = branches()
    near = rows_in(near_ref, 0, 10)

    @pl.when(jnp.logical_not(odd))
    def _():
        adjoint_part(
            8, 0, near, rows_in(active_ref, 0, 10), rows_in(forecast_ref, 0, 10), back_ref,
            out_back_ref, cot, target, take,
        )

    @pl.when(odd)
    def _():
        residual_part(
            in_order(8), near, own_ref, kernel_ref, bias_ref, out_weight_ref, shifted, take
        )


def second_kernel(
    far_ref, part_ref, own_ref, bg_ref, active_ref, forecast_ref, kernel_ref, bias_ref,
    out_weight_ref, back_ref, out_back_ref, sums_ref, out_ref, shifted, cot, target, wide,
):
    def step(row, resid, adjoint):
        own = rows_of(own_ref, row + 2).astype(F32)
        innovation = innovation_of(sums_ref[row], own)
        value = own - STEP * (resid.astype(F32) - adjoint.astype(F32) + innovation)
        wide[latitude(row), :] = value

    even, opening, odd = branches()
    far = rows_in(far_ref, 0, 10)

    @pl.when(even)
    def _():
        residual_part(
            in_order(8), far, own_ref, kernel_ref, bias_ref, out_weight_ref, shifted,
            lambda row, resid: step(row, resid, rows_of(part_ref, row)),
        )

    @pl.when(opening)
    def _():
        for row in range(ROWS):
            own = rows_of(own_ref, row + 2).astype(F32)
            resid = (own - rows_of(bg_ref, row).astype(F32)).astype(BF16)
            step(row, resid, rows_of(part_ref, row))

    @pl.when(odd)
    def _():
        adjoint_part(
            8, 0, far, rows_in(active_ref, 0, 10), rows_in(forecast_ref, 0, 10), back_ref,
            out_back_ref, cot, target, lambda row, adjoint: step(row, rows_of(part_ref, row), adjoint),
        )

    out_ref[...] = wide[...].reshape(C, ROWS, LON).astype(BF16)


def exchange(value, partner):
    windows, strips = lax.axis_size("tm"), lax.axis_size("lat")
    pairs = []
    for window in range(windows):
        for strip in range(strips):
            to_window, to_strip = partner(window, strip, windows - 1, strips - 1)
            pairs.append((window * strips + strip, to_window * strips + to_strip))
    return lax.ppermute(value, ("tm", "lat"), pairs)


def near_strip(window, strip, last_window, last_strip):
    return window, strip ^ 1


def far_strip(window, strip, last_window, last_strip):
    if strip in (0, last_strip):
        return window ^ 1, strip
    return window, ((strip + 1) ^ 1) - 1


def near_window(window, strip, last_window, last_strip):
    return window ^ 1, strip


def far_window(window, strip, last_window, last_strip):
    if window in (0, last_window):
        return window, strip ^ 2
    return ((window + 1) ^ 1) - 1, strip


def shape(rows, dtype=BF16):
    return jax.ShapeDtypeStruct((rows, LON), dtype)


def shifted_scratch(count):
    return [pltpu.VMEM((3, (count + 2) * C, LON), BF16)]


def gradient_scratch(count):
    return shifted_scratch(count) + [
        pltpu.VMEM(((count + 2) * HID, LON), BF16),
        pltpu.VMEM(((count + 2) * C, LON), BF16),
    ]


def row_flops(rows):
    return rows * 2 * LON * HID * 10 * C


def on_device(
    window_snapshots, background, obs_values, obs_index, input_kernel_weight, hidden_bias_vector,
    output_pointwise_weight,
):
    out_weight = output_pointwise_weight

    def forward(pairs, state):
        count = state.shape[0] // C - 2
        return call(
            functools.partial(forward_kernel, pairs),
            (shape(2 * len(pairs) * HID), shape(2 * len(pairs) * C)),
            shifted_scratch(count),
            row_flops(2 * len(pairs)), 2 << 20,
        )(state, forward_weight, bias, out_weight)

    own, ground, first, second = call(
        pack_kernel,
        (shape(ROWS * C), shape(ROWS * C), shape(PAYLOAD), shape(PAYLOAD)),
        [
            pltpu.VMEM((C, ROWS, LON), BF16),
            pltpu.VMEM((C, ROWS, LON), BF16),
            pltpu.VMEM((C, OBS), BF16),
            pltpu.VMEM((1, OBS), jnp.int32),
            pltpu.VMEM((C * ROWS, LON), F32),
            pltpu.VMEM((C * ROWS, LON), F32),
            pltpu.SemaphoreType.DMA((4,)),
        ],
        0, 1 << 20, pl.BlockSpec(memory_space=pltpu.HBM),
    )(
        *(
            pltpu.with_memory_space_constraint(value, pltpu.HBM)
            for value in (window_snapshots[0], background, obs_values[0], obs_index)
        )
    )
    first = exchange(first, near_strip)
    second = exchange(second, far_strip)
    far_own = exchange(own, far_window)

    taps = jnp.transpose(input_kernel_weight, (0, 1, 3, 2)).reshape(9 * C, HID)
    sums, forward_weight, back_weight, bias, out_back = call(
        prepare_kernel,
        (
            jax.ShapeDtypeStruct((ROWS, 72, LON), F32),
            jax.ShapeDtypeStruct((HID, 9 * C), BF16),
            jax.ShapeDtypeStruct((3 * C, 3 * HID), BF16),
            jax.ShapeDtypeStruct((HID, LON), F32),
            jax.ShapeDtypeStruct((HID, C), BF16),
        ),
        [], ROWS * 2 * 80 * OBS * LON, 1 << 20,
    )(obs_values[0], obs_index, taps, hidden_bias_vector[None, :], out_weight)
    weights = (forward_weight, bias, out_weight, back_weight, out_back)
    inside = forward(in_order(6), own)
    first, second, inside, sums = lax.optimization_barrier((first, second, inside, sums))

    ext, sent, halo, above, below = call(
        extend_kernel,
        (shape(16 * C), shape(14 * C), shape(6 * C), shape(2 * C), shape(2 * C)),
        [], 0, 1 << 20,
    )(own, first, second)
    far = exchange(halo, far_window)
    near = exchange(sent, near_window)
    outside = forward(((0, 1), (2, 3), (10, 11), (12, 13)), ext)
    part, inner = call(
        first_near_kernel, (shape(12 * C), shape(12 * C)), gradient_scratch(12),
        row_flops(12), 2 << 20,
    )(near, far_own, ext, *inside, *outside, *weights)
    state, sent = call(
        first_kernel, (shape(12 * C), shape(10 * C)), gradient_scratch(12), row_flops(12),
        2 << 20,
    )(
        far, far_own, part, inner, ext, ground, *inside, *outside, *weights, sums, above, below
    )
    far = exchange(sent, far_window)
    near = exchange(sent, near_window)
    given = (state, ground, *forward(in_order(10), state), *weights)
    part = call(
        second_near_kernel, shape(8 * C), gradient_scratch(8), row_flops(8), 2 << 20
    )(near, state, *given[2:])
    analysis = call(
        second_kernel,
        jax.ShapeDtypeStruct((C, ROWS, LON), BF16),
        gradient_scratch(8) + [pltpu.VMEM((C * ROWS, LON), F32)],
        row_flops(8), 2 << 20,
    )(far, part, *given, sums)
    return analysis[None]


def solution(mesh):
    placed = (
        P("tm", None, "lat", None),
        P(None, "lat", None),
        P("tm", None, "lat"),
        P("tm", "lat"),
        P(),
        P(),
        P(),
    )
    return jax.shard_map(
        on_device, mesh=mesh, in_specs=placed, out_specs=P("tm", None, "lat", None), check_vma=False
    )
```

```python
import functools

import jax
import jax.numpy as jnp
from jax import lax
from jax.experimental import pallas as pl
from jax.experimental.pallas import tpu as pltpu
from jax.sharding import PartitionSpec as P


C = 64
HID = 256
ROWS = 8
LON = 128
OBS = 256
STEP = 0.3

F32 = jnp.float32
BF16 = jnp.bfloat16
VMEM = pl.BlockSpec(memory_space=pltpu.VMEM)

X_PART = 4 * C
PAYLOAD = X_PART + 2 * C


def call(kernel, outs, scratch, flops, bytes_accessed, spec=VMEM, grant=48 << 20):
    def run(*args):
        return pl.pallas_call(
            kernel,
            out_shape=outs,
            in_specs=[spec] * len(args),
            out_specs=jax.tree.map(lambda _: VMEM, outs),
            scratch_shapes=scratch,
            cost_estimate=pl.CostEstimate(
                flops=flops, bytes_accessed=bytes_accessed, transcendentals=0
            ),
            compiler_params=pltpu.CompilerParams(vmem_limit_bytes=grant),
        )(*args)

    return run


def rows_of(ref, first, width=C):
    return ref[first * width : (first + 1) * width, :]


def rows_in(ref, first, count):
    return [(ref, row) for row in range(first, first + count)]


def at(rows, place, width=C):
    ref, row = rows[place]
    return rows_of(ref, row, width)


def beside(rows, a, b):
    return jnp.concatenate([at(rows, a), at(rows, b)], axis=1)


def latitude(row):
    return pl.ds(row, C, stride=ROWS)


def local_cells(index):
    local = index - lax.axis_index("lat") * (ROWS * LON)
    high = lax.shift_right_arithmetic(local, 7)
    return local - high * LON, high


def with_ones(values):
    return jnp.concatenate([values, jnp.ones((16, OBS), BF16)], axis=0)


def observation_sums(values, low, high, row):
    cell = lax.broadcasted_iota(jnp.int32, (LON, OBS), 0)
    hit = jnp.where((low == cell) & (high == row), 1.0, 0.0).astype(BF16)
    return lax.dot_general(
        values, hit, (((1,), (1,)), ((), ())), preferred_element_type=F32
    )


def innovation_of(sums, own):
    return sums[C : C + 1, :] * own - sums[:C, :]


def pack_kernel(
    x_hbm, obs_hbm, index_hbm, bg_hbm, taps_hbm, out_weight_hbm, bias_hbm, own_ref, bg_rows_ref,
    first_ref, second_ref, obs_ref, index_ref, taps_ref, out_weight_ref, bias_ref, x_ref, bg_ref,
    xs, bs, sems,
):
    copies = [
        pltpu.make_async_copy(source, target, sems.at[place])
        for place, (source, target) in enumerate(
            (
                (x_hbm, x_ref), (obs_hbm, obs_ref), (index_hbm, index_ref), (bg_hbm, bg_ref),
                (taps_hbm, taps_ref), (out_weight_hbm, out_weight_ref), (bias_hbm, bias_ref),
            )
        )
    ]
    for copy in copies:
        copy.start()
    copies[0].wait()
    even = lax.rem(lax.axis_index("lat"), 2) == 0

    def send(place, up, down):
        at = slice(place * C, (place + 1) * C)
        first_ref[at, :] = jnp.where(even, down, up).astype(BF16)
        second_ref[at, :] = jnp.where(even, up, down).astype(BF16)

    xs[...] = x_ref[...].astype(F32).reshape(ROWS * C, LON)
    for row in range(4):
        up, down = xs[latitude(row), :], xs[latitude(row + 4), :]
        own_ref[row * C : (row + 1) * C, :] = up.astype(BF16)
        own_ref[(row + 4) * C : (row + 5) * C, :] = down.astype(BF16)
        send(row, up, down)
    copies[1].wait()
    copies[2].wait()
    low, high = local_cells(index_ref[...])
    values = with_ones(obs_ref[...])
    copies[3].wait()
    bs[...] = bg_ref[...].astype(F32).reshape(ROWS * C, LON)
    opening = lax.axis_index("tm") == 0

    def edge(row):
        own = xs[latitude(row), :]
        ground = bs[latitude(row), :]
        value = innovation_of(observation_sums(values, low, high, row), own)
        return value + jnp.where(opening, own - ground, 0.0)

    for row in range(2):
        send(4 + row, edge(row), edge(row + 6))
    for row in range(ROWS):
        bg_rows_ref[row * C : (row + 1) * C, :] = bs[latitude(row), :].astype(BF16)
    for copy in copies[4:]:
        copy.wait()


def extend_kernel(
    own_ref, first_ref, second_ref, ext_ref, near_ref, far_ref, above_edge_ref, below_edge_ref
):
    strip = lax.axis_index("lat")
    even = lax.rem(strip, 2) == 0
    zero = jnp.zeros((X_PART, LON), BF16)
    above = jnp.where(even, second_ref[...], first_ref[...])
    below = jnp.where(even, first_ref[...], second_ref[...])
    above_edge_ref[...] = above[X_PART:, :]
    below_edge_ref[...] = below[X_PART:, :]
    above = jnp.where(strip > 0, above[:X_PART, :], zero)
    below = jnp.where(strip < lax.axis_size("lat") - 1, below[:X_PART, :], zero)
    far_ref[: 3 * C, :] = above[C:, :]
    far_ref[3 * C :, :] = below[: 3 * C, :]
    near_ref[: 3 * C, :] = above[C:, :]
    near_ref[3 * C : 11 * C, :] = own_ref[...]
    near_ref[11 * C :, :] = below[: 3 * C, :]
    ext_ref[:X_PART, :] = above
    ext_ref[X_PART : X_PART + ROWS * C, :] = own_ref[...]
    ext_ref[X_PART + ROWS * C :, :] = below


def roll_rows(rows, shifted, pairs):
    for place in sorted({first + a for pair in pairs for first in pair for a in range(3)}):
        into = slice(place * C, (place + 1) * C)
        value = at(rows, place)
        wide = value.astype(F32)
        shifted[0, into, :] = pltpu.roll(wide, 1, 1).astype(BF16)
        shifted[1, into, :] = value
        shifted[2, into, :] = pltpu.roll(wide, LON - 1, 1).astype(BF16)


def hidden(shifted, kernel_ref, bias, pair):
    def stack(first):
        return jnp.concatenate(
            [
                shifted[b, (first + a) * C : (first + a + 1) * C, :]
                for a in range(3)
                for b in range(3)
            ],
            axis=0,
        )

    cells = jnp.concatenate([stack(row) for row in pair], axis=1)
    before = jnp.dot(kernel_ref[...], cells, preferred_element_type=F32) + bias
    return jnp.tanh(before).astype(BF16)


def store_pair(ref, first, value, width=C):
    ref[first * width : (first + 1) * width, :] = value[:, :LON]
    ref[(first + 1) * width : (first + 2) * width, :] = value[:, LON:]


def wide_bias(bias_ref):
    return jnp.concatenate([bias_ref[...], bias_ref[...]], axis=1)


def forward_kernel(
    pairs, state_ref, kernel_ref, bias_ref, out_weight_ref, active_ref, forecast_ref, shifted
):
    rows = rows_in(state_ref, 0, state_ref.shape[0] // C)
    roll_rows(rows, shifted, pairs)
    bias = wide_bias(bias_ref)
    for place, (a, b) in enumerate(pairs):
        active = hidden(shifted, kernel_ref, bias, (a, b))
        store_pair(active_ref, 2 * place, active, HID)
        step = jnp.dot(out_weight_ref[...], active, preferred_element_type=F32)
        centre = beside(rows, a + 1, b + 1).astype(F32)
        store_pair(forecast_ref, 2 * place, (centre + step).astype(BF16))


def prepare_kernel(
    obs_ref, index_ref, kernel_ref, bias_ref, out_weight_ref, sums_ref, forward_ref, back_ref,
    wide_bias_ref, out_back_ref,
):
    low, high = local_cells(index_ref[...])
    values = with_ones(obs_ref[...])
    for row in range(ROWS):
        sums_ref[row] = observation_sums(values, low, high, row)[:72, :]
    forward_ref[...] = kernel_ref[...].T
    out_back_ref[...] = out_weight_ref[...].T
    wide_bias_ref[...] = jnp.broadcast_to(bias_ref[...], (LON, HID)).T
    for a in range(3):
        back_ref[:, a * HID : (a + 1) * HID] = kernel_ref[(2 - a) * 3 * C : (3 - a) * 3 * C, :]


def residual_part(
    pairs, prev, own_ref, kernel_ref, bias_ref, out_weight_ref, shifted, take
):
    roll_rows(prev, shifted, pairs)
    bias = wide_bias(bias_ref)
    own_rows = rows_in(own_ref, 2, max(b for _, b in pairs) + 1)
    for a, b in pairs:
        active = hidden(shifted, kernel_ref, bias, (a, b))
        step = jnp.dot(out_weight_ref[...], active, preferred_element_type=F32)
        centre = beside(prev, a + 1, b + 1).astype(F32)
        guess = (centre + step).astype(BF16).astype(F32)
        resid = (beside(own_rows, a, b).astype(F32) - guess).astype(BF16)
        take(a, resid[:, :LON])
        take(b, resid[:, LON:])


def strip_ends():
    strip = lax.axis_index("lat")
    return -strip * ROWS, (lax.axis_size("lat") - strip) * ROWS


def adjoint_part(
    count, margin, later, active, forecast, back_ref, out_back_ref, cot, target, take
):
    top, bottom = strip_ends()
    for row in range(0, count + 2, 2):
        resid = beside(later, row, row + 1).astype(F32) - beside(forecast, row, row + 1).astype(F32)
        resid = resid.astype(BF16)
        store_pair(target, row, resid)
        projected = jnp.dot(out_back_ref[...], resid, preferred_element_type=F32)
        for half in range(2):
            place = row + half - margin - 1
            value = at(active, row + half, HID).astype(F32)
            value = (1.0 - value * value) * projected[:, half * LON : (half + 1) * LON]
            if not 0 <= place < ROWS:
                value = jnp.where((place >= top) & (place < bottom), value, 0.0)
            cot[(row + half) * HID : (row + half + 1) * HID, :] = value.astype(BF16)
    closing = lax.axis_index("tm") == lax.axis_size("tm") - 1
    for row in range(0, count, 2):
        cells = jnp.concatenate(
            [cot[row * HID : (row + 3) * HID, :], cot[(row + 1) * HID : (row + 4) * HID, :]], axis=1
        )
        spread = jnp.dot(back_ref[...], cells, preferred_element_type=F32)
        for half in range(2):
            lanes = slice(half * LON, (half + 1) * LON)
            pulled = (
                pltpu.roll(spread[:C, lanes], LON - 1, 1)
                + spread[C : 2 * C, lanes]
                + pltpu.roll(spread[2 * C :, lanes], 1, 1)
            )
            resid = rows_of(target, row + half + 1).astype(F32)
            take(row + half, jnp.where(closing, 0.0, resid + pulled).astype(BF16))


def branches():
    window = lax.axis_index("tm")
    even = lax.rem(window, 2) == 0
    opening = window == 0
    return even & jnp.logical_not(opening), opening, jnp.logical_not(even)


def in_order(count):
    return tuple((row, row + 1) for row in range(0, count, 2))


INNER = ((3, 4), (5, 6), (7, 8))
OUTER = ((0, 1), (2, 9), (10, 11))


def first_near_kernel(
    near_ref, far_own_ref, own_ref, active_in_ref, forecast_in_ref, active_out_ref, forecast_out_ref,
    kernel_ref, bias_ref, out_weight_ref, back_ref, out_back_ref, part_ref, inner_ref, shifted, cot,
    target,
):
    def put(ref):
        def take(row, value):
            ref[row * C : (row + 1) * C, :] = value

        return take

    even, _, odd = branches()

    @pl.when(jnp.logical_not(odd))
    def _():
        adjoint_part(
            12, 2, rows_in(near_ref, 0, 14), split_rows(active_out_ref, active_in_ref),
            split_rows(forecast_out_ref, forecast_in_ref), back_ref, out_back_ref, cot, target,
            put(part_ref),
        )

    @pl.when(even)
    def _():
        prev = [None] * 3 + rows_in(far_own_ref, 0, ROWS)
        residual_part(
            INNER, prev, own_ref, kernel_ref, bias_ref, out_weight_ref, shifted, put(inner_ref)
        )

    @pl.when(odd)
    def _():
        residual_part(
            in_order(12), rows_in(near_ref, 0, 14), own_ref, kernel_ref, bias_ref, out_weight_ref,
            shifted, put(part_ref),
        )


def split_rows(outside_ref, inside_ref):
    return rows_in(outside_ref, 0, 4) + rows_in(inside_ref, 0, 6) + rows_in(outside_ref, 4, 4)


def first_kernel(
    far_ref, far_own_ref, part_ref, inner_ref, own_ref, bg_ref, active_in_ref, forecast_in_ref,
    active_out_ref, forecast_out_ref, kernel_ref, bias_ref, out_weight_ref, back_ref, out_back_ref,
    sums_ref, above_ref, below_ref, state_ref, sent_ref, shifted, cot, target,
):
    top, bottom = strip_ends()

    def step(row, resid, adjoint):
        own = rows_of(own_ref, row + 2).astype(F32)
        place = row - 2
        if place < 0:
            innovation = rows_of(above_ref, row).astype(F32)
        elif place >= ROWS:
            innovation = rows_of(below_ref, place - ROWS).astype(F32)
        else:
            innovation = innovation_of(sums_ref[place], own)
        value = own - STEP * (resid.astype(F32) - adjoint.astype(F32) + innovation)
        if not 0 <= place < ROWS:
            value = jnp.where((place >= top) & (place < bottom), value, 0.0)
        value = value.astype(BF16)
        state_ref[row * C : (row + 1) * C, :] = value
        if 1 <= row < 11:
            sent_ref[(row - 1) * C : row * C, :] = value

    even, opening, odd = branches()
    far = rows_in(far_ref, 0, 3) + rows_in(far_own_ref, 0, ROWS) + rows_in(far_ref, 3, 3)

    @pl.when(even)
    def _():
        residual_part(
            OUTER, far, own_ref, kernel_ref, bias_ref, out_weight_ref, shifted,
            lambda row, resid: step(row, resid, rows_of(part_ref, row)),
        )
        for row in range(3, 9):
            step(row, rows_of(inner_ref, row), rows_of(part_ref, row))

    @pl.when(opening)
    def _():
        for row in range(12):
            place = row - 2
            resid = jnp.zeros((C, LON), BF16)
            if 0 <= place < ROWS:
                own = rows_of(own_ref, row + 2).astype(F32)
                resid = (own - rows_of(bg_ref, place).astype(F32)).astype(BF16)
            step(row, resid, rows_of(part_ref, row))

    @pl.when(odd)
    def _():
        adjoint_part(
            12, 2, far, split_rows(active_out_ref, active_in_ref),
            split_rows(forecast_out_ref, forecast_in_ref), back_ref, out_back_ref, cot, target,
            lambda row, adjoint: step(row, rows_of(part_ref, row), adjoint),
        )


def second_near_kernel(
    near_ref, own_ref, active_ref, forecast_ref, kernel_ref, bias_ref, out_weight_ref, back_ref,
    out_back_ref, part_ref, shifted, cot, target,
):
    def take(row, value):
        part_ref[row * C : (row + 1) * C, :] = value

    _, _, odd = branches()
    near = rows_in(near_ref, 0, 10)

    @pl.when(jnp.logical_not(odd))
    def _():
        adjoint_part(
            8, 0, near, rows_in(active_ref, 0, 10), rows_in(forecast_ref, 0, 10), back_ref,
            out_back_ref, cot, target, take,
        )

    @pl.when(odd)
    def _():
        residual_part(
            in_order(8), near, own_ref, kernel_ref, bias_ref, out_weight_ref, shifted, take
        )


def second_kernel(
    far_ref, part_ref, own_ref, bg_ref, active_ref, forecast_ref, kernel_ref, bias_ref,
    out_weight_ref, back_ref, out_back_ref, sums_ref, out_ref, shifted, cot, target, wide,
):
    def step(row, resid, adjoint):
        own = rows_of(own_ref, row + 2).astype(F32)
        innovation = innovation_of(sums_ref[row], own)
        value = own - STEP * (resid.astype(F32) - adjoint.astype(F32) + innovation)
        wide[latitude(row), :] = value

    even, opening, odd = branches()
    far = rows_in(far_ref, 0, 10)

    @pl.when(even)
    def _():
        residual_part(
            in_order(8), far, own_ref, kernel_ref, bias_ref, out_weight_ref, shifted,
            lambda row, resid: step(row, resid, rows_of(part_ref, row)),
        )

    @pl.when(opening)
    def _():
        for row in range(ROWS):
            own = rows_of(own_ref, row + 2).astype(F32)
            resid = (own - rows_of(bg_ref, row).astype(F32)).astype(BF16)
            step(row, resid, rows_of(part_ref, row))

    @pl.when(odd)
    def _():
        adjoint_part(
            8, 0, far, rows_in(active_ref, 0, 10), rows_in(forecast_ref, 0, 10), back_ref,
            out_back_ref, cot, target, lambda row, adjoint: step(row, rows_of(part_ref, row), adjoint),
        )

    out_ref[...] = wide[...].reshape(C, ROWS, LON).astype(BF16)


def exchange(value, partner):
    windows, strips = lax.axis_size("tm"), lax.axis_size("lat")
    pairs = []
    for window in range(windows):
        for strip in range(strips):
            to_window, to_strip = partner(window, strip, windows - 1, strips - 1)
            pairs.append((window * strips + strip, to_window * strips + to_strip))
    return lax.ppermute(value, ("tm", "lat"), pairs)


def near_strip(window, strip, last_window, last_strip):
    return window, strip ^ 1


def far_strip(window, strip, last_window, last_strip):
    if strip in (0, last_strip):
        return window ^ 1, strip
    return window, ((strip + 1) ^ 1) - 1


def near_window(window, strip, last_window, last_strip):
    return window ^ 1, strip


def far_window(window, strip, last_window, last_strip):
    if window in (0, last_window):
        return window, strip ^ 2
    return ((window + 1) ^ 1) - 1, strip


def shape(rows, dtype=BF16):
    return jax.ShapeDtypeStruct((rows, LON), dtype)


def shifted_scratch(count):
    return [pltpu.VMEM((3, (count + 2) * C, LON), BF16)]


def gradient_scratch(count):
    return shifted_scratch(count) + [
        pltpu.VMEM(((count + 2) * HID, LON), BF16),
        pltpu.VMEM(((count + 2) * C, LON), BF16),
    ]


def row_flops(rows):
    return rows * 2 * LON * HID * 10 * C


def on_device(
    window_snapshots, background, obs_values, obs_index, input_kernel_weight, hidden_bias_vector,
    output_pointwise_weight,
):
    def forward(pairs, state):
        count = state.shape[0] // C - 2
        return call(
            functools.partial(forward_kernel, pairs),
            (shape(2 * len(pairs) * HID), shape(2 * len(pairs) * C)),
            shifted_scratch(count),
            row_flops(2 * len(pairs)), 2 << 20,
        )(state, forward_weight, bias, out_weight)

    taps = jnp.transpose(input_kernel_weight, (0, 1, 3, 2)).reshape(9 * C, HID)
    own, ground, first, second, observed, index, taps, out_weight, bias = call(
        pack_kernel,
        (
            shape(ROWS * C), shape(ROWS * C), shape(PAYLOAD), shape(PAYLOAD),
            jax.ShapeDtypeStruct((C, OBS), BF16),
            jax.ShapeDtypeStruct((1, OBS), jnp.int32),
            jax.ShapeDtypeStruct((9 * C, HID), BF16),
            jax.ShapeDtypeStruct((C, HID), BF16),
            jax.ShapeDtypeStruct((1, HID), F32),
        ),
        [
            pltpu.VMEM((C, ROWS, LON), BF16),
            pltpu.VMEM((C, ROWS, LON), BF16),
            pltpu.VMEM((C * ROWS, LON), F32),
            pltpu.VMEM((C * ROWS, LON), F32),
            pltpu.SemaphoreType.DMA((7,)),
        ],
        0, 1 << 20, pl.BlockSpec(memory_space=pltpu.HBM),
    )(
        *(
            pltpu.with_memory_space_constraint(value, pltpu.HBM)
            for value in (
                window_snapshots[0], obs_values[0], obs_index, background, taps,
                output_pointwise_weight, hidden_bias_vector[None, :],
            )
        )
    )
    second = exchange(second, far_strip)
    first = exchange(first, near_strip)
    far_own = exchange(own, far_window)

    sums, forward_weight, back_weight, bias, out_back = call(
        prepare_kernel,
        (
            jax.ShapeDtypeStruct((ROWS, 72, LON), F32),
            jax.ShapeDtypeStruct((HID, 9 * C), BF16),
            jax.ShapeDtypeStruct((3 * C, 3 * HID), BF16),
            jax.ShapeDtypeStruct((HID, LON), F32),
            jax.ShapeDtypeStruct((HID, C), BF16),
        ),
        [], ROWS * 2 * 80 * OBS * LON, 1 << 20,
    )(observed, index, taps, bias, out_weight)
    weights = (forward_weight, bias, out_weight, back_weight, out_back)
    inside = forward(in_order(6), own)
    first, second, inside, sums = lax.optimization_barrier((first, second, inside, sums))

    ext, sent, halo, above, below = call(
        extend_kernel,
        (shape(16 * C), shape(14 * C), shape(6 * C), shape(2 * C), shape(2 * C)),
        [], 0, 1 << 20,
    )(own, first, second)
    far = exchange(halo, far_window)
    near = exchange(sent, near_window)
    outside = forward(((0, 1), (2, 3), (10, 11), (12, 13)), ext)
    part, inner = call(
        first_near_kernel, (shape(12 * C), shape(12 * C)), gradient_scratch(12),
        row_flops(12), 2 << 20,
    )(near, far_own, ext, *inside, *outside, *weights)
    state, sent = call(
        first_kernel, (shape(12 * C), shape(10 * C)), gradient_scratch(12), row_flops(12),
        2 << 20,
    )(
        far, far_own, part, inner, ext, ground, *inside, *outside, *weights, sums, above, below
    )
    far = exchange(sent, far_window)
    near = exchange(sent, near_window)
    given = (state, ground, *forward(in_order(10), state), *weights)
    part = call(
        second_near_kernel, shape(8 * C), gradient_scratch(8), row_flops(8), 2 << 20
    )(near, state, *given[2:])
    analysis = call(
        second_kernel,
        jax.ShapeDtypeStruct((C, ROWS, LON), BF16),
        gradient_scratch(8) + [pltpu.VMEM((C * ROWS, LON), F32)],
        row_flops(8), 2 << 20,
    )(far, part, *given, sums)
    return analysis[None]


def solution(mesh):
    placed = (
        P("tm", None, "lat", None),
        P(None, "lat", None),
        P("tm", None, "lat"),
        P("tm", "lat"),
        P(),
        P(),
        P(),
    )
    return jax.shard_map(
        on_device, mesh=mesh, in_specs=placed, out_specs=P("tm", None, "lat", None), check_vma=False
    )
```

```python
import functools

import jax
import jax.numpy as jnp
from jax import lax
from jax.experimental import pallas as pl
from jax.experimental.pallas import tpu as pltpu
from jax.sharding import PartitionSpec as P


C = 64
HID = 256
ROWS = 8
LON = 128
OBS = 256
STEP = 0.3

F32 = jnp.float32
BF16 = jnp.bfloat16
VMEM = pl.BlockSpec(memory_space=pltpu.VMEM)

X_PART = 4 * C
PAYLOAD = X_PART + 2 * C


def call(kernel, outs, scratch, flops, bytes_accessed, spec=VMEM, grant=48 << 20):
    def run(*args):
        return pl.pallas_call(
            kernel,
            out_shape=outs,
            in_specs=[spec] * len(args),
            out_specs=jax.tree.map(lambda _: VMEM, outs),
            scratch_shapes=scratch,
            cost_estimate=pl.CostEstimate(
                flops=flops, bytes_accessed=bytes_accessed, transcendentals=0
            ),
            compiler_params=pltpu.CompilerParams(vmem_limit_bytes=grant),
        )(*args)

    return run


def rows_of(ref, first, width=C):
    return ref[first * width : (first + 1) * width, :]


def rows_in(ref, first, count):
    return [(ref, row) for row in range(first, first + count)]


def at(rows, place, width=C):
    ref, row = rows[place]
    return rows_of(ref, row, width)


def beside(rows, a, b):
    return jnp.concatenate([at(rows, a), at(rows, b)], axis=1)


def latitude(row):
    return pl.ds(row, C, stride=ROWS)


def local_cells(index):
    local = index - lax.axis_index("lat") * (ROWS * LON)
    high = lax.shift_right_arithmetic(local, 7)
    return local - high * LON, high


def with_ones(values):
    return jnp.concatenate([values, jnp.ones((16, OBS), BF16)], axis=0)


def observation_sums(values, low, high, row):
    cell = lax.broadcasted_iota(jnp.int32, (LON, OBS), 0)
    hit = jnp.where((low == cell) & (high == row), 1.0, 0.0).astype(BF16)
    return lax.dot_general(
        values, hit, (((1,), (1,)), ((), ())), preferred_element_type=F32
    )


def innovation_of(sums, own):
    return sums[C : C + 1, :] * own - sums[:C, :]


def pack_kernel(
    x_hbm, obs_hbm, index_hbm, bg_hbm, taps_hbm, out_weight_hbm, bias_hbm, own_ref, bg_rows_ref,
    first_ref, second_ref, obs_ref, index_ref, taps_ref, out_weight_ref, bias_ref, x_ref, bg_ref,
    xs, bs, sems,
):
    copies = [
        pltpu.make_async_copy(source, target, sems.at[place])
        for place, (source, target) in enumerate(
            (
                (x_hbm, x_ref), (obs_hbm, obs_ref), (index_hbm, index_ref), (bg_hbm, bg_ref),
                (taps_hbm, taps_ref), (out_weight_hbm, out_weight_ref), (bias_hbm, bias_ref),
            )
        )
    ]
    for copy in copies:
        copy.start()
    copies[0].wait()
    even = lax.rem(lax.axis_index("lat"), 2) == 0

    def send(place, up, down):
        at = slice(place * C, (place + 1) * C)
        first_ref[at, :] = jnp.where(even, down, up).astype(BF16)
        second_ref[at, :] = jnp.where(even, up, down).astype(BF16)

    xs[...] = x_ref[...].astype(F32).reshape(ROWS * C, LON)
    for row in range(4):
        up, down = xs[latitude(row), :], xs[latitude(row + 4), :]
        own_ref[row * C : (row + 1) * C, :] = up.astype(BF16)
        own_ref[(row + 4) * C : (row + 5) * C, :] = down.astype(BF16)
        send(row, up, down)
    copies[1].wait()
    copies[2].wait()
    low, high = local_cells(index_ref[...])
    values = with_ones(obs_ref[...])
    copies[3].wait()
    bs[...] = bg_ref[...].astype(F32).reshape(ROWS * C, LON)
    opening = lax.axis_index("tm") == 0

    def edge(row):
        own = xs[latitude(row), :]
        ground = bs[latitude(row), :]
        value = innovation_of(observation_sums(values, low, high, row), own)
        return value + jnp.where(opening, own - ground, 0.0)

    for row in range(2):
        send(4 + row, edge(row), edge(row + 6))
    for row in range(ROWS):
        bg_rows_ref[row * C : (row + 1) * C, :] = bs[latitude(row), :].astype(BF16)
    for copy in copies[4:]:
        copy.wait()


def extend_kernel(
    own_ref, first_ref, second_ref, ext_ref, near_ref, far_ref, above_edge_ref, below_edge_ref
):
    strip = lax.axis_index("lat")
    even = lax.rem(strip, 2) == 0
    zero = jnp.zeros((X_PART, LON), BF16)
    above = jnp.where(even, second_ref[...], first_ref[...])
    below = jnp.where(even, first_ref[...], second_ref[...])
    above_edge_ref[...] = above[X_PART:, :]
    below_edge_ref[...] = below[X_PART:, :]
    above = jnp.where(strip > 0, above[:X_PART, :], zero)
    below = jnp.where(strip < lax.axis_size("lat") - 1, below[:X_PART, :], zero)
    far_ref[: 3 * C, :] = above[C:, :]
    far_ref[3 * C :, :] = below[: 3 * C, :]
    near_ref[: 3 * C, :] = above[C:, :]
    near_ref[3 * C : 11 * C, :] = own_ref[...]
    near_ref[11 * C :, :] = below[: 3 * C, :]
    ext_ref[:X_PART, :] = above
    ext_ref[X_PART : X_PART + ROWS * C, :] = own_ref[...]
    ext_ref[X_PART + ROWS * C :, :] = below


def turn(value, b):
    return value if b == 1 else pltpu.roll(value, 1 if b == 0 else LON - 1, 1)


def actives(work, rows, kernel_ref, quad_ref, bias_ref, shifted, mixed):
    quads, pairs = work
    bias = jnp.concatenate([bias_ref[...], bias_ref[...]], axis=1)
    for place, pair in enumerate(pair for quad in quads for pair in quad):
        d = [at(rows, pair[0] + a).astype(F32) for a in range(4)]
        for j, value in enumerate((d[0] - d[2], d[1] + d[2], d[2] - d[1], d[1] - d[3])):
            for b in range(3):
                start = (3 * place + b) * C
                mixed[j, start : start + C, :] = turn(value, b).astype(BF16)
    for place in sorted({first + a for pair in pairs for first in pair for a in range(3)}):
        value = at(rows, place)
        for b in range(3):
            moved = value if b == 1 else turn(value.astype(F32), b).astype(BF16)
            shifted[b, place * C : (place + 1) * C, :] = moved
    for place, (first, second) in enumerate(quads):
        start, middle, end = (3 * C * (2 * place + n) for n in range(3))
        m = [
            jnp.dot(
                quad_ref[j * HID : (j + 1) * HID, :],
                jnp.concatenate([mixed[j, start:middle, :], mixed[j, middle:end, :]], axis=1),
                preferred_element_type=F32,
            )
            for j in range(4)
        ]
        yield (first[0], second[0]), jnp.tanh(m[0] + m[1] + m[2] + bias).astype(BF16)
        yield (first[1], second[1]), jnp.tanh(m[1] - m[2] - m[3] + bias).astype(BF16)

    def stack(first):
        return jnp.concatenate(
            [
                shifted[b, (first + a) * C : (first + a + 1) * C, :]
                for a in range(3)
                for b in range(3)
            ],
            axis=0,
        )

    for pair in pairs:
        cells = jnp.concatenate([stack(row) for row in pair], axis=1)
        before = jnp.dot(kernel_ref[...], cells, preferred_element_type=F32) + bias
        yield pair, jnp.tanh(before).astype(BF16)


def rows_of_work(work):
    quads, pairs = work
    return sorted([row for quad in quads for pair in quad for row in pair] + [r for p in pairs for r in p])


def store_pair(ref, first, value, width=C):
    ref[first * width : (first + 1) * width, :] = value[:, :LON]
    ref[(first + 1) * width : (first + 2) * width, :] = value[:, LON:]


def forward_kernel(
    work, state_ref, kernel_ref, quad_ref, bias_ref, out_weight_ref, active_ref, forecast_ref,
    shifted, mixed,
):
    rows = rows_in(state_ref, 0, state_ref.shape[0] // C)
    places = {row: place for place, row in enumerate(rows_of_work(work))}
    for pair, active in actives(work, rows, kernel_ref, quad_ref, bias_ref, shifted, mixed):
        step = jnp.dot(out_weight_ref[...], active, preferred_element_type=F32)
        centre = beside(rows, pair[0] + 1, pair[1] + 1).astype(F32)
        forecast = (centre + step).astype(BF16)
        for half, row in enumerate(pair):
            lanes = slice(half * LON, (half + 1) * LON)
            place = places[row]
            active_ref[place * HID : (place + 1) * HID, :] = active[:, lanes]
            forecast_ref[place * C : (place + 1) * C, :] = forecast[:, lanes]


def prepare_kernel(
    obs_ref, index_ref, kernel_ref, bias_ref, out_weight_ref, sums_ref, forward_ref, quad_ref,
    back_ref, wide_bias_ref, out_back_ref,
):
    low, high = local_cells(index_ref[...])
    values = with_ones(obs_ref[...])
    for row in range(ROWS):
        sums_ref[row] = observation_sums(values, low, high, row)[:72, :]
    forward_ref[...] = kernel_ref[...].T
    g = [kernel_ref[a * 3 * C : (a + 1) * 3 * C, :].astype(F32) for a in range(3)]
    ends = g[0] + g[2]
    for j, value in enumerate((g[0], 0.5 * (ends + g[1]), 0.5 * (ends - g[1]), g[2])):
        quad_ref[j * HID : (j + 1) * HID, :] = value.astype(BF16).T
    out_back_ref[...] = out_weight_ref[...].T
    wide_bias_ref[...] = jnp.broadcast_to(bias_ref[...], (LON, HID)).T
    for a in range(3):
        back_ref[:, a * HID : (a + 1) * HID] = kernel_ref[(2 - a) * 3 * C : (3 - a) * 3 * C, :]


def residual_part(
    work, prev, own_ref, kernel_ref, quad_ref, bias_ref, out_weight_ref, shifted, mixed, take
):
    own_rows = rows_in(own_ref, 2, max(rows_of_work(work)) + 1)
    for (a, b), active in actives(work, prev, kernel_ref, quad_ref, bias_ref, shifted, mixed):
        step = jnp.dot(out_weight_ref[...], active, preferred_element_type=F32)
        centre = beside(prev, a + 1, b + 1).astype(F32)
        guess = (centre + step).astype(BF16).astype(F32)
        resid = (beside(own_rows, a, b).astype(F32) - guess).astype(BF16)
        take(a, resid[:, :LON])
        take(b, resid[:, LON:])


def strip_ends():
    strip = lax.axis_index("lat")
    return -strip * ROWS, (lax.axis_size("lat") - strip) * ROWS


def adjoint_part(
    count, margin, later, active, forecast, back_ref, out_back_ref, cot, target, take
):
    top, bottom = strip_ends()
    for row in range(0, count + 2, 2):
        resid = beside(later, row, row + 1).astype(F32) - beside(forecast, row, row + 1).astype(F32)
        resid = resid.astype(BF16)
        store_pair(target, row, resid)
        projected = jnp.dot(out_back_ref[...], resid, preferred_element_type=F32)
        for half in range(2):
            place = row + half - margin - 1
            value = at(active, row + half, HID).astype(F32)
            value = (1.0 - value * value) * projected[:, half * LON : (half + 1) * LON]
            if not 0 <= place < ROWS:
                value = jnp.where((place >= top) & (place < bottom), value, 0.0)
            cot[(row + half) * HID : (row + half + 1) * HID, :] = value.astype(BF16)
    closing = lax.axis_index("tm") == lax.axis_size("tm") - 1
    for row in range(0, count, 2):
        cells = jnp.concatenate(
            [cot[row * HID : (row + 3) * HID, :], cot[(row + 1) * HID : (row + 4) * HID, :]], axis=1
        )
        spread = jnp.dot(back_ref[...], cells, preferred_element_type=F32)
        for half in range(2):
            lanes = slice(half * LON, (half + 1) * LON)
            pulled = (
                pltpu.roll(spread[:C, lanes], LON - 1, 1)
                + spread[C : 2 * C, lanes]
                + pltpu.roll(spread[2 * C :, lanes], 1, 1)
            )
            resid = rows_of(target, row + half + 1).astype(F32)
            take(row + half, jnp.where(closing, 0.0, resid + pulled).astype(BF16))


def branches():
    window = lax.axis_index("tm")
    even = lax.rem(window, 2) == 0
    opening = window == 0
    return even & jnp.logical_not(opening), opening, jnp.logical_not(even)


def quads_of(count):
    return tuple(((row, row + 1), (row + 2, row + 3)) for row in range(0, count - 3, 4))


INSIDE = (quads_of(4), ((4, 5),))
OUTSIDE = ((((0, 1), (2, 3)), ((10, 11), (12, 13))), ())
INNER = ((((3, 4), (5, 6)),), ((7, 8),))
OUTER = ((((0, 1), (10, 11)),), ((2, 9),))
TWELVE = (quads_of(12), ())
TEN = (quads_of(8), ((8, 9),))
EIGHT = (quads_of(8), ())


def first_near_kernel(
    near_ref, far_own_ref, own_ref, active_in_ref, forecast_in_ref, active_out_ref, forecast_out_ref,
    kernel_ref, quad_ref, bias_ref, out_weight_ref, back_ref, out_back_ref, part_ref, inner_ref, shifted, mixed,
    cot, target,
):
    def put(ref):
        def take(row, value):
            ref[row * C : (row + 1) * C, :] = value

        return take

    even, _, odd = branches()

    @pl.when(jnp.logical_not(odd))
    def _():
        adjoint_part(
            12, 2, rows_in(near_ref, 0, 14), split_rows(active_out_ref, active_in_ref),
            split_rows(forecast_out_ref, forecast_in_ref), back_ref, out_back_ref, cot, target,
            put(part_ref),
        )

    @pl.when(even)
    def _():
        prev = [None] * 3 + rows_in(far_own_ref, 0, ROWS)
        residual_part(
            INNER, prev, own_ref, kernel_ref, quad_ref, bias_ref, out_weight_ref,
            shifted, mixed, put(inner_ref)
        )

    @pl.when(odd)
    def _():
        residual_part(
            TWELVE, rows_in(near_ref, 0, 14), own_ref, kernel_ref, quad_ref, bias_ref, out_weight_ref,
            shifted, mixed, put(part_ref),
        )


def split_rows(outside_ref, inside_ref):
    return rows_in(outside_ref, 0, 4) + rows_in(inside_ref, 0, 6) + rows_in(outside_ref, 4, 4)


def first_kernel(
    far_ref, far_own_ref, part_ref, inner_ref, own_ref, bg_ref, active_in_ref, forecast_in_ref,
    active_out_ref, forecast_out_ref, kernel_ref, quad_ref, bias_ref, out_weight_ref, back_ref, out_back_ref,
    sums_ref, above_ref, below_ref, state_ref, sent_ref, shifted, mixed, cot, target,
):
    top, bottom = strip_ends()

    def step(row, resid, adjoint):
        own = rows_of(own_ref, row + 2).astype(F32)
        place = row - 2
        if place < 0:
            innovation = rows_of(above_ref, row).astype(F32)
        elif place >= ROWS:
            innovation = rows_of(below_ref, place - ROWS).astype(F32)
        else:
            innovation = innovation_of(sums_ref[place], own)
        value = own - STEP * (resid.astype(F32) - adjoint.astype(F32) + innovation)
        if not 0 <= place < ROWS:
            value = jnp.where((place >= top) & (place < bottom), value, 0.0)
        value = value.astype(BF16)
        state_ref[row * C : (row + 1) * C, :] = value
        if 1 <= row < 11:
            sent_ref[(row - 1) * C : row * C, :] = value

    even, opening, odd = branches()
    far = rows_in(far_ref, 0, 3) + rows_in(far_own_ref, 0, ROWS) + rows_in(far_ref, 3, 3)

    @pl.when(even)
    def _():
        residual_part(
            OUTER, far, own_ref, kernel_ref, quad_ref, bias_ref, out_weight_ref, shifted,
            mixed, lambda row, resid: step(row, resid, rows_of(part_ref, row)),
        )
        for row in range(3, 9):
            step(row, rows_of(inner_ref, row), rows_of(part_ref, row))

    @pl.when(opening)
    def _():
        for row in range(12):
            place = row - 2
            resid = jnp.zeros((C, LON), BF16)
            if 0 <= place < ROWS:
                own = rows_of(own_ref, row + 2).astype(F32)
                resid = (own - rows_of(bg_ref, place).astype(F32)).astype(BF16)
            step(row, resid, rows_of(part_ref, row))

    @pl.when(odd)
    def _():
        adjoint_part(
            12, 2, far, split_rows(active_out_ref, active_in_ref),
            split_rows(forecast_out_ref, forecast_in_ref), back_ref, out_back_ref, cot, target,
            lambda row, adjoint: step(row, rows_of(part_ref, row), adjoint),
        )


def second_near_kernel(
    near_ref, own_ref, active_ref, forecast_ref, kernel_ref, quad_ref, bias_ref, out_weight_ref,
    back_ref, out_back_ref, part_ref, shifted, mixed, cot, target,
):
    def take(row, value):
        part_ref[row * C : (row + 1) * C, :] = value

    _, _, odd = branches()
    near = rows_in(near_ref, 0, 10)

    @pl.when(jnp.logical_not(odd))
    def _():
        adjoint_part(
            8, 0, near, rows_in(active_ref, 0, 10), rows_in(forecast_ref, 0, 10), back_ref,
            out_back_ref, cot, target, take,
        )

    @pl.when(odd)
    def _():
        residual_part(
            EIGHT, near, own_ref, kernel_ref, quad_ref, bias_ref, out_weight_ref,
            shifted, mixed, take
        )


def second_kernel(
    far_ref, part_ref, own_ref, bg_ref, active_ref, forecast_ref, kernel_ref, quad_ref, bias_ref,
    out_weight_ref, back_ref, out_back_ref, sums_ref, out_ref, shifted, mixed, cot, target, wide,
):
    def step(row, resid, adjoint):
        own = rows_of(own_ref, row + 2).astype(F32)
        innovation = innovation_of(sums_ref[row], own)
        value = own - STEP * (resid.astype(F32) - adjoint.astype(F32) + innovation)
        wide[latitude(row), :] = value

    even, opening, odd = branches()
    far = rows_in(far_ref, 0, 10)

    @pl.when(even)
    def _():
        residual_part(
            EIGHT, far, own_ref, kernel_ref, quad_ref, bias_ref, out_weight_ref, shifted,
            mixed, lambda row, resid: step(row, resid, rows_of(part_ref, row)),
        )

    @pl.when(opening)
    def _():
        for row in range(ROWS):
            own = rows_of(own_ref, row + 2).astype(F32)
            resid = (own - rows_of(bg_ref, row).astype(F32)).astype(BF16)
            step(row, resid, rows_of(part_ref, row))

    @pl.when(odd)
    def _():
        adjoint_part(
            8, 0, far, rows_in(active_ref, 0, 10), rows_in(forecast_ref, 0, 10), back_ref,
            out_back_ref, cot, target, lambda row, adjoint: step(row, rows_of(part_ref, row), adjoint),
        )

    out_ref[...] = wide[...].reshape(C, ROWS, LON).astype(BF16)


def exchange(value, partner):
    windows, strips = lax.axis_size("tm"), lax.axis_size("lat")
    pairs = []
    for window in range(windows):
        for strip in range(strips):
            to_window, to_strip = partner(window, strip, windows - 1, strips - 1)
            pairs.append((window * strips + strip, to_window * strips + to_strip))
    return lax.ppermute(value, ("tm", "lat"), pairs)


def near_strip(window, strip, last_window, last_strip):
    return window, strip ^ 1


def far_strip(window, strip, last_window, last_strip):
    if strip in (0, last_strip):
        return window ^ 1, strip
    return window, ((strip + 1) ^ 1) - 1


def near_window(window, strip, last_window, last_strip):
    return window ^ 1, strip


def far_window(window, strip, last_window, last_strip):
    if window in (0, last_window):
        return window, strip ^ 2
    return ((window + 1) ^ 1) - 1, strip


def shape(rows, dtype=BF16):
    return jax.ShapeDtypeStruct((rows, LON), dtype)


def conv_scratch(count):
    return [
        pltpu.VMEM((3, (count + 2) * C, LON), BF16),
        pltpu.VMEM((4, (count // 2) * 3 * C, LON), BF16),
    ]


def gradient_scratch(count):
    return conv_scratch(count) + [
        pltpu.VMEM(((count + 2) * HID, LON), BF16),
        pltpu.VMEM(((count + 2) * C, LON), BF16),
    ]


def row_flops(rows):
    return rows * 2 * LON * HID * 10 * C


def on_device(
    window_snapshots, background, obs_values, obs_index, input_kernel_weight, hidden_bias_vector,
    output_pointwise_weight,
):
    def forward(work, state):
        count = len(rows_of_work(work))
        return call(
            functools.partial(forward_kernel, work),
            (shape(count * HID), shape(count * C)),
            conv_scratch(state.shape[0] // C - 2),
            row_flops(count), 2 << 20,
        )(state, forward_weight, quad_weight, bias, out_weight)

    taps = jnp.transpose(input_kernel_weight, (0, 1, 3, 2)).reshape(9 * C, HID)
    own, ground, first, second, observed, index, taps, out_weight, bias = call(
        pack_kernel,
        (
            shape(ROWS * C), shape(ROWS * C), shape(PAYLOAD), shape(PAYLOAD),
            jax.ShapeDtypeStruct((C, OBS), BF16),
            jax.ShapeDtypeStruct((1, OBS), jnp.int32),
            jax.ShapeDtypeStruct((9 * C, HID), BF16),
            jax.ShapeDtypeStruct((C, HID), BF16),
            jax.ShapeDtypeStruct((1, HID), F32),
        ),
        [
            pltpu.VMEM((C, ROWS, LON), BF16),
            pltpu.VMEM((C, ROWS, LON), BF16),
            pltpu.VMEM((C * ROWS, LON), F32),
            pltpu.VMEM((C * ROWS, LON), F32),
            pltpu.SemaphoreType.DMA((7,)),
        ],
        0, 1 << 20, pl.BlockSpec(memory_space=pltpu.HBM),
    )(
        *(
            pltpu.with_memory_space_constraint(value, pltpu.HBM)
            for value in (
                window_snapshots[0], obs_values[0], obs_index, background, taps,
                output_pointwise_weight, hidden_bias_vector[None, :],
            )
        )
    )
    second = exchange(second, far_strip)
    first = exchange(first, near_strip)
    far_own = exchange(own, far_window)

    sums, forward_weight, quad_weight, back_weight, bias, out_back = call(
        prepare_kernel,
        (
            jax.ShapeDtypeStruct((ROWS, 72, LON), F32),
            jax.ShapeDtypeStruct((HID, 9 * C), BF16),
            jax.ShapeDtypeStruct((4 * HID, 3 * C), BF16),
            jax.ShapeDtypeStruct((3 * C, 3 * HID), BF16),
            jax.ShapeDtypeStruct((HID, LON), F32),
            jax.ShapeDtypeStruct((HID, C), BF16),
        ),
        [], ROWS * 2 * 80 * OBS * LON, 1 << 20,
    )(observed, index, taps, bias, out_weight)
    weights = (forward_weight, quad_weight, bias, out_weight, back_weight, out_back)
    inside = forward(INSIDE, own)
    first, second, inside, sums = lax.optimization_barrier((first, second, inside, sums))

    ext, sent, halo, above, below = call(
        extend_kernel,
        (shape(16 * C), shape(14 * C), shape(6 * C), shape(2 * C), shape(2 * C)),
        [], 0, 1 << 20,
    )(own, first, second)
    far = exchange(halo, far_window)
    near = exchange(sent, near_window)
    outside = forward(OUTSIDE, ext)
    part, inner = call(
        first_near_kernel, (shape(12 * C), shape(12 * C)), gradient_scratch(12),
        row_flops(12), 2 << 20,
    )(near, far_own, ext, *inside, *outside, *weights)
    state, sent = call(
        first_kernel, (shape(12 * C), shape(10 * C)), gradient_scratch(12), row_flops(12),
        2 << 20,
    )(
        far, far_own, part, inner, ext, ground, *inside, *outside, *weights, sums, above, below
    )
    far = exchange(sent, far_window)
    near = exchange(sent, near_window)
    given = (state, ground, *forward(TEN, state), *weights)
    part = call(
        second_near_kernel, shape(8 * C), gradient_scratch(8), row_flops(8), 2 << 20
    )(near, state, *given[2:])
    analysis = call(
        second_kernel,
        jax.ShapeDtypeStruct((C, ROWS, LON), BF16),
        gradient_scratch(8) + [pltpu.VMEM((C * ROWS, LON), F32)],
        row_flops(8), 2 << 20,
    )(far, part, *given, sums)
    return analysis[None]


def solution(mesh):
    placed = (
        P("tm", None, "lat", None),
        P(None, "lat", None),
        P("tm", None, "lat"),
        P("tm", "lat"),
        P(),
        P(),
        P(),
    )
    return jax.shard_map(
        on_device, mesh=mesh, in_specs=placed, out_specs=P("tm", None, "lat", None), check_vma=False
    )
```

```python
import functools

import jax
import jax.numpy as jnp
from jax import lax
from jax.experimental import pallas as pl
from jax.experimental.pallas import tpu as pltpu
from jax.sharding import PartitionSpec as P


C = 64
HID = 256
ROWS = 8
LON = 128
OBS = 256
STEP = 0.3

F32 = jnp.float32
BF16 = jnp.bfloat16
VMEM = pl.BlockSpec(memory_space=pltpu.VMEM)

X_PART = 4 * C
PAYLOAD = X_PART + 2 * C


def call(kernel, outs, scratch, flops, bytes_accessed, spec=VMEM, grant=48 << 20):
    def run(*args):
        return pl.pallas_call(
            kernel,
            out_shape=outs,
            in_specs=[spec] * len(args),
            out_specs=jax.tree.map(lambda _: VMEM, outs),
            scratch_shapes=scratch,
            cost_estimate=pl.CostEstimate(
                flops=flops, bytes_accessed=bytes_accessed, transcendentals=0
            ),
            compiler_params=pltpu.CompilerParams(vmem_limit_bytes=grant),
        )(*args)

    return run


def rows_of(ref, first, width=C):
    return ref[first * width : (first + 1) * width, :]


def rows_in(ref, first, count):
    return [(ref, row) for row in range(first, first + count)]


def at(rows, place, width=C):
    ref, row = rows[place]
    return rows_of(ref, row, width)


def beside(rows, *places):
    return jnp.concatenate([at(rows, place) for place in places], axis=1)


def latitude(row):
    return pl.ds(row, C, stride=ROWS)


def local_cells(index):
    local = index - lax.axis_index("lat") * (ROWS * LON)
    high = lax.shift_right_arithmetic(local, 7)
    return local - high * LON, high


def with_ones(values):
    return jnp.concatenate([values, jnp.ones((16, OBS), BF16)], axis=0)


def observation_sums(values, low, high, row):
    cell = lax.broadcasted_iota(jnp.int32, (LON, OBS), 0)
    hit = jnp.where((low == cell) & (high == row), 1.0, 0.0).astype(BF16)
    return lax.dot_general(
        values, hit, (((1,), (1,)), ((), ())), preferred_element_type=F32
    )


def innovation_of(sums, own):
    return sums[C : C + 1, :] * own - sums[:C, :]


def pack_kernel(
    x_hbm, obs_hbm, index_hbm, bg_hbm, taps_hbm, out_weight_hbm, bias_hbm, own_ref, bg_rows_ref,
    up_ref, down_ref, obs_ref, index_ref, taps_ref, out_weight_ref, bias_ref, x_ref, bg_ref,
    xs, bs, sems,
):
    copies = [
        pltpu.make_async_copy(source, target, sems.at[place])
        for place, (source, target) in enumerate(
            (
                (x_hbm, x_ref), (obs_hbm, obs_ref), (index_hbm, index_ref), (bg_hbm, bg_ref),
                (taps_hbm, taps_ref), (out_weight_hbm, out_weight_ref), (bias_hbm, bias_ref),
            )
        )
    ]
    for copy in copies:
        copy.start()
    copies[0].wait()

    def send(place, up, down):
        up_ref[place * C : (place + 1) * C, :] = up.astype(BF16)
        down_ref[place * C : (place + 1) * C, :] = down.astype(BF16)

    xs[...] = x_ref[...].astype(F32).reshape(ROWS * C, LON)
    for row in range(4):
        up, down = xs[latitude(row), :], xs[latitude(row + 4), :]
        own_ref[row * C : (row + 1) * C, :] = up.astype(BF16)
        own_ref[(row + 4) * C : (row + 5) * C, :] = down.astype(BF16)
        send(row, up, down)
    copies[1].wait()
    copies[2].wait()
    low, high = local_cells(index_ref[...])
    values = with_ones(obs_ref[...])
    copies[3].wait()
    bs[...] = bg_ref[...].astype(F32).reshape(ROWS * C, LON)
    opening = lax.axis_index("tm") == 0

    def edge(row):
        own = xs[latitude(row), :]
        ground = bs[latitude(row), :]
        value = innovation_of(observation_sums(values, low, high, row), own)
        return value + jnp.where(opening, own - ground, 0.0)

    for row in range(2):
        send(4 + row, edge(row), edge(row + 6))
    for row in range(ROWS):
        bg_rows_ref[row * C : (row + 1) * C, :] = bs[latitude(row), :].astype(BF16)
    for copy in copies[4:]:
        copy.wait()


def extend_kernel(
    own_ref, above_ref, below_ref, ext_ref, near_ref, far_ref, above_edge_ref, below_edge_ref
):
    strip = lax.axis_index("lat")
    zero = jnp.zeros((X_PART, LON), BF16)
    above_edge_ref[...] = above_ref[X_PART:, :]
    below_edge_ref[...] = below_ref[X_PART:, :]
    above = jnp.where(strip > 0, above_ref[:X_PART, :], zero)
    below = jnp.where(strip < lax.axis_size("lat") - 1, below_ref[:X_PART, :], zero)
    far_ref[: 3 * C, :] = above[C:, :]
    far_ref[3 * C :, :] = below[: 3 * C, :]
    near_ref[: 3 * C, :] = above[C:, :]
    near_ref[3 * C : 11 * C, :] = own_ref[...]
    near_ref[11 * C :, :] = below[: 3 * C, :]
    ext_ref[:X_PART, :] = above
    ext_ref[X_PART : X_PART + ROWS * C, :] = own_ref[...]
    ext_ref[X_PART + ROWS * C :, :] = below


def turn(value, b):
    return value if b == 1 else pltpu.roll(value, 1 if b == 0 else LON - 1, 1)


def actives(work, rows, conv_ref, bias_ref, mixed):
    for place, pair in enumerate(pair for group in work for pair in group):
        d = [at(rows, pair[0] + a).astype(F32) for a in range(4)]
        for j, value in enumerate((d[0] - d[2], d[1] + d[2], d[2] - d[1], d[1] - d[3])):
            for b in range(3):
                start = (3 * place + b) * C
                mixed[j, start : start + C, :] = turn(value, b).astype(BF16)
    place = 0
    for group in work:
        bias = jnp.concatenate([bias_ref[...]] * len(group), axis=1)
        spans = [slice(3 * C * (place + n), 3 * C * (place + n + 1)) for n in range(len(group))]
        place += len(group)
        m = [
            jnp.dot(
                conv_ref[j * HID : (j + 1) * HID, :],
                jnp.concatenate([mixed[j, span, :] for span in spans], axis=1),
                preferred_element_type=F32,
            )
            for j in range(4)
        ]
        upper, lower = zip(*group)
        yield upper, jnp.tanh(m[0] + m[1] + m[2] + bias).astype(BF16)
        yield lower, jnp.tanh(m[1] - m[2] - m[3] + bias).astype(BF16)


def rows_of_work(work):
    return sorted(row for group in work for pair in group for row in pair)


def lanes_of(half):
    return slice(half * LON, (half + 1) * LON)


def store_pair(ref, first, value, width=C):
    ref[first * width : (first + 1) * width, :] = value[:, :LON]
    ref[(first + 1) * width : (first + 2) * width, :] = value[:, LON:]


def forward_kernel(
    work, state_ref, conv_ref, bias_ref, out_weight_ref, active_ref, forecast_ref, mixed
):
    rows = rows_in(state_ref, 0, state_ref.shape[0] // C)
    order = {row: place for place, row in enumerate(rows_of_work(work))}
    for some, active in actives(work, rows, conv_ref, bias_ref, mixed):
        step = jnp.dot(out_weight_ref[...], active, preferred_element_type=F32)
        centre = beside(rows, *(row + 1 for row in some)).astype(F32)
        forecast = (centre + step).astype(BF16)
        for half, row in enumerate(some):
            place = order[row]
            active_ref[place * HID : (place + 1) * HID, :] = active[:, lanes_of(half)]
            forecast_ref[place * C : (place + 1) * C, :] = forecast[:, lanes_of(half)]


def prepare_kernel(
    obs_ref, index_ref, kernel_ref, bias_ref, out_weight_ref, sums_ref, conv_ref, back_ref,
    wide_bias_ref, out_back_ref,
):
    low, high = local_cells(index_ref[...])
    values = with_ones(obs_ref[...])
    for row in range(ROWS):
        sums_ref[row] = observation_sums(values, low, high, row)[:72, :]
    g = [kernel_ref[a * 3 * C : (a + 1) * 3 * C, :].astype(F32) for a in range(3)]
    ends = g[0] + g[2]
    for j, value in enumerate((g[0], 0.5 * (ends + g[1]), 0.5 * (ends - g[1]), g[2])):
        conv_ref[j * HID : (j + 1) * HID, :] = value.astype(BF16).T
    out_back_ref[...] = out_weight_ref[...].T
    wide_bias_ref[...] = jnp.broadcast_to(bias_ref[...], (LON, HID)).T
    for a in range(3):
        back_ref[:, a * HID : (a + 1) * HID] = kernel_ref[(2 - a) * 3 * C : (3 - a) * 3 * C, :]


def residual_part(
    work, prev, own_ref, conv_ref, bias_ref, out_weight_ref, mixed, take
):
    own_rows = rows_in(own_ref, 2, max(rows_of_work(work)) + 1)
    for some, active in actives(work, prev, conv_ref, bias_ref, mixed):
        step = jnp.dot(out_weight_ref[...], active, preferred_element_type=F32)
        centre = beside(prev, *(row + 1 for row in some)).astype(F32)
        guess = (centre + step).astype(BF16).astype(F32)
        resid = (beside(own_rows, *some).astype(F32) - guess).astype(BF16)
        for half, row in enumerate(some):
            take(row, resid[:, lanes_of(half)])


def strip_ends():
    strip = lax.axis_index("lat")
    return -strip * ROWS, (lax.axis_size("lat") - strip) * ROWS


def adjoint_part(
    count, margin, later, active, forecast, back_ref, out_back_ref, cot, target, take
):
    top, bottom = strip_ends()
    for row in range(0, count + 2, 2):
        resid = beside(later, row, row + 1).astype(F32) - beside(forecast, row, row + 1).astype(F32)
        resid = resid.astype(BF16)
        store_pair(target, row, resid)
        projected = jnp.dot(out_back_ref[...], resid, preferred_element_type=F32)
        for half in range(2):
            place = row + half - margin - 1
            value = at(active, row + half, HID).astype(F32)
            value = (1.0 - value * value) * projected[:, half * LON : (half + 1) * LON]
            if not 0 <= place < ROWS:
                value = jnp.where((place >= top) & (place < bottom), value, 0.0)
            cot[(row + half) * HID : (row + half + 1) * HID, :] = value.astype(BF16)
    closing = lax.axis_index("tm") == lax.axis_size("tm") - 1
    for row in range(0, count, 2):
        cells = jnp.concatenate(
            [cot[row * HID : (row + 3) * HID, :], cot[(row + 1) * HID : (row + 4) * HID, :]], axis=1
        )
        spread = jnp.dot(back_ref[...], cells, preferred_element_type=F32)
        for half in range(2):
            lanes = slice(half * LON, (half + 1) * LON)
            pulled = (
                pltpu.roll(spread[:C, lanes], LON - 1, 1)
                + spread[C : 2 * C, lanes]
                + pltpu.roll(spread[2 * C :, lanes], 1, 1)
            )
            resid = rows_of(target, row + half + 1).astype(F32)
            take(row + half, jnp.where(closing, 0.0, resid + pulled).astype(BF16))


def branches():
    window = lax.axis_index("tm")
    even = lax.rem(window, 2) == 0
    opening = window == 0
    return even & jnp.logical_not(opening), opening, jnp.logical_not(even)


def quads_of(count):
    return tuple(((row, row + 1), (row + 2, row + 3)) for row in range(0, count - 3, 4))


INSIDE = (((0, 1), (2, 3)), ((4, 5),))
OUTSIDE = (((0, 1), (2, 3)), ((10, 11), (12, 13)))
INNER = (((4, 5), (6, 7)),)
OUTER = (((0, 1), (2, 3)), ((8, 9), (10, 11)))
TWELVE = quads_of(12)
TEN = quads_of(8) + (((8, 9),),)
EIGHT = quads_of(8)


def first_near_kernel(
    near_ref, far_own_ref, own_ref, active_in_ref, forecast_in_ref, active_out_ref, forecast_out_ref,
    conv_ref, bias_ref, out_weight_ref, back_ref, out_back_ref, part_ref, inner_ref, mixed,
    cot, target,
):
    def put(ref):
        def take(row, value):
            ref[row * C : (row + 1) * C, :] = value

        return take

    even, _, odd = branches()

    @pl.when(jnp.logical_not(odd))
    def _():
        adjoint_part(
            12, 2, rows_in(near_ref, 0, 14), split_rows(active_out_ref, active_in_ref),
            split_rows(forecast_out_ref, forecast_in_ref), back_ref, out_back_ref, cot, target,
            put(part_ref),
        )

    @pl.when(even)
    def _():
        prev = [None] * 3 + rows_in(far_own_ref, 0, ROWS)
        residual_part(
            INNER, prev, own_ref, conv_ref, bias_ref, out_weight_ref,
            mixed, put(inner_ref)
        )

    @pl.when(odd)
    def _():
        residual_part(
            TWELVE, rows_in(near_ref, 0, 14), own_ref, conv_ref, bias_ref, out_weight_ref,
            mixed, put(part_ref),
        )


def split_rows(outside_ref, inside_ref):
    return rows_in(outside_ref, 0, 4) + rows_in(inside_ref, 0, 6) + rows_in(outside_ref, 4, 4)


def first_kernel(
    far_ref, far_own_ref, part_ref, inner_ref, own_ref, bg_ref, active_in_ref, forecast_in_ref,
    active_out_ref, forecast_out_ref, conv_ref, bias_ref, out_weight_ref, back_ref, out_back_ref,
    sums_ref, above_ref, below_ref, state_ref, sent_ref, mixed, cot, target,
):
    top, bottom = strip_ends()

    def step(row, resid, adjoint):
        own = rows_of(own_ref, row + 2).astype(F32)
        place = row - 2
        if place < 0:
            innovation = rows_of(above_ref, row).astype(F32)
        elif place >= ROWS:
            innovation = rows_of(below_ref, place - ROWS).astype(F32)
        else:
            innovation = innovation_of(sums_ref[place], own)
        value = own - STEP * (resid.astype(F32) - adjoint.astype(F32) + innovation)
        if not 0 <= place < ROWS:
            value = jnp.where((place >= top) & (place < bottom), value, 0.0)
        value = value.astype(BF16)
        state_ref[row * C : (row + 1) * C, :] = value
        if 1 <= row < 11:
            sent_ref[(row - 1) * C : row * C, :] = value

    even, opening, odd = branches()
    far = rows_in(far_ref, 0, 3) + rows_in(far_own_ref, 0, ROWS) + rows_in(far_ref, 3, 3)

    @pl.when(even)
    def _():
        residual_part(
            OUTER, far, own_ref, conv_ref, bias_ref, out_weight_ref,
            mixed, lambda row, resid: step(row, resid, rows_of(part_ref, row)),
        )
        for row in range(4, 8):
            step(row, rows_of(inner_ref, row), rows_of(part_ref, row))

    @pl.when(opening)
    def _():
        for row in range(12):
            place = row - 2
            resid = jnp.zeros((C, LON), BF16)
            if 0 <= place < ROWS:
                own = rows_of(own_ref, row + 2).astype(F32)
                resid = (own - rows_of(bg_ref, place).astype(F32)).astype(BF16)
            step(row, resid, rows_of(part_ref, row))

    @pl.when(odd)
    def _():
        adjoint_part(
            12, 2, far, split_rows(active_out_ref, active_in_ref),
            split_rows(forecast_out_ref, forecast_in_ref), back_ref, out_back_ref, cot, target,
            lambda row, adjoint: step(row, rows_of(part_ref, row), adjoint),
        )


def second_near_kernel(
    near_ref, own_ref, active_ref, forecast_ref, conv_ref, bias_ref, out_weight_ref,
    back_ref, out_back_ref, part_ref, mixed, cot, target,
):
    def take(row, value):
        part_ref[row * C : (row + 1) * C, :] = value

    _, _, odd = branches()
    near = rows_in(near_ref, 0, 10)

    @pl.when(jnp.logical_not(odd))
    def _():
        adjoint_part(
            8, 0, near, rows_in(active_ref, 0, 10), rows_in(forecast_ref, 0, 10), back_ref,
            out_back_ref, cot, target, take,
        )

    @pl.when(odd)
    def _():
        residual_part(
            EIGHT, near, own_ref, conv_ref, bias_ref, out_weight_ref,
            mixed, take
        )


def second_kernel(
    far_ref, part_ref, own_ref, bg_ref, active_ref, forecast_ref, conv_ref, bias_ref,
    out_weight_ref, back_ref, out_back_ref, sums_ref, out_ref, mixed, cot, target, wide,
):
    def step(row, resid, adjoint):
        own = rows_of(own_ref, row + 2).astype(F32)
        innovation = innovation_of(sums_ref[row], own)
        value = own - STEP * (resid.astype(F32) - adjoint.astype(F32) + innovation)
        wide[latitude(row), :] = value

    even, opening, odd = branches()
    far = rows_in(far_ref, 0, 10)

    @pl.when(even)
    def _():
        residual_part(
            EIGHT, far, own_ref, conv_ref, bias_ref, out_weight_ref,
            mixed, lambda row, resid: step(row, resid, rows_of(part_ref, row)),
        )

    @pl.when(opening)
    def _():
        for row in range(ROWS):
            own = rows_of(own_ref, row + 2).astype(F32)
            resid = (own - rows_of(bg_ref, row).astype(F32)).astype(BF16)
            step(row, resid, rows_of(part_ref, row))

    @pl.when(odd)
    def _():
        adjoint_part(
            8, 0, far, rows_in(active_ref, 0, 10), rows_in(forecast_ref, 0, 10), back_ref,
            out_back_ref, cot, target, lambda row, adjoint: step(row, rows_of(part_ref, row), adjoint),
        )

    out_ref[...] = wide[...].reshape(C, ROWS, LON).astype(BF16)


def exchange(value, partner):
    windows, strips = lax.axis_size("tm"), lax.axis_size("lat")
    pairs = []
    for window in range(windows):
        for strip in range(strips):
            to_window, to_strip = partner(window, strip, windows - 1, strips - 1)
            pairs.append((window * strips + strip, to_window * strips + to_strip))
    return lax.ppermute(value, ("tm", "lat"), pairs)


def strip_below(window, strip, last_window, last_strip):
    return window, (strip + 1) % (last_strip + 1)


def strip_above(window, strip, last_window, last_strip):
    return window, (strip - 1) % (last_strip + 1)


def near_window(window, strip, last_window, last_strip):
    return window ^ 1, strip


def far_window(window, strip, last_window, last_strip):
    if window in (0, last_window):
        return window, strip ^ 2
    return ((window + 1) ^ 1) - 1, strip


def shape(rows, dtype=BF16):
    return jax.ShapeDtypeStruct((rows, LON), dtype)


def conv_scratch(count):
    return [
        pltpu.VMEM((4, (count // 2) * 3 * C, LON), BF16),
    ]


def gradient_scratch(count):
    return conv_scratch(count) + [
        pltpu.VMEM(((count + 2) * HID, LON), BF16),
        pltpu.VMEM(((count + 2) * C, LON), BF16),
    ]


def row_flops(rows):
    return rows * 2 * LON * HID * 10 * C


def on_device(
    window_snapshots, background, obs_values, obs_index, input_kernel_weight, hidden_bias_vector,
    output_pointwise_weight,
):
    def forward(work, state):
        count = len(rows_of_work(work))
        return call(
            functools.partial(forward_kernel, work),
            (shape(count * HID), shape(count * C)),
            conv_scratch(state.shape[0] // C - 2),
            row_flops(count), 2 << 20,
        )(state, conv_weight, bias, out_weight)

    taps = jnp.transpose(input_kernel_weight, (0, 1, 3, 2)).reshape(9 * C, HID)
    own, ground, up, down, observed, index, taps, out_weight, bias = call(
        pack_kernel,
        (
            shape(ROWS * C), shape(ROWS * C), shape(PAYLOAD), shape(PAYLOAD),
            jax.ShapeDtypeStruct((C, OBS), BF16),
            jax.ShapeDtypeStruct((1, OBS), jnp.int32),
            jax.ShapeDtypeStruct((9 * C, HID), BF16),
            jax.ShapeDtypeStruct((C, HID), BF16),
            jax.ShapeDtypeStruct((1, HID), F32),
        ),
        [
            pltpu.VMEM((C, ROWS, LON), BF16),
            pltpu.VMEM((C, ROWS, LON), BF16),
            pltpu.VMEM((C * ROWS, LON), F32),
            pltpu.VMEM((C * ROWS, LON), F32),
            pltpu.SemaphoreType.DMA((7,)),
        ],
        0, 1 << 20, pl.BlockSpec(memory_space=pltpu.HBM),
    )(
        *(
            pltpu.with_memory_space_constraint(value, pltpu.HBM)
            for value in (
                window_snapshots[0], obs_values[0], obs_index, background, taps,
                output_pointwise_weight, hidden_bias_vector[None, :],
            )
        )
    )
    above = exchange(down, strip_below)
    below = exchange(up, strip_above)
    far_own = exchange(own, far_window)

    sums, conv_weight, back_weight, bias, out_back = call(
        prepare_kernel,
        (
            jax.ShapeDtypeStruct((ROWS, 72, LON), F32),
            jax.ShapeDtypeStruct((4 * HID, 3 * C), BF16),
            jax.ShapeDtypeStruct((3 * C, 3 * HID), BF16),
            jax.ShapeDtypeStruct((HID, LON), F32),
            jax.ShapeDtypeStruct((HID, C), BF16),
        ),
        [], ROWS * 2 * 80 * OBS * LON, 1 << 20,
    )(observed, index, taps, bias, out_weight)
    weights = (conv_weight, bias, out_weight, back_weight, out_back)
    inside = forward(INSIDE, own)
    above, below, inside, sums = lax.optimization_barrier((above, below, inside, sums))

    ext, sent, halo, above_edge, below_edge = call(
        extend_kernel,
        (shape(16 * C), shape(14 * C), shape(6 * C), shape(2 * C), shape(2 * C)),
        [], 0, 1 << 20,
    )(own, above, below)
    far = exchange(halo, far_window)
    near = exchange(sent, near_window)
    outside = forward(OUTSIDE, ext)
    part, inner = call(
        first_near_kernel, (shape(12 * C), shape(12 * C)), gradient_scratch(12),
        row_flops(12), 2 << 20,
    )(near, far_own, ext, *inside, *outside, *weights)
    state, sent = call(
        first_kernel, (shape(12 * C), shape(10 * C)), gradient_scratch(12), row_flops(12),
        2 << 20,
    )(
        far, far_own, part, inner, ext, ground, *inside, *outside, *weights, sums,
        above_edge, below_edge,
    )
    far = exchange(sent, far_window)
    near = exchange(sent, near_window)
    given = (state, ground, *forward(TEN, state), *weights)
    part = call(
        second_near_kernel, shape(8 * C), gradient_scratch(8), row_flops(8), 2 << 20
    )(near, state, *given[2:])
    analysis = call(
        second_kernel,
        jax.ShapeDtypeStruct((C, ROWS, LON), BF16),
        gradient_scratch(8) + [pltpu.VMEM((C * ROWS, LON), F32)],
        row_flops(8), 2 << 20,
    )(far, part, *given, sums)
    return analysis[None]


def solution(mesh):
    placed = (
        P("tm", None, "lat", None),
        P(None, "lat", None),
        P("tm", None, "lat"),
        P("tm", "lat"),
        P(),
        P(),
        P(),
    )
    return jax.shard_map(
        on_device, mesh=mesh, in_specs=placed, out_specs=P("tm", None, "lat", None), check_vma=False
    )
```

```python
import functools

import jax
import jax.numpy as jnp
from jax import lax
from jax.experimental import pallas as pl
from jax.experimental.pallas import tpu as pltpu
from jax.sharding import PartitionSpec as P


C = 64
HID = 256
ROWS = 8
LON = 128
OBS = 256
STEP = 0.3

F32 = jnp.float32
BF16 = jnp.bfloat16
VMEM = pl.BlockSpec(memory_space=pltpu.VMEM)

X_PART = 4 * C
PAYLOAD = X_PART + 2 * C


def call(kernel, outs, scratch, flops, bytes_accessed, spec=VMEM, grant=48 << 20):
    def run(*args):
        return pl.pallas_call(
            kernel,
            out_shape=outs,
            in_specs=[spec] * len(args),
            out_specs=jax.tree.map(lambda _: VMEM, outs),
            scratch_shapes=scratch,
            cost_estimate=pl.CostEstimate(
                flops=flops, bytes_accessed=bytes_accessed, transcendentals=0
            ),
            compiler_params=pltpu.CompilerParams(vmem_limit_bytes=grant),
        )(*args)

    return run


def rows_of(ref, first, width=C):
    return ref[first * width : (first + 1) * width, :]


def rows_in(ref, first, count):
    return [(ref, row) for row in range(first, first + count)]


def at(rows, place, width=C):
    ref, row = rows[place]
    return rows_of(ref, row, width)


def beside(rows, *places):
    return jnp.concatenate([at(rows, place) for place in places], axis=1)


def latitude(row):
    return pl.ds(row, C, stride=ROWS)


def local_cells(index):
    local = index - lax.axis_index("lat") * (ROWS * LON)
    high = lax.shift_right_arithmetic(local, 7)
    return local - high * LON, high


def with_ones(values):
    return jnp.concatenate([values, jnp.ones((16, OBS), BF16)], axis=0)


def observation_sums(values, low, high, row):
    cell = lax.broadcasted_iota(jnp.int32, (LON, OBS), 0)
    hit = jnp.where((low == cell) & (high == row), 1.0, 0.0).astype(BF16)
    return lax.dot_general(
        values, hit, (((1,), (1,)), ((), ())), preferred_element_type=F32
    )


def innovation_of(sums, own):
    return sums[C : C + 1, :] * own - sums[:C, :]


def pack_kernel(
    x_hbm, obs_hbm, index_hbm, bg_hbm, taps_hbm, out_weight_hbm, bias_hbm, own_ref, bg_rows_ref,
    first_ref, second_ref, obs_ref, index_ref, taps_ref, out_weight_ref, bias_ref, x_ref, bg_ref,
    xs, bs, sems,
):
    copies = [
        pltpu.make_async_copy(source, target, sems.at[place])
        for place, (source, target) in enumerate(
            (
                (x_hbm, x_ref), (obs_hbm, obs_ref), (index_hbm, index_ref), (bg_hbm, bg_ref),
                (taps_hbm, taps_ref), (out_weight_hbm, out_weight_ref), (bias_hbm, bias_ref),
            )
        )
    ]
    for copy in copies:
        copy.start()
    copies[0].wait()
    even = lax.rem(lax.axis_index("lat"), 2) == 0

    def send(place, up, down):
        at = slice(place * C, (place + 1) * C)
        first_ref[at, :] = jnp.where(even, down, up).astype(BF16)
        second_ref[at, :] = jnp.where(even, up, down).astype(BF16)

    xs[...] = x_ref[...].astype(F32).reshape(ROWS * C, LON)
    for row in range(4):
        up, down = xs[latitude(row), :], xs[latitude(row + 4), :]
        own_ref[row * C : (row + 1) * C, :] = up.astype(BF16)
        own_ref[(row + 4) * C : (row + 5) * C, :] = down.astype(BF16)
        send(row, up, down)
    copies[1].wait()
    copies[2].wait()
    low, high = local_cells(index_ref[...])
    values = with_ones(obs_ref[...])
    copies[3].wait()
    bs[...] = bg_ref[...].astype(F32).reshape(ROWS * C, LON)
    opening = lax.axis_index("tm") == 0

    def edge(row):
        own = xs[latitude(row), :]
        ground = bs[latitude(row), :]
        value = innovation_of(observation_sums(values, low, high, row), own)
        return value + jnp.where(opening, own - ground, 0.0)

    for row in range(2):
        send(4 + row, edge(row), edge(row + 6))
    for row in range(ROWS):
        bg_rows_ref[row * C : (row + 1) * C, :] = bs[latitude(row), :].astype(BF16)
    for copy in copies[4:]:
        copy.wait()


def extend_kernel(
    own_ref, first_ref, second_ref, ext_ref, near_ref, far_ref, above_edge_ref, below_edge_ref
):
    strip = lax.axis_index("lat")
    even = lax.rem(strip, 2) == 0
    zero = jnp.zeros((X_PART, LON), BF16)
    above = jnp.where(even, second_ref[...], first_ref[...])
    below = jnp.where(even, first_ref[...], second_ref[...])
    above_edge_ref[...] = above[X_PART:, :]
    below_edge_ref[...] = below[X_PART:, :]
    above = jnp.where(strip > 0, above[:X_PART, :], zero)
    below = jnp.where(strip < lax.axis_size("lat") - 1, below[:X_PART, :], zero)
    far_ref[: 3 * C, :] = above[C:, :]
    far_ref[3 * C :, :] = below[: 3 * C, :]
    near_ref[: 3 * C, :] = above[C:, :]
    near_ref[3 * C : 11 * C, :] = own_ref[...]
    near_ref[11 * C :, :] = below[: 3 * C, :]
    ext_ref[:X_PART, :] = above
    ext_ref[X_PART : X_PART + ROWS * C, :] = own_ref[...]
    ext_ref[X_PART + ROWS * C :, :] = below


def turn(value, b):
    return value if b == 1 else pltpu.roll(value, 1 if b == 0 else LON - 1, 1)


def actives(work, rows, conv_ref, bias_ref, mixed):
    for place, pair in enumerate(pair for group in work for pair in group):
        d = [at(rows, pair[0] + a).astype(F32) for a in range(4)]
        for j, value in enumerate((d[0] - d[2], d[1] + d[2], d[2] - d[1], d[1] - d[3])):
            for b in range(3):
                start = (3 * place + b) * C
                mixed[j, start : start + C, :] = turn(value, b).astype(BF16)
    place = 0
    for group in work:
        bias = jnp.concatenate([bias_ref[...]] * len(group), axis=1)
        spans = [slice(3 * C * (place + n), 3 * C * (place + n + 1)) for n in range(len(group))]
        place += len(group)
        m = [
            jnp.dot(
                conv_ref[j * HID : (j + 1) * HID, :],
                jnp.concatenate([mixed[j, span, :] for span in spans], axis=1),
                preferred_element_type=F32,
            )
            for j in range(4)
        ]
        upper, lower = zip(*group)
        yield upper, jnp.tanh(m[0] + m[1] + m[2] + bias).astype(BF16)
        yield lower, jnp.tanh(m[1] - m[2] - m[3] + bias).astype(BF16)


def rows_of_work(work):
    return sorted(row for group in work for pair in group for row in pair)


def lanes_of(half):
    return slice(half * LON, (half + 1) * LON)


def store_pair(ref, first, value, width=C):
    ref[first * width : (first + 1) * width, :] = value[:, :LON]
    ref[(first + 1) * width : (first + 2) * width, :] = value[:, LON:]


def forward_kernel(
    work, state_ref, conv_ref, bias_ref, out_weight_ref, active_ref, forecast_ref, mixed
):
    rows = rows_in(state_ref, 0, state_ref.shape[0] // C)
    order = {row: place for place, row in enumerate(rows_of_work(work))}
    for some, active in actives(work, rows, conv_ref, bias_ref, mixed):
        step = jnp.dot(out_weight_ref[...], active, preferred_element_type=F32)
        centre = beside(rows, *(row + 1 for row in some)).astype(F32)
        forecast = (centre + step).astype(BF16)
        for half, row in enumerate(some):
            place = order[row]
            active_ref[place * HID : (place + 1) * HID, :] = active[:, lanes_of(half)]
            forecast_ref[place * C : (place + 1) * C, :] = forecast[:, lanes_of(half)]


def prepare_kernel(
    obs_ref, index_ref, kernel_ref, bias_ref, out_weight_ref, sums_ref, conv_ref, back_ref,
    wide_bias_ref, out_back_ref,
):
    low, high = local_cells(index_ref[...])
    values = with_ones(obs_ref[...])
    for row in range(ROWS):
        sums_ref[row] = observation_sums(values, low, high, row)[:72, :]
    g = [kernel_ref[a * 3 * C : (a + 1) * 3 * C, :].astype(F32) for a in range(3)]
    ends = g[0] + g[2]
    for j, value in enumerate((g[0], 0.5 * (ends + g[1]), 0.5 * (ends - g[1]), g[2])):
        conv_ref[j * HID : (j + 1) * HID, :] = value.astype(BF16).T
    out_back_ref[...] = out_weight_ref[...].T
    wide_bias_ref[...] = jnp.broadcast_to(bias_ref[...], (LON, HID)).T
    for a in range(3):
        back_ref[:, a * HID : (a + 1) * HID] = kernel_ref[(2 - a) * 3 * C : (3 - a) * 3 * C, :]


def residual_part(
    work, prev, own_ref, conv_ref, bias_ref, out_weight_ref, mixed, take
):
    own_rows = rows_in(own_ref, 2, max(rows_of_work(work)) + 1)
    for some, active in actives(work, prev, conv_ref, bias_ref, mixed):
        step = jnp.dot(out_weight_ref[...], active, preferred_element_type=F32)
        centre = beside(prev, *(row + 1 for row in some)).astype(F32)
        guess = (centre + step).astype(BF16).astype(F32)
        resid = (beside(own_rows, *some).astype(F32) - guess).astype(BF16)
        for half, row in enumerate(some):
            take(row, resid[:, lanes_of(half)])


def strip_ends():
    strip = lax.axis_index("lat")
    return -strip * ROWS, (lax.axis_size("lat") - strip) * ROWS


def adjoint_part(
    count, margin, later, active, forecast, back_ref, out_back_ref, cot, target, take
):
    top, bottom = strip_ends()
    for row in range(0, count + 2, 2):
        resid = beside(later, row, row + 1).astype(F32) - beside(forecast, row, row + 1).astype(F32)
        resid = resid.astype(BF16)
        store_pair(target, row, resid)
        projected = jnp.dot(out_back_ref[...], resid, preferred_element_type=F32)
        for half in range(2):
            place = row + half - margin - 1
            value = at(active, row + half, HID).astype(F32)
            value = (1.0 - value * value) * projected[:, half * LON : (half + 1) * LON]
            if not 0 <= place < ROWS:
                value = jnp.where((place >= top) & (place < bottom), value, 0.0)
            cot[(row + half) * HID : (row + half + 1) * HID, :] = value.astype(BF16)
    closing = lax.axis_index("tm") == lax.axis_size("tm") - 1
    for row in range(0, count, 2):
        cells = jnp.concatenate(
            [cot[row * HID : (row + 3) * HID, :], cot[(row + 1) * HID : (row + 4) * HID, :]], axis=1
        )
        spread = jnp.dot(back_ref[...], cells, preferred_element_type=F32)
        for half in range(2):
            lanes = slice(half * LON, (half + 1) * LON)
            pulled = (
                pltpu.roll(spread[:C, lanes], LON - 1, 1)
                + spread[C : 2 * C, lanes]
                + pltpu.roll(spread[2 * C :, lanes], 1, 1)
            )
            resid = rows_of(target, row + half + 1).astype(F32)
            take(row + half, jnp.where(closing, 0.0, resid + pulled).astype(BF16))


def branches():
    window = lax.axis_index("tm")
    even = lax.rem(window, 2) == 0
    opening = window == 0
    return even & jnp.logical_not(opening), opening, jnp.logical_not(even)


def quads_of(count):
    return tuple(((row, row + 1), (row + 2, row + 3)) for row in range(0, count - 3, 4))


INSIDE = (((0, 1), (2, 3)), ((4, 5),))
OUTSIDE = (((0, 1), (2, 3)), ((10, 11), (12, 13)))
INNER = (((4, 5), (6, 7)),)
OUTER = (((0, 1), (2, 3)), ((8, 9), (10, 11)))
TWELVE = quads_of(12)
TEN = quads_of(8) + (((8, 9),),)
EIGHT = quads_of(8)


def first_near_kernel(
    near_ref, far_own_ref, own_ref, active_in_ref, forecast_in_ref, active_out_ref, forecast_out_ref,
    conv_ref, bias_ref, out_weight_ref, back_ref, out_back_ref, part_ref, inner_ref, mixed,
    cot, target,
):
    def put(ref):
        def take(row, value):
            ref[row * C : (row + 1) * C, :] = value

        return take

    even, _, odd = branches()

    @pl.when(jnp.logical_not(odd))
    def _():
        adjoint_part(
            12, 2, rows_in(near_ref, 0, 14), split_rows(active_out_ref, active_in_ref),
            split_rows(forecast_out_ref, forecast_in_ref), back_ref, out_back_ref, cot, target,
            put(part_ref),
        )

    @pl.when(even)
    def _():
        prev = [None] * 3 + rows_in(far_own_ref, 0, ROWS)
        residual_part(
            INNER, prev, own_ref, conv_ref, bias_ref, out_weight_ref,
            mixed, put(inner_ref)
        )

    @pl.when(odd)
    def _():
        residual_part(
            TWELVE, rows_in(near_ref, 0, 14), own_ref, conv_ref, bias_ref, out_weight_ref,
            mixed, put(part_ref),
        )


def split_rows(outside_ref, inside_ref):
    return rows_in(outside_ref, 0, 4) + rows_in(inside_ref, 0, 6) + rows_in(outside_ref, 4, 4)


def first_kernel(
    far_ref, far_own_ref, part_ref, inner_ref, own_ref, bg_ref, active_in_ref, forecast_in_ref,
    active_out_ref, forecast_out_ref, conv_ref, bias_ref, out_weight_ref, back_ref, out_back_ref,
    sums_ref, above_ref, below_ref, state_ref, sent_ref, mixed, cot, target,
):
    top, bottom = strip_ends()

    def step(row, resid, adjoint):
        own = rows_of(own_ref, row + 2).astype(F32)
        place = row - 2
        if place < 0:
            innovation = rows_of(above_ref, row).astype(F32)
        elif place >= ROWS:
            innovation = rows_of(below_ref, place - ROWS).astype(F32)
        else:
            innovation = innovation_of(sums_ref[place], own)
        value = own - STEP * (resid.astype(F32) - adjoint.astype(F32) + innovation)
        if not 0 <= place < ROWS:
            value = jnp.where((place >= top) & (place < bottom), value, 0.0)
        value = value.astype(BF16)
        state_ref[row * C : (row + 1) * C, :] = value
        if 1 <= row < 11:
            sent_ref[(row - 1) * C : row * C, :] = value

    even, opening, odd = branches()
    far = rows_in(far_ref, 0, 3) + rows_in(far_own_ref, 0, ROWS) + rows_in(far_ref, 3, 3)

    @pl.when(even)
    def _():
        residual_part(
            OUTER, far, own_ref, conv_ref, bias_ref, out_weight_ref,
            mixed, lambda row, resid: step(row, resid, rows_of(part_ref, row)),
        )
        for row in range(4, 8):
            step(row, rows_of(inner_ref, row), rows_of(part_ref, row))

    @pl.when(opening)
    def _():
        for row in range(12):
            place = row - 2
            resid = jnp.zeros((C, LON), BF16)
            if 0 <= place < ROWS:
                own = rows_of(own_ref, row + 2).astype(F32)
                resid = (own - rows_of(bg_ref, place).astype(F32)).astype(BF16)
            step(row, resid, rows_of(part_ref, row))

    @pl.when(odd)
    def _():
        adjoint_part(
            12, 2, far, split_rows(active_out_ref, active_in_ref),
            split_rows(forecast_out_ref, forecast_in_ref), back_ref, out_back_ref, cot, target,
            lambda row, adjoint: step(row, rows_of(part_ref, row), adjoint),
        )


def second_near_kernel(
    near_ref, own_ref, active_ref, forecast_ref, conv_ref, bias_ref, out_weight_ref,
    back_ref, out_back_ref, part_ref, mixed, cot, target,
):
    def take(row, value):
        part_ref[row * C : (row + 1) * C, :] = value

    _, _, odd = branches()
    near = rows_in(near_ref, 0, 10)

    @pl.when(jnp.logical_not(odd))
    def _():
        adjoint_part(
            8, 0, near, rows_in(active_ref, 0, 10), rows_in(forecast_ref, 0, 10), back_ref,
            out_back_ref, cot, target, take,
        )

    @pl.when(odd)
    def _():
        residual_part(
            EIGHT, near, own_ref, conv_ref, bias_ref, out_weight_ref,
            mixed, take
        )


def second_kernel(
    far_ref, part_ref, own_ref, bg_ref, active_ref, forecast_ref, conv_ref, bias_ref,
    out_weight_ref, back_ref, out_back_ref, sums_ref, out_ref, mixed, cot, target, wide,
):
    def step(row, resid, adjoint):
        own = rows_of(own_ref, row + 2).astype(F32)
        innovation = innovation_of(sums_ref[row], own)
        value = own - STEP * (resid.astype(F32) - adjoint.astype(F32) + innovation)
        wide[latitude(row), :] = value

    even, opening, odd = branches()
    far = rows_in(far_ref, 0, 10)

    @pl.when(even)
    def _():
        residual_part(
            EIGHT, far, own_ref, conv_ref, bias_ref, out_weight_ref,
            mixed, lambda row, resid: step(row, resid, rows_of(part_ref, row)),
        )

    @pl.when(opening)
    def _():
        for row in range(ROWS):
            own = rows_of(own_ref, row + 2).astype(F32)
            resid = (own - rows_of(bg_ref, row).astype(F32)).astype(BF16)
            step(row, resid, rows_of(part_ref, row))

    @pl.when(odd)
    def _():
        adjoint_part(
            8, 0, far, rows_in(active_ref, 0, 10), rows_in(forecast_ref, 0, 10), back_ref,
            out_back_ref, cot, target, lambda row, adjoint: step(row, rows_of(part_ref, row), adjoint),
        )

    out_ref[...] = wide[...].reshape(C, ROWS, LON).astype(BF16)


def exchange(value, partner):
    windows, strips = lax.axis_size("tm"), lax.axis_size("lat")
    pairs = []
    for window in range(windows):
        for strip in range(strips):
            to_window, to_strip = partner(window, strip, windows - 1, strips - 1)
            pairs.append((window * strips + strip, to_window * strips + to_strip))
    return lax.ppermute(value, ("tm", "lat"), pairs)


def near_strip(window, strip, last_window, last_strip):
    return window, strip ^ 1


def far_strip(window, strip, last_window, last_strip):
    if strip in (0, last_strip):
        return window ^ 1, strip
    return window, ((strip + 1) ^ 1) - 1


def near_window(window, strip, last_window, last_strip):
    return window ^ 1, strip


def far_window(window, strip, last_window, last_strip):
    if window in (0, last_window):
        return window, strip ^ 2
    return ((window + 1) ^ 1) - 1, strip


def shape(rows, dtype=BF16):
    return jax.ShapeDtypeStruct((rows, LON), dtype)


def conv_scratch(count):
    return [
        pltpu.VMEM((4, (count // 2) * 3 * C, LON), BF16),
    ]


def gradient_scratch(count):
    return conv_scratch(count) + [
        pltpu.VMEM(((count + 2) * HID, LON), BF16),
        pltpu.VMEM(((count + 2) * C, LON), BF16),
    ]


def row_flops(rows):
    return rows * 2 * LON * HID * 10 * C


def on_device(
    window_snapshots, background, obs_values, obs_index, input_kernel_weight, hidden_bias_vector,
    output_pointwise_weight,
):
    def forward(work, state):
        count = len(rows_of_work(work))
        return call(
            functools.partial(forward_kernel, work),
            (shape(count * HID), shape(count * C)),
            conv_scratch(state.shape[0] // C - 2),
            row_flops(count), 2 << 20,
        )(state, conv_weight, bias, out_weight)

    taps = jnp.transpose(input_kernel_weight, (0, 1, 3, 2)).reshape(9 * C, HID)
    own, ground, first, second, observed, index, taps, out_weight, bias = call(
        pack_kernel,
        (
            shape(ROWS * C), shape(ROWS * C), shape(PAYLOAD), shape(PAYLOAD),
            jax.ShapeDtypeStruct((C, OBS), BF16),
            jax.ShapeDtypeStruct((1, OBS), jnp.int32),
            jax.ShapeDtypeStruct((9 * C, HID), BF16),
            jax.ShapeDtypeStruct((C, HID), BF16),
            jax.ShapeDtypeStruct((1, HID), F32),
        ),
        [
            pltpu.VMEM((C, ROWS, LON), BF16),
            pltpu.VMEM((C, ROWS, LON), BF16),
            pltpu.VMEM((C * ROWS, LON), F32),
            pltpu.VMEM((C * ROWS, LON), F32),
            pltpu.SemaphoreType.DMA((7,)),
        ],
        0, 1 << 20, pl.BlockSpec(memory_space=pltpu.HBM),
    )(
        *(
            pltpu.with_memory_space_constraint(value, pltpu.HBM)
            for value in (
                window_snapshots[0], obs_values[0], obs_index, background, taps,
                output_pointwise_weight, hidden_bias_vector[None, :],
            )
        )
    )
    second = exchange(second, far_strip)
    first = exchange(first, near_strip)
    far_own = exchange(own, far_window)

    sums, conv_weight, back_weight, bias, out_back = call(
        prepare_kernel,
        (
            jax.ShapeDtypeStruct((ROWS, 72, LON), F32),
            jax.ShapeDtypeStruct((4 * HID, 3 * C), BF16),
            jax.ShapeDtypeStruct((3 * C, 3 * HID), BF16),
            jax.ShapeDtypeStruct((HID, LON), F32),
            jax.ShapeDtypeStruct((HID, C), BF16),
        ),
        [], ROWS * 2 * 80 * OBS * LON, 1 << 20,
    )(observed, index, taps, bias, out_weight)
    weights = (conv_weight, bias, out_weight, back_weight, out_back)
    inside = forward(INSIDE, own)
    first, second, inside, sums = lax.optimization_barrier((first, second, inside, sums))

    ext, sent, halo, above_edge, below_edge = call(
        extend_kernel,
        (shape(16 * C), shape(14 * C), shape(6 * C), shape(2 * C), shape(2 * C)),
        [], 0, 1 << 20,
    )(own, first, second)
    far = exchange(halo, far_window)
    near = exchange(sent, near_window)
    outside = forward(OUTSIDE, ext)
    part, inner = call(
        first_near_kernel, (shape(12 * C), shape(12 * C)), gradient_scratch(12),
        row_flops(12), 2 << 20,
    )(near, far_own, ext, *inside, *outside, *weights)
    state, sent = call(
        first_kernel, (shape(12 * C), shape(10 * C)), gradient_scratch(12), row_flops(12),
        2 << 20,
    )(
        far, far_own, part, inner, ext, ground, *inside, *outside, *weights, sums,
        above_edge, below_edge,
    )
    far = exchange(sent, far_window)
    near = exchange(sent, near_window)
    given = (state, ground, *forward(TEN, state), *weights)
    part = call(
        second_near_kernel, shape(8 * C), gradient_scratch(8), row_flops(8), 2 << 20
    )(near, state, *given[2:])
    analysis = call(
        second_kernel,
        jax.ShapeDtypeStruct((C, ROWS, LON), BF16),
        gradient_scratch(8) + [pltpu.VMEM((C * ROWS, LON), F32)],
        row_flops(8), 2 << 20,
    )(far, part, *given, sums)
    return analysis[None]


def solution(mesh):
    placed = (
        P("tm", None, "lat", None),
        P(None, "lat", None),
        P("tm", None, "lat"),
        P("tm", "lat"),
        P(),
        P(),
        P(),
    )
    return jax.shard_map(
        on_device, mesh=mesh, in_specs=placed, out_specs=P("tm", None, "lat", None), check_vma=False
    )
```

```python
import functools

import jax
import jax.numpy as jnp
from jax import lax
from jax.experimental import pallas as pl
from jax.experimental.pallas import tpu as pltpu
from jax.sharding import PartitionSpec as P


C = 64
HID = 256
ROWS = 8
LON = 128
OBS = 256
STEP = 0.3

F32 = jnp.float32
BF16 = jnp.bfloat16
VMEM = pl.BlockSpec(memory_space=pltpu.VMEM)

X_PART = 4 * C
PAYLOAD = X_PART + 2 * C


def call(kernel, outs, scratch, flops, bytes_accessed, spec=VMEM, grant=48 << 20):
    def run(*args):
        return pl.pallas_call(
            kernel,
            out_shape=outs,
            in_specs=[spec] * len(args),
            out_specs=jax.tree.map(lambda _: VMEM, outs),
            scratch_shapes=scratch,
            cost_estimate=pl.CostEstimate(
                flops=flops, bytes_accessed=bytes_accessed, transcendentals=0
            ),
            compiler_params=pltpu.CompilerParams(vmem_limit_bytes=grant),
        )(*args)

    return run


def rows_of(ref, first, width=C):
    return ref[first * width : (first + 1) * width, :]


def rows_in(ref, first, count):
    return [(ref, row) for row in range(first, first + count)]


def at(rows, place, width=C):
    ref, row = rows[place]
    return rows_of(ref, row, width)


def beside(rows, *places):
    return jnp.concatenate([at(rows, place) for place in places], axis=1)


def latitude(row):
    return pl.ds(row, C, stride=ROWS)


def local_cells(index):
    local = index - lax.axis_index("lat") * (ROWS * LON)
    high = lax.shift_right_arithmetic(local, 7)
    return local - high * LON, high


def with_ones(values):
    return jnp.concatenate([values, jnp.ones((16, OBS), BF16)], axis=0)


def observation_sums(values, low, high, row):
    cell = lax.broadcasted_iota(jnp.int32, (LON, OBS), 0)
    hit = jnp.where((low == cell) & (high == row), 1.0, 0.0).astype(BF16)
    return lax.dot_general(
        values, hit, (((1,), (1,)), ((), ())), preferred_element_type=F32
    )


def innovation_of(sums, own):
    return sums[C : C + 1, :] * own - sums[:C, :]


def pack_kernel(
    x_hbm, obs_hbm, index_hbm, bg_hbm, taps_hbm, out_weight_hbm, bias_hbm, first_ref, second_ref,
    x_ref, bg_ref, obs_ref, index_ref, taps_ref, out_weight_ref, bias_ref, xs, bs, sems,
):
    copies = [
        pltpu.make_async_copy(source, target, sems.at[place])
        for place, (source, target) in enumerate(
            (
                (x_hbm, x_ref), (obs_hbm, obs_ref), (index_hbm, index_ref), (bg_hbm, bg_ref),
                (taps_hbm, taps_ref), (out_weight_hbm, out_weight_ref), (bias_hbm, bias_ref),
            )
        )
    ]
    for copy in copies:
        copy.start()
    copies[1].wait()
    copies[2].wait()
    low, high = local_cells(index_ref[...])
    values = with_ones(obs_ref[...])
    sums = {row: observation_sums(values, low, high, row) for row in (0, 1, 6, 7)}
    even = lax.rem(lax.axis_index("lat"), 2) == 0

    def send(place, up, down):
        at = slice(place * C, (place + 1) * C)
        first_ref[at, :] = jnp.where(even, down, up).astype(BF16)
        second_ref[at, :] = jnp.where(even, up, down).astype(BF16)

    copies[0].wait()
    xs[...] = x_ref[...].astype(F32).reshape(ROWS * C, LON)
    for row in range(4):
        send(row, xs[latitude(row), :], xs[latitude(row + 4), :])
    copies[3].wait()
    bs[...] = bg_ref[...].astype(F32).reshape(ROWS * C, LON)
    opening = lax.axis_index("tm") == 0

    def edge(row):
        own = xs[latitude(row), :]
        value = innovation_of(sums[row], own)
        return value + jnp.where(opening, own - bs[latitude(row), :], 0.0)

    for row in range(2):
        send(4 + row, edge(row), edge(row + 6))
    for copy in copies[4:]:
        copy.wait()


def extend_kernel(
    own_ref, first_ref, second_ref, ext_ref, halo_ref, above_edge_ref, below_edge_ref
):
    strip = lax.axis_index("lat")
    even = lax.rem(strip, 2) == 0
    zero = jnp.zeros((X_PART, LON), BF16)
    above = jnp.where(even, second_ref[...], first_ref[...])
    below = jnp.where(even, first_ref[...], second_ref[...])
    above_edge_ref[...] = above[X_PART:, :]
    below_edge_ref[...] = below[X_PART:, :]
    above = jnp.where(strip > 0, above[:X_PART, :], zero)
    below = jnp.where(strip < lax.axis_size("lat") - 1, below[:X_PART, :], zero)
    halo_ref[: 3 * C, :] = above[C:, :]
    halo_ref[3 * C :, :] = below[: 3 * C, :]
    ext_ref[:X_PART, :] = above
    ext_ref[X_PART : X_PART + ROWS * C, :] = own_ref[...]
    ext_ref[X_PART + ROWS * C :, :] = below


def turn(value, b):
    return value if b == 1 else pltpu.roll(value, 1 if b == 0 else LON - 1, 1)


def actives(work, rows, conv_ref, bias_ref, mixed):
    for place, pair in enumerate(pair for group in work for pair in group):
        d = [at(rows, pair[0] + a).astype(F32) for a in range(4)]
        for j, value in enumerate((d[0] - d[2], d[1] + d[2], d[2] - d[1], d[1] - d[3])):
            for b in range(3):
                start = (3 * place + b) * C
                mixed[j, start : start + C, :] = turn(value, b).astype(BF16)
    place = 0
    for group in work:
        bias = jnp.concatenate([bias_ref[...]] * len(group), axis=1)
        spans = [slice(3 * C * (place + n), 3 * C * (place + n + 1)) for n in range(len(group))]
        place += len(group)
        m = [
            jnp.dot(
                conv_ref[j * HID : (j + 1) * HID, :],
                jnp.concatenate([mixed[j, span, :] for span in spans], axis=1),
                preferred_element_type=F32,
            )
            for j in range(4)
        ]
        upper, lower = zip(*group)
        yield upper, jnp.tanh(m[0] + m[1] + m[2] + bias).astype(BF16)
        yield lower, jnp.tanh(m[1] - m[2] - m[3] + bias).astype(BF16)


def rows_of_work(work):
    return sorted(row for group in work for pair in group for row in pair)


def lanes_of(half):
    return slice(half * LON, (half + 1) * LON)


def store_pair(ref, first, value, width=C):
    ref[first * width : (first + 1) * width, :] = value[:, :LON]
    ref[(first + 1) * width : (first + 2) * width, :] = value[:, LON:]


def forward_kernel(
    work, state_ref, conv_ref, bias_ref, out_weight_ref, active_ref, forecast_ref, mixed
):
    rows = rows_in(state_ref, 0, state_ref.shape[0] // C)
    order = {row: place for place, row in enumerate(rows_of_work(work))}
    for some, active in actives(work, rows, conv_ref, bias_ref, mixed):
        step = jnp.dot(out_weight_ref[...], active, preferred_element_type=F32)
        centre = beside(rows, *(row + 1 for row in some)).astype(F32)
        forecast = (centre + step).astype(BF16)
        for half, row in enumerate(some):
            place = order[row]
            active_ref[place * HID : (place + 1) * HID, :] = active[:, lanes_of(half)]
            forecast_ref[place * C : (place + 1) * C, :] = forecast[:, lanes_of(half)]


def prepare_kernel(
    x_ref, bg_ref, obs_ref, index_ref, kernel_ref, bias_ref, out_weight_ref, own_ref, bg_rows_ref,
    sums_ref, conv_ref, back_ref, wide_bias_ref, out_back_ref, xs, bs,
):
    xs[...] = x_ref[...].astype(F32).reshape(ROWS * C, LON)
    bs[...] = bg_ref[...].astype(F32).reshape(ROWS * C, LON)
    for row in range(ROWS):
        own_ref[row * C : (row + 1) * C, :] = xs[latitude(row), :].astype(BF16)
        bg_rows_ref[row * C : (row + 1) * C, :] = bs[latitude(row), :].astype(BF16)
    low, high = local_cells(index_ref[...])
    values = with_ones(obs_ref[...])
    for row in range(ROWS):
        sums_ref[row] = observation_sums(values, low, high, row)[:72, :]
    g = [kernel_ref[a * 3 * C : (a + 1) * 3 * C, :].astype(F32) for a in range(3)]
    ends = g[0] + g[2]
    for j, value in enumerate((g[0], 0.5 * (ends + g[1]), 0.5 * (ends - g[1]), g[2])):
        conv_ref[j * HID : (j + 1) * HID, :] = value.astype(BF16).T
    out_back_ref[...] = out_weight_ref[...].T
    wide_bias_ref[...] = jnp.broadcast_to(bias_ref[...], (LON, HID)).T
    for a in range(3):
        back_ref[:, a * HID : (a + 1) * HID] = kernel_ref[(2 - a) * 3 * C : (3 - a) * 3 * C, :]


def residual_part(
    work, prev, own_ref, conv_ref, bias_ref, out_weight_ref, mixed, take
):
    own_rows = rows_in(own_ref, 2, max(rows_of_work(work)) + 1)
    for some, active in actives(work, prev, conv_ref, bias_ref, mixed):
        step = jnp.dot(out_weight_ref[...], active, preferred_element_type=F32)
        centre = beside(prev, *(row + 1 for row in some)).astype(F32)
        guess = (centre + step).astype(BF16).astype(F32)
        resid = (beside(own_rows, *some).astype(F32) - guess).astype(BF16)
        for half, row in enumerate(some):
            take(row, resid[:, lanes_of(half)])


def strip_ends():
    strip = lax.axis_index("lat")
    return -strip * ROWS, (lax.axis_size("lat") - strip) * ROWS


def adjoint_part(
    count, margin, later, active, forecast, back_ref, out_back_ref, cot, target, take
):
    top, bottom = strip_ends()
    for row in range(0, count + 2, 2):
        resid = beside(later, row, row + 1).astype(F32) - beside(forecast, row, row + 1).astype(F32)
        resid = resid.astype(BF16)
        store_pair(target, row, resid)
        projected = jnp.dot(out_back_ref[...], resid, preferred_element_type=F32)
        for half in range(2):
            place = row + half - margin - 1
            value = at(active, row + half, HID).astype(F32)
            value = (1.0 - value * value) * projected[:, half * LON : (half + 1) * LON]
            if not 0 <= place < ROWS:
                value = jnp.where((place >= top) & (place < bottom), value, 0.0)
            cot[(row + half) * HID : (row + half + 1) * HID, :] = value.astype(BF16)
    closing = lax.axis_index("tm") == lax.axis_size("tm") - 1
    for row in range(0, count, 2):
        cells = jnp.concatenate(
            [cot[row * HID : (row + 3) * HID, :], cot[(row + 1) * HID : (row + 4) * HID, :]], axis=1
        )
        spread = jnp.dot(back_ref[...], cells, preferred_element_type=F32)
        for half in range(2):
            lanes = slice(half * LON, (half + 1) * LON)
            pulled = (
                pltpu.roll(spread[:C, lanes], LON - 1, 1)
                + spread[C : 2 * C, lanes]
                + pltpu.roll(spread[2 * C :, lanes], 1, 1)
            )
            resid = rows_of(target, row + half + 1).astype(F32)
            take(row + half, jnp.where(closing, 0.0, resid + pulled).astype(BF16))


def branches():
    window = lax.axis_index("tm")
    even = lax.rem(window, 2) == 0
    opening = window == 0
    return even & jnp.logical_not(opening), opening, jnp.logical_not(even)


def quads_of(count):
    return tuple(((row, row + 1), (row + 2, row + 3)) for row in range(0, count - 3, 4))


INSIDE = (((0, 1), (2, 3)), ((4, 5),))
OUTSIDE = (((0, 1), (2, 3)), ((10, 11), (12, 13)))
INNER = (((4, 5), (6, 7)),)
OUTER = (((0, 1), (2, 3)), ((8, 9), (10, 11)))
TWELVE = quads_of(12)
TEN = quads_of(8) + (((8, 9),),)
EIGHT = quads_of(8)


def first_near_kernel(
    near_ref, near_own_ref, far_own_ref, own_ref, active_in_ref, forecast_in_ref, active_out_ref, forecast_out_ref,
    conv_ref, bias_ref, out_weight_ref, back_ref, out_back_ref, part_ref, inner_ref, mixed,
    cot, target,
):
    def put(ref):
        def take(row, value):
            ref[row * C : (row + 1) * C, :] = value

        return take

    even, _, odd = branches()
    near = rows_in(near_ref, 0, 3) + rows_in(near_own_ref, 0, ROWS) + rows_in(near_ref, 3, 3)

    @pl.when(jnp.logical_not(odd))
    def _():
        adjoint_part(
            12, 2, near, split_rows(active_out_ref, active_in_ref),
            split_rows(forecast_out_ref, forecast_in_ref), back_ref, out_back_ref, cot, target,
            put(part_ref),
        )

    @pl.when(even)
    def _():
        prev = [None] * 3 + rows_in(far_own_ref, 0, ROWS)
        residual_part(
            INNER, prev, own_ref, conv_ref, bias_ref, out_weight_ref,
            mixed, put(inner_ref)
        )

    @pl.when(odd)
    def _():
        residual_part(
            TWELVE, near, own_ref, conv_ref, bias_ref, out_weight_ref,
            mixed, put(part_ref),
        )


def split_rows(outside_ref, inside_ref):
    return rows_in(outside_ref, 0, 4) + rows_in(inside_ref, 0, 6) + rows_in(outside_ref, 4, 4)


def first_kernel(
    far_ref, far_own_ref, part_ref, inner_ref, own_ref, bg_ref, active_in_ref, forecast_in_ref,
    active_out_ref, forecast_out_ref, conv_ref, bias_ref, out_weight_ref, back_ref, out_back_ref,
    sums_ref, above_ref, below_ref, state_ref, sent_ref, mixed, cot, target,
):
    top, bottom = strip_ends()

    def step(row, resid, adjoint):
        own = rows_of(own_ref, row + 2).astype(F32)
        place = row - 2
        if place < 0:
            innovation = rows_of(above_ref, row).astype(F32)
        elif place >= ROWS:
            innovation = rows_of(below_ref, place - ROWS).astype(F32)
        else:
            innovation = innovation_of(sums_ref[place], own)
        value = own - STEP * (resid.astype(F32) - adjoint.astype(F32) + innovation)
        if not 0 <= place < ROWS:
            value = jnp.where((place >= top) & (place < bottom), value, 0.0)
        value = value.astype(BF16)
        state_ref[row * C : (row + 1) * C, :] = value
        if 1 <= row < 11:
            sent_ref[(row - 1) * C : row * C, :] = value

    even, opening, odd = branches()
    far = rows_in(far_ref, 0, 3) + rows_in(far_own_ref, 0, ROWS) + rows_in(far_ref, 3, 3)

    @pl.when(even)
    def _():
        residual_part(
            OUTER, far, own_ref, conv_ref, bias_ref, out_weight_ref,
            mixed, lambda row, resid: step(row, resid, rows_of(part_ref, row)),
        )
        for row in range(4, 8):
            step(row, rows_of(inner_ref, row), rows_of(part_ref, row))

    @pl.when(opening)
    def _():
        for row in range(12):
            place = row - 2
            resid = jnp.zeros((C, LON), BF16)
            if 0 <= place < ROWS:
                own = rows_of(own_ref, row + 2).astype(F32)
                resid = (own - rows_of(bg_ref, place).astype(F32)).astype(BF16)
            step(row, resid, rows_of(part_ref, row))

    @pl.when(odd)
    def _():
        adjoint_part(
            12, 2, far, split_rows(active_out_ref, active_in_ref),
            split_rows(forecast_out_ref, forecast_in_ref), back_ref, out_back_ref, cot, target,
            lambda row, adjoint: step(row, rows_of(part_ref, row), adjoint),
        )


def second_near_kernel(
    near_ref, own_ref, active_ref, forecast_ref, conv_ref, bias_ref, out_weight_ref,
    back_ref, out_back_ref, part_ref, mixed, cot, target,
):
    def take(row, value):
        part_ref[row * C : (row + 1) * C, :] = value

    _, _, odd = branches()
    near = rows_in(near_ref, 0, 10)

    @pl.when(jnp.logical_not(odd))
    def _():
        adjoint_part(
            8, 0, near, rows_in(active_ref, 0, 10), rows_in(forecast_ref, 0, 10), back_ref,
            out_back_ref, cot, target, take,
        )

    @pl.when(odd)
    def _():
        residual_part(
            EIGHT, near, own_ref, conv_ref, bias_ref, out_weight_ref,
            mixed, take
        )


def second_kernel(
    far_ref, part_ref, own_ref, bg_ref, active_ref, forecast_ref, conv_ref, bias_ref,
    out_weight_ref, back_ref, out_back_ref, sums_ref, out_ref, mixed, cot, target, wide,
):
    def step(row, resid, adjoint):
        own = rows_of(own_ref, row + 2).astype(F32)
        innovation = innovation_of(sums_ref[row], own)
        value = own - STEP * (resid.astype(F32) - adjoint.astype(F32) + innovation)
        wide[latitude(row), :] = value

    even, opening, odd = branches()
    far = rows_in(far_ref, 0, 10)

    @pl.when(even)
    def _():
        residual_part(
            EIGHT, far, own_ref, conv_ref, bias_ref, out_weight_ref,
            mixed, lambda row, resid: step(row, resid, rows_of(part_ref, row)),
        )

    @pl.when(opening)
    def _():
        for row in range(ROWS):
            own = rows_of(own_ref, row + 2).astype(F32)
            resid = (own - rows_of(bg_ref, row).astype(F32)).astype(BF16)
            step(row, resid, rows_of(part_ref, row))

    @pl.when(odd)
    def _():
        adjoint_part(
            8, 0, far, rows_in(active_ref, 0, 10), rows_in(forecast_ref, 0, 10), back_ref,
            out_back_ref, cot, target, lambda row, adjoint: step(row, rows_of(part_ref, row), adjoint),
        )

    out_ref[...] = wide[...].reshape(C, ROWS, LON).astype(BF16)


def exchange(value, partner):
    windows, strips = lax.axis_size("tm"), lax.axis_size("lat")
    pairs = []
    for window in range(windows):
        for strip in range(strips):
            to_window, to_strip = partner(window, strip, windows - 1, strips - 1)
            pairs.append((window * strips + strip, to_window * strips + to_strip))
    return lax.ppermute(value, ("tm", "lat"), pairs)


def near_strip(window, strip, last_window, last_strip):
    return window, strip ^ 1


def far_strip(window, strip, last_window, last_strip):
    if strip in (0, last_strip):
        return window ^ 1, strip
    return window, ((strip + 1) ^ 1) - 1


def near_window(window, strip, last_window, last_strip):
    return window ^ 1, strip


def far_window(window, strip, last_window, last_strip):
    if window in (0, last_window):
        return window, strip ^ 2
    return ((window + 1) ^ 1) - 1, strip


def shape(rows, dtype=BF16):
    return jax.ShapeDtypeStruct((rows, LON), dtype)


def conv_scratch(count):
    return [
        pltpu.VMEM((4, (count // 2) * 3 * C, LON), BF16),
    ]


def gradient_scratch(count):
    return conv_scratch(count) + [
        pltpu.VMEM(((count + 2) * HID, LON), BF16),
        pltpu.VMEM(((count + 2) * C, LON), BF16),
    ]


def row_flops(rows):
    return rows * 2 * LON * HID * 10 * C


def on_device(
    window_snapshots, background, obs_values, obs_index, input_kernel_weight, hidden_bias_vector,
    output_pointwise_weight,
):
    def forward(work, state):
        count = len(rows_of_work(work))
        return call(
            functools.partial(forward_kernel, work),
            (shape(count * HID), shape(count * C)),
            conv_scratch(state.shape[0] // C - 2),
            row_flops(count), 2 << 20,
        )(state, conv_weight, bias, out_weight)

    taps = jnp.transpose(input_kernel_weight, (0, 1, 3, 2)).reshape(9 * C, HID)
    first, second, x, ground, observed, index, taps, out_weight, bias = call(
        pack_kernel,
        (
            shape(PAYLOAD), shape(PAYLOAD),
            jax.ShapeDtypeStruct((C, ROWS, LON), BF16),
            jax.ShapeDtypeStruct((C, ROWS, LON), BF16),
            jax.ShapeDtypeStruct((C, OBS), BF16),
            jax.ShapeDtypeStruct((1, OBS), jnp.int32),
            jax.ShapeDtypeStruct((9 * C, HID), BF16),
            jax.ShapeDtypeStruct((C, HID), BF16),
            jax.ShapeDtypeStruct((1, HID), F32),
        ),
        [
            pltpu.VMEM((C * ROWS, LON), F32),
            pltpu.VMEM((C * ROWS, LON), F32),
            pltpu.SemaphoreType.DMA((7,)),
        ],
        0, 1 << 20, pl.BlockSpec(memory_space=pltpu.HBM),
    )(
        *(
            pltpu.with_memory_space_constraint(value, pltpu.HBM)
            for value in (
                window_snapshots[0], obs_values[0], obs_index, background, taps,
                output_pointwise_weight, hidden_bias_vector[None, :],
            )
        )
    )
    second = exchange(second, far_strip)
    first = exchange(first, near_strip)
    own, ground, sums, conv_weight, back_weight, bias, out_back = call(
        prepare_kernel,
        (
            shape(ROWS * C), shape(ROWS * C),
            jax.ShapeDtypeStruct((ROWS, 72, LON), F32),
            jax.ShapeDtypeStruct((4 * HID, 3 * C), BF16),
            jax.ShapeDtypeStruct((3 * C, 3 * HID), BF16),
            jax.ShapeDtypeStruct((HID, LON), F32),
            jax.ShapeDtypeStruct((HID, C), BF16),
        ),
        [pltpu.VMEM((C * ROWS, LON), F32), pltpu.VMEM((C * ROWS, LON), F32)],
        ROWS * 2 * 80 * OBS * LON, 1 << 20,
    )(x, ground, observed, index, taps, bias, out_weight)
    far_own = exchange(own, far_window)
    near_own = exchange(own, near_window)
    weights = (conv_weight, bias, out_weight, back_weight, out_back)
    inside = forward(INSIDE, own)
    first, second, inside, sums = lax.optimization_barrier((first, second, inside, sums))

    ext, halo, above_edge, below_edge = call(
        extend_kernel,
        (shape(16 * C), shape(6 * C), shape(2 * C), shape(2 * C)),
        [], 0, 1 << 20,
    )(own, first, second)
    far = exchange(halo, far_window)
    near = exchange(halo, near_window)
    outside = forward(OUTSIDE, ext)
    part, inner = call(
        first_near_kernel, (shape(12 * C), shape(12 * C)), gradient_scratch(12),
        row_flops(12), 2 << 20,
    )(near, near_own, far_own, ext, *inside, *outside, *weights)
    state, sent = call(
        first_kernel, (shape(12 * C), shape(10 * C)), gradient_scratch(12), row_flops(12),
        2 << 20,
    )(
        far, far_own, part, inner, ext, ground, *inside, *outside, *weights, sums,
        above_edge, below_edge,
    )
    far = exchange(sent, far_window)
    near = exchange(sent, near_window)
    given = (state, ground, *forward(TEN, state), *weights)
    part = call(
        second_near_kernel, shape(8 * C), gradient_scratch(8), row_flops(8), 2 << 20
    )(near, state, *given[2:])
    analysis = call(
        second_kernel,
        jax.ShapeDtypeStruct((C, ROWS, LON), BF16),
        gradient_scratch(8) + [pltpu.VMEM((C * ROWS, LON), F32)],
        row_flops(8), 2 << 20,
    )(far, part, *given, sums)
    return analysis[None]


def solution(mesh):
    placed = (
        P("tm", None, "lat", None),
        P(None, "lat", None),
        P("tm", None, "lat"),
        P("tm", "lat"),
        P(),
        P(),
        P(),
    )
    return jax.shard_map(
        on_device, mesh=mesh, in_specs=placed, out_specs=P("tm", None, "lat", None), check_vma=False
    )
```

```python
import functools

import jax
import jax.numpy as jnp
from jax import lax
from jax.experimental import pallas as pl
from jax.experimental.pallas import tpu as pltpu
from jax.sharding import PartitionSpec as P


C = 64
HID = 256
ROWS = 8
LON = 128
OBS = 256
STEP = 0.3

F32 = jnp.float32
BF16 = jnp.bfloat16
VMEM = pl.BlockSpec(memory_space=pltpu.VMEM)

X_PART = 4 * C
PAYLOAD = X_PART + 2 * C


def call(kernel, outs, scratch, flops, bytes_accessed, spec=VMEM, grant=48 << 20):
    def run(*args):
        return pl.pallas_call(
            kernel,
            out_shape=outs,
            in_specs=[spec] * len(args),
            out_specs=jax.tree.map(lambda _: VMEM, outs),
            scratch_shapes=scratch,
            cost_estimate=pl.CostEstimate(
                flops=flops, bytes_accessed=bytes_accessed, transcendentals=0
            ),
            compiler_params=pltpu.CompilerParams(vmem_limit_bytes=grant),
        )(*args)

    return run


def rows_of(ref, first, width=C):
    return ref[first * width : (first + 1) * width, :]


def rows_in(ref, first, count):
    return [(ref, row) for row in range(first, first + count)]


def at(rows, place, width=C):
    ref, row = rows[place]
    return rows_of(ref, row, width)


def beside(rows, *places):
    return jnp.concatenate([at(rows, place) for place in places], axis=1)


def latitude(row):
    return pl.ds(row, C, stride=ROWS)


def local_cells(index):
    local = index - lax.axis_index("lat") * (ROWS * LON)
    high = lax.shift_right_arithmetic(local, 7)
    return local - high * LON, high


def with_ones(values):
    return jnp.concatenate([values, jnp.ones((16, OBS), BF16)], axis=0)


def observation_sums(values, low, high, row):
    cell = lax.broadcasted_iota(jnp.int32, (LON, OBS), 0)
    hit = jnp.where((low == cell) & (high == row), 1.0, 0.0).astype(BF16)
    return lax.dot_general(
        values, hit, (((1,), (1,)), ((), ())), preferred_element_type=F32
    )


def innovation_of(sums, own):
    return sums[C : C + 1, :] * own - sums[:C, :]


def pack_kernel(
    x_hbm, obs_hbm, index_hbm, bg_hbm, taps_hbm, out_weight_hbm, bias_hbm, first_ref, second_ref,
    x_ref, bg_ref, obs_ref, index_ref, taps_ref, out_weight_ref, bias_ref, xs, bs, sems,
):
    copies = [
        pltpu.make_async_copy(source, target, sems.at[place])
        for place, (source, target) in enumerate(
            (
                (x_hbm, x_ref), (obs_hbm, obs_ref), (index_hbm, index_ref), (bg_hbm, bg_ref),
                (taps_hbm, taps_ref), (out_weight_hbm, out_weight_ref), (bias_hbm, bias_ref),
            )
        )
    ]
    for copy in copies:
        copy.start()
    copies[1].wait()
    copies[2].wait()
    low, high = local_cells(index_ref[...])
    values = with_ones(obs_ref[...])
    sums = {row: observation_sums(values, low, high, row) for row in (0, 1, 6, 7)}
    even = lax.rem(lax.axis_index("lat"), 2) == 0

    def send(place, up, down):
        at = slice(place * C, (place + 1) * C)
        first_ref[at, :] = jnp.where(even, down, up).astype(BF16)
        second_ref[at, :] = jnp.where(even, up, down).astype(BF16)

    copies[0].wait()
    xs[...] = x_ref[...].astype(F32).reshape(ROWS * C, LON)
    for row in range(4):
        send(row, xs[latitude(row), :], xs[latitude(row + 4), :])

    def edge(row):
        return innovation_of(sums[row], xs[latitude(row), :])

    for row in range(2):
        send(4 + row, edge(row), edge(row + 6))
    copies[3].wait()

    @pl.when(lax.axis_index("tm") == 0)
    def _():
        bs[...] = bg_ref[...].astype(F32).reshape(ROWS * C, LON)

        def opening_edge(row):
            return edge(row) + (xs[latitude(row), :] - bs[latitude(row), :])

        for row in range(2):
            send(4 + row, opening_edge(row), opening_edge(row + 6))

    for copy in copies[4:]:
        copy.wait()


def extend_kernel(
    own_ref, first_ref, second_ref, ext_ref, halo_ref, above_edge_ref, below_edge_ref
):
    strip = lax.axis_index("lat")
    even = lax.rem(strip, 2) == 0
    zero = jnp.zeros((X_PART, LON), BF16)
    above = jnp.where(even, second_ref[...], first_ref[...])
    below = jnp.where(even, first_ref[...], second_ref[...])
    above_edge_ref[...] = above[X_PART:, :]
    below_edge_ref[...] = below[X_PART:, :]
    above = jnp.where(strip > 0, above[:X_PART, :], zero)
    below = jnp.where(strip < lax.axis_size("lat") - 1, below[:X_PART, :], zero)
    halo_ref[: 3 * C, :] = above[C:, :]
    halo_ref[3 * C :, :] = below[: 3 * C, :]
    ext_ref[:X_PART, :] = above
    ext_ref[X_PART : X_PART + ROWS * C, :] = own_ref[...]
    ext_ref[X_PART + ROWS * C :, :] = below


def turn(value, b):
    return value if b == 1 else pltpu.roll(value, 1 if b == 0 else LON - 1, 1)


def actives(work, rows, conv_ref, bias_ref, mixed):
    for place, pair in enumerate(pair for group in work for pair in group):
        d = [at(rows, pair[0] + a).astype(F32) for a in range(4)]
        for j, value in enumerate((d[0] - d[2], d[1] + d[2], d[2] - d[1], d[1] - d[3])):
            for b in range(3):
                start = (3 * place + b) * C
                mixed[j, start : start + C, :] = turn(value, b).astype(BF16)
    place = 0
    for group in work:
        bias = jnp.concatenate([bias_ref[...]] * len(group), axis=1)
        spans = [slice(3 * C * (place + n), 3 * C * (place + n + 1)) for n in range(len(group))]
        place += len(group)
        m = [
            jnp.dot(
                conv_ref[j * HID : (j + 1) * HID, :],
                jnp.concatenate([mixed[j, span, :] for span in spans], axis=1),
                preferred_element_type=F32,
            )
            for j in range(4)
        ]
        upper, lower = zip(*group)
        yield upper, jnp.tanh(m[0] + m[1] + m[2] + bias).astype(BF16)
        yield lower, jnp.tanh(m[1] - m[2] - m[3] + bias).astype(BF16)


def rows_of_work(work):
    return sorted(row for group in work for pair in group for row in pair)


def lanes_of(half):
    return slice(half * LON, (half + 1) * LON)


def store_pair(ref, first, value, width=C):
    ref[first * width : (first + 1) * width, :] = value[:, :LON]
    ref[(first + 1) * width : (first + 2) * width, :] = value[:, LON:]


def forward_kernel(
    work, state_ref, conv_ref, bias_ref, out_weight_ref, active_ref, forecast_ref, mixed
):
    rows = rows_in(state_ref, 0, state_ref.shape[0] // C)
    order = {row: place for place, row in enumerate(rows_of_work(work))}
    for some, active in actives(work, rows, conv_ref, bias_ref, mixed):
        step = jnp.dot(out_weight_ref[...], active, preferred_element_type=F32)
        centre = beside(rows, *(row + 1 for row in some)).astype(F32)
        forecast = (centre + step).astype(BF16)
        for half, row in enumerate(some):
            place = order[row]
            active_ref[place * HID : (place + 1) * HID, :] = active[:, lanes_of(half)]
            forecast_ref[place * C : (place + 1) * C, :] = forecast[:, lanes_of(half)]


def prepare_kernel(
    x_ref, bg_ref, obs_ref, index_ref, kernel_ref, bias_ref, out_weight_ref, own_ref, bg_rows_ref,
    sums_ref, conv_ref, back_ref, wide_bias_ref, out_back_ref, xs, bs,
):
    xs[...] = x_ref[...].astype(F32).reshape(ROWS * C, LON)
    bs[...] = bg_ref[...].astype(F32).reshape(ROWS * C, LON)
    for row in range(ROWS):
        own_ref[row * C : (row + 1) * C, :] = xs[latitude(row), :].astype(BF16)
        bg_rows_ref[row * C : (row + 1) * C, :] = bs[latitude(row), :].astype(BF16)
    low, high = local_cells(index_ref[...])
    values = with_ones(obs_ref[...])
    for row in range(ROWS):
        sums_ref[row] = observation_sums(values, low, high, row)[:72, :]
    g = [kernel_ref[a * 3 * C : (a + 1) * 3 * C, :].astype(F32) for a in range(3)]
    ends = g[0] + g[2]
    for j, value in enumerate((g[0], 0.5 * (ends + g[1]), 0.5 * (ends - g[1]), g[2])):
        conv_ref[j * HID : (j + 1) * HID, :] = value.astype(BF16).T
    out_back_ref[...] = out_weight_ref[...].T
    wide_bias_ref[...] = jnp.broadcast_to(bias_ref[...], (LON, HID)).T
    for a in range(3):
        back_ref[:, a * HID : (a + 1) * HID] = kernel_ref[(2 - a) * 3 * C : (3 - a) * 3 * C, :]


def residual_part(
    work, prev, own_ref, conv_ref, bias_ref, out_weight_ref, mixed, take
):
    own_rows = rows_in(own_ref, 2, max(rows_of_work(work)) + 1)
    for some, active in actives(work, prev, conv_ref, bias_ref, mixed):
        step = jnp.dot(out_weight_ref[...], active, preferred_element_type=F32)
        centre = beside(prev, *(row + 1 for row in some)).astype(F32)
        guess = (centre + step).astype(BF16).astype(F32)
        resid = (beside(own_rows, *some).astype(F32) - guess).astype(BF16)
        for half, row in enumerate(some):
            take(row, resid[:, lanes_of(half)])


def strip_ends():
    strip = lax.axis_index("lat")
    return -strip * ROWS, (lax.axis_size("lat") - strip) * ROWS


def adjoint_part(
    count, margin, later, active, forecast, back_ref, out_back_ref, cot, target, take
):
    top, bottom = strip_ends()
    for row in range(0, count + 2, 2):
        resid = beside(later, row, row + 1).astype(F32) - beside(forecast, row, row + 1).astype(F32)
        resid = resid.astype(BF16)
        store_pair(target, row, resid)
        projected = jnp.dot(out_back_ref[...], resid, preferred_element_type=F32)
        for half in range(2):
            place = row + half - margin - 1
            value = at(active, row + half, HID).astype(F32)
            value = (1.0 - value * value) * projected[:, half * LON : (half + 1) * LON]
            if not 0 <= place < ROWS:
                value = jnp.where((place >= top) & (place < bottom), value, 0.0)
            cot[(row + half) * HID : (row + half + 1) * HID, :] = value.astype(BF16)
    closing = lax.axis_index("tm") == lax.axis_size("tm") - 1
    for row in range(0, count, 2):
        cells = jnp.concatenate(
            [cot[row * HID : (row + 3) * HID, :], cot[(row + 1) * HID : (row + 4) * HID, :]], axis=1
        )
        spread = jnp.dot(back_ref[...], cells, preferred_element_type=F32)
        for half in range(2):
            lanes = slice(half * LON, (half + 1) * LON)
            pulled = (
                pltpu.roll(spread[:C, lanes], LON - 1, 1)
                + spread[C : 2 * C, lanes]
                + pltpu.roll(spread[2 * C :, lanes], 1, 1)
            )
            resid = rows_of(target, row + half + 1).astype(F32)
            take(row + half, jnp.where(closing, 0.0, resid + pulled).astype(BF16))


def branches():
    window = lax.axis_index("tm")
    even = lax.rem(window, 2) == 0
    opening = window == 0
    return even & jnp.logical_not(opening), opening, jnp.logical_not(even)


def quads_of(count):
    return tuple(((row, row + 1), (row + 2, row + 3)) for row in range(0, count - 3, 4))


INSIDE = (((0, 1), (2, 3)), ((4, 5),))
OUTSIDE = (((0, 1), (2, 3)), ((10, 11), (12, 13)))
INNER = (((4, 5), (6, 7)),)
OUTER = (((0, 1), (2, 3)), ((8, 9), (10, 11)))
TWELVE = quads_of(12)
TEN = quads_of(8) + (((8, 9),),)
EIGHT = quads_of(8)


def first_near_kernel(
    near_ref, near_own_ref, far_own_ref, own_ref, active_in_ref, forecast_in_ref, active_out_ref, forecast_out_ref,
    conv_ref, bias_ref, out_weight_ref, back_ref, out_back_ref, part_ref, inner_ref, mixed,
    cot, target,
):
    def put(ref):
        def take(row, value):
            ref[row * C : (row + 1) * C, :] = value

        return take

    even, _, odd = branches()
    near = rows_in(near_ref, 0, 3) + rows_in(near_own_ref, 0, ROWS) + rows_in(near_ref, 3, 3)

    @pl.when(jnp.logical_not(odd))
    def _():
        adjoint_part(
            12, 2, near, split_rows(active_out_ref, active_in_ref),
            split_rows(forecast_out_ref, forecast_in_ref), back_ref, out_back_ref, cot, target,
            put(part_ref),
        )

    @pl.when(even)
    def _():
        prev = [None] * 3 + rows_in(far_own_ref, 0, ROWS)
        residual_part(
            INNER, prev, own_ref, conv_ref, bias_ref, out_weight_ref,
            mixed, put(inner_ref)
        )

    @pl.when(odd)
    def _():
        residual_part(
            TWELVE, near, own_ref, conv_ref, bias_ref, out_weight_ref,
            mixed, put(part_ref),
        )


def split_rows(outside_ref, inside_ref):
    return rows_in(outside_ref, 0, 4) + rows_in(inside_ref, 0, 6) + rows_in(outside_ref, 4, 4)


def first_kernel(
    far_ref, far_own_ref, part_ref, inner_ref, own_ref, bg_ref, active_in_ref, forecast_in_ref,
    active_out_ref, forecast_out_ref, conv_ref, bias_ref, out_weight_ref, back_ref, out_back_ref,
    sums_ref, above_ref, below_ref, state_ref, sent_ref, mixed, cot, target,
):
    top, bottom = strip_ends()

    def step(row, resid, adjoint):
        own = rows_of(own_ref, row + 2).astype(F32)
        place = row - 2
        if place < 0:
            innovation = rows_of(above_ref, row).astype(F32)
        elif place >= ROWS:
            innovation = rows_of(below_ref, place - ROWS).astype(F32)
        else:
            innovation = innovation_of(sums_ref[place], own)
        value = own - STEP * (resid.astype(F32) - adjoint.astype(F32) + innovation)
        if not 0 <= place < ROWS:
            value = jnp.where((place >= top) & (place < bottom), value, 0.0)
        value = value.astype(BF16)
        state_ref[row * C : (row + 1) * C, :] = value
        if 1 <= row < 11:
            sent_ref[(row - 1) * C : row * C, :] = value

    even, opening, odd = branches()
    far = rows_in(far_ref, 0, 3) + rows_in(far_own_ref, 0, ROWS) + rows_in(far_ref, 3, 3)

    @pl.when(even)
    def _():
        residual_part(
            OUTER, far, own_ref, conv_ref, bias_ref, out_weight_ref,
            mixed, lambda row, resid: step(row, resid, rows_of(part_ref, row)),
        )
        for row in range(4, 8):
            step(row, rows_of(inner_ref, row), rows_of(part_ref, row))

    @pl.when(opening)
    def _():
        for row in range(12):
            place = row - 2
            resid = jnp.zeros((C, LON), BF16)
            if 0 <= place < ROWS:
                own = rows_of(own_ref, row + 2).astype(F32)
                resid = (own - rows_of(bg_ref, place).astype(F32)).astype(BF16)
            step(row, resid, rows_of(part_ref, row))

    @pl.when(odd)
    def _():
        adjoint_part(
            12, 2, far, split_rows(active_out_ref, active_in_ref),
            split_rows(forecast_out_ref, forecast_in_ref), back_ref, out_back_ref, cot, target,
            lambda row, adjoint: step(row, rows_of(part_ref, row), adjoint),
        )


def second_near_kernel(
    near_ref, own_ref, active_ref, forecast_ref, conv_ref, bias_ref, out_weight_ref,
    back_ref, out_back_ref, part_ref, mixed, cot, target,
):
    def take(row, value):
        part_ref[row * C : (row + 1) * C, :] = value

    _, _, odd = branches()
    near = rows_in(near_ref, 0, 10)

    @pl.when(jnp.logical_not(odd))
    def _():
        adjoint_part(
            8, 0, near, rows_in(active_ref, 0, 10), rows_in(forecast_ref, 0, 10), back_ref,
            out_back_ref, cot, target, take,
        )

    @pl.when(odd)
    def _():
        residual_part(
            EIGHT, near, own_ref, conv_ref, bias_ref, out_weight_ref,
            mixed, take
        )


def second_kernel(
    far_ref, part_ref, own_ref, bg_ref, active_ref, forecast_ref, conv_ref, bias_ref,
    out_weight_ref, back_ref, out_back_ref, sums_ref, out_ref, mixed, cot, target, wide,
):
    def step(row, resid, adjoint):
        own = rows_of(own_ref, row + 2).astype(F32)
        innovation = innovation_of(sums_ref[row], own)
        value = own - STEP * (resid.astype(F32) - adjoint.astype(F32) + innovation)
        wide[latitude(row), :] = value

    even, opening, odd = branches()
    far = rows_in(far_ref, 0, 10)

    @pl.when(even)
    def _():
        residual_part(
            EIGHT, far, own_ref, conv_ref, bias_ref, out_weight_ref,
            mixed, lambda row, resid: step(row, resid, rows_of(part_ref, row)),
        )

    @pl.when(opening)
    def _():
        for row in range(ROWS):
            own = rows_of(own_ref, row + 2).astype(F32)
            resid = (own - rows_of(bg_ref, row).astype(F32)).astype(BF16)
            step(row, resid, rows_of(part_ref, row))

    @pl.when(odd)
    def _():
        adjoint_part(
            8, 0, far, rows_in(active_ref, 0, 10), rows_in(forecast_ref, 0, 10), back_ref,
            out_back_ref, cot, target, lambda row, adjoint: step(row, rows_of(part_ref, row), adjoint),
        )

    out_ref[...] = wide[...].reshape(C, ROWS, LON).astype(BF16)


def exchange(value, partner):
    windows, strips = lax.axis_size("tm"), lax.axis_size("lat")
    pairs = []
    for window in range(windows):
        for strip in range(strips):
            to_window, to_strip = partner(window, strip, windows - 1, strips - 1)
            pairs.append((window * strips + strip, to_window * strips + to_strip))
    return lax.ppermute(value, ("tm", "lat"), pairs)


def near_strip(window, strip, last_window, last_strip):
    return window, strip ^ 1


def far_strip(window, strip, last_window, last_strip):
    if strip in (0, last_strip):
        return window ^ 1, strip
    return window, ((strip + 1) ^ 1) - 1


def near_window(window, strip, last_window, last_strip):
    return window ^ 1, strip


def far_window(window, strip, last_window, last_strip):
    if window in (0, last_window):
        return window, strip ^ 2
    return ((window + 1) ^ 1) - 1, strip


def shape(rows, dtype=BF16):
    return jax.ShapeDtypeStruct((rows, LON), dtype)


def conv_scratch(count):
    return [
        pltpu.VMEM((4, (count // 2) * 3 * C, LON), BF16),
    ]


def gradient_scratch(count):
    return conv_scratch(count) + [
        pltpu.VMEM(((count + 2) * HID, LON), BF16),
        pltpu.VMEM(((count + 2) * C, LON), BF16),
    ]


def row_flops(rows):
    return rows * 2 * LON * HID * 10 * C


def on_device(
    window_snapshots, background, obs_values, obs_index, input_kernel_weight, hidden_bias_vector,
    output_pointwise_weight,
):
    def forward(work, state):
        count = len(rows_of_work(work))
        return call(
            functools.partial(forward_kernel, work),
            (shape(count * HID), shape(count * C)),
            conv_scratch(state.shape[0] // C - 2),
            row_flops(count), 2 << 20,
        )(state, conv_weight, bias, out_weight)

    taps = jnp.transpose(input_kernel_weight, (0, 1, 3, 2)).reshape(9 * C, HID)
    first, second, x, ground, observed, index, taps, out_weight, bias = call(
        pack_kernel,
        (
            shape(PAYLOAD), shape(PAYLOAD),
            jax.ShapeDtypeStruct((C, ROWS, LON), BF16),
            jax.ShapeDtypeStruct((C, ROWS, LON), BF16),
            jax.ShapeDtypeStruct((C, OBS), BF16),
            jax.ShapeDtypeStruct((1, OBS), jnp.int32),
            jax.ShapeDtypeStruct((9 * C, HID), BF16),
            jax.ShapeDtypeStruct((C, HID), BF16),
            jax.ShapeDtypeStruct((1, HID), F32),
        ),
        [
            pltpu.VMEM((C * ROWS, LON), F32),
            pltpu.VMEM((C * ROWS, LON), F32),
            pltpu.SemaphoreType.DMA((7,)),
        ],
        0, 1 << 20, pl.BlockSpec(memory_space=pltpu.HBM),
    )(
        *(
            pltpu.with_memory_space_constraint(value, pltpu.HBM)
            for value in (
                window_snapshots[0], obs_values[0], obs_index, background, taps,
                output_pointwise_weight, hidden_bias_vector[None, :],
            )
        )
    )
    second = exchange(second, far_strip)
    first = exchange(first, near_strip)
    own, ground, sums, conv_weight, back_weight, bias, out_back = call(
        prepare_kernel,
        (
            shape(ROWS * C), shape(ROWS * C),
            jax.ShapeDtypeStruct((ROWS, 72, LON), F32),
            jax.ShapeDtypeStruct((4 * HID, 3 * C), BF16),
            jax.ShapeDtypeStruct((3 * C, 3 * HID), BF16),
            jax.ShapeDtypeStruct((HID, LON), F32),
            jax.ShapeDtypeStruct((HID, C), BF16),
        ),
        [pltpu.VMEM((C * ROWS, LON), F32), pltpu.VMEM((C * ROWS, LON), F32)],
        ROWS * 2 * 80 * OBS * LON, 1 << 20,
    )(x, ground, observed, index, taps, bias, out_weight)
    far_own = exchange(own, far_window)
    near_own = exchange(own, near_window)
    weights = (conv_weight, bias, out_weight, back_weight, out_back)
    inside = forward(INSIDE, own)
    first, second, inside, sums = lax.optimization_barrier((first, second, inside, sums))

    ext, halo, above_edge, below_edge = call(
        extend_kernel,
        (shape(16 * C), shape(6 * C), shape(2 * C), shape(2 * C)),
        [], 0, 1 << 20,
    )(own, first, second)
    far = exchange(halo, far_window)
    near = exchange(halo, near_window)
    outside = forward(OUTSIDE, ext)
    part, inner = call(
        first_near_kernel, (shape(12 * C), shape(12 * C)), gradient_scratch(12),
        row_flops(12), 2 << 20,
    )(near, near_own, far_own, ext, *inside, *outside, *weights)
    state, sent = call(
        first_kernel, (shape(12 * C), shape(10 * C)), gradient_scratch(12), row_flops(12),
        2 << 20,
    )(
        far, far_own, part, inner, ext, ground, *inside, *outside, *weights, sums,
        above_edge, below_edge,
    )
    far = exchange(sent, far_window)
    near = exchange(sent, near_window)
    given = (state, ground, *forward(TEN, state), *weights)
    part = call(
        second_near_kernel, shape(8 * C), gradient_scratch(8), row_flops(8), 2 << 20
    )(near, state, *given[2:])
    analysis = call(
        second_kernel,
        jax.ShapeDtypeStruct((C, ROWS, LON), BF16),
        gradient_scratch(8) + [pltpu.VMEM((C * ROWS, LON), F32)],
        row_flops(8), 2 << 20,
    )(far, part, *given, sums)
    return analysis[None]


def solution(mesh):
    placed = (
        P("tm", None, "lat", None),
        P(None, "lat", None),
        P("tm", None, "lat"),
        P("tm", "lat"),
        P(),
        P(),
        P(),
    )
    return jax.shard_map(
        on_device, mesh=mesh, in_specs=placed, out_specs=P("tm", None, "lat", None), check_vma=False
    )
```
